256 devices in a mesh: ctx: 16 (over y_hi, z), head: 8 (over x, core), rep: 2 (over y_lo).
Axes of the slice: x: 4, y: 4 (y_hi: 2, y_lo: 2; y = y_hi * 2 + y_lo), z: 8, core: 2. Of those that a mesh axis runs over, the one named last changes fastest.
Arguments:
- query_latent: bfloat16 [8192, 1536], P(('rep', 'ctx')), parts along dimension 0, may hold values from -6 to 6
- key_rows: bfloat16 [8192, 576], P(('rep', 'ctx')), parts along dimension 0, may hold values from -640 to 640
- key_cache: bfloat16 [1024, 576], P('rep'), parts along dimension 0, may hold values from -640 to 640
- prompt_start: int32 [2], P('rep'), parts along dimension 0, may hold values from 0 to 512
- w_query: bfloat16 [1536, 12288], P(None, 'head'), may hold values from -0.15625 to 0.15625
- w_key_up: bfloat16 [64, 128, 512], P('head'), may hold values from -0.5 to 0.5
- w_value_up: bfloat16 [64, 512, 128], P('head'), may hold values from -0.25 to 0.25
- w_output: bfloat16 [64, 128, 7168], P('head', 'ctx'), may hold values from -0.09375 to 0.09375
Outputs:
- layer_out: bfloat16 [8192, 7168], P(('rep', 'ctx'), 'head'), parts along dimension 0
The draws below stay inside these ranges and needn't reach their ends.
There are 2 independent parts, one for each index of `rep`. The reference program is written for one: setup_inputs(seed, part) draws one part's arguments, and reference() takes and returns one part's arrays. A program takes and returns all parts, laid end to end along the dimension named above; an argument that names none is the same for every part. Nothing has to cross between parts.
All inputs are finite; a program needn't handle non-finite values.
Results may differ from the reference program's by a relative error of at most 0.017.
The reference program's roundings to bfloat16 on the way count: a program that leaves them out, or rounds other values in their place, can miss the bound.
Values may be sent and summed in bfloat16 or wider, within the bound.
No kernel may reach another device: no remote copies, remote signals or barrier semaphores. Data moves between devices by JAX's collectives and lax.ppermute only.
A program may use at most 128 MiB of HBM per device.

```python
import jax
import jax.numpy as jnp
from jax import lax

D = 7168
HEADS = 64
NOPE = 128
ROPE = 64
VDIM = 128
LATENT = 512
QLORA = 1536
WINDOW = 512
TOK_DEV = 256
TOKENS = 4096


def latent_rows(key, row_count):
    drawn_key, rope_key = jax.random.split(key, 2)
    latent_part = jnp.clip(jax.random.normal(drawn_key, (row_count, LATENT), jnp.float32), -6.0, 6.0)
    rope_part = jnp.clip(jax.random.normal(rope_key, (row_count, ROPE), jnp.float32), -6.0, 6.0)
    return jnp.concatenate([latent_part, rope_part], 1)


def draw_key_rows(key, part):
    return latent_rows(jax.random.fold_in(key, 11), TOKENS).astype(jnp.bfloat16)


def draw_key_cache(key, part):
    return latent_rows(jax.random.fold_in(key, 23), WINDOW).astype(jnp.bfloat16)


def strengthened(result, own_key, source, target, blocks, factor):
    def block_of(position):
        return (jnp.arange(result.shape[position]) // (result.shape[position] // blocks)).reshape((-1,) + (1,) * (result.ndim - 1 - position))

    near = jax.random.permutation(own_key, blocks)[block_of(target)]
    second = (block_of(target) + blocks // 2) % blocks
    return jnp.where((block_of(source) == near) | (block_of(source) == second), factor * result, result)


def level_of(own_key, shape, shards, least, top_value):
    def one(axis_at, shards_of):
        steps = jax.random.uniform(jax.random.fold_in(jax.random.fold_in(own_key, 6), axis_at), (shards_of,), jnp.float32, least / len(shards), top_value / len(shards))
        return jnp.repeat(jnp.exp(steps), shape[axis_at] // shards_of).reshape((-1,) + (1,) * (len(shape) - axis_at - 1))

    gain = one(*shards[0])
    for cut in shards[1:]:
        gain = gain * one(*cut)
    return gain


def normal_values(key, shape, scale, most, shards=(), kind=jnp.bfloat16):
    array = jax.random.normal(key, shape, jnp.float32) * scale
    if len(shards) > 0:
        array = level_of(key, shape, shards, -0.22, 0.18) * array
    return jnp.clip(array, min=-most, max=most).astype(kind)


def heavy_noise(rng, extent, scale, bound, cuts, heavy, held_as=jnp.bfloat16):
    result = scale * jax.random.normal(rng, extent, jnp.float32)
    if cuts:
        result = result * level_of(rng, extent, cuts, -0.22, 0.18)
    return jnp.clip(strengthened(result, jax.random.fold_in(rng, 3), *heavy), -bound, bound).astype(held_as)


def setup_inputs(seed: int = 0, part: int = 0) -> dict:
    key_of = jax.random.split(jax.random.key(seed), 9)
    own_keys = jax.random.split(jax.random.fold_in(key_of[8], part), 9)
    query_latent = normal_values(own_keys[0], (TOKENS, QLORA), 1.0, 6.0, ((0, 16),))
    key_rows = draw_key_rows(jax.random.fold_in(jax.random.fold_in(key_of[8], part), 71), part)
    key_cache = draw_key_cache(jax.random.fold_in(jax.random.fold_in(key_of[8], part), 71), part)
    prompt_start = jax.random.randint(own_keys[3], (1,), 0, WINDOW + 1).astype(jnp.int32)
    w_query = normal_values(key_of[4], (QLORA, HEADS * (NOPE + ROPE)), QLORA ** -0.5, 0.15625, ((1, 8),))
    w_key_up = normal_values(key_of[5], (HEADS, NOPE, LATENT), NOPE ** -0.5, 0.5, ((0, 8),))
    w_value_up = normal_values(key_of[6], (HEADS, LATENT, VDIM), LATENT ** -0.5, 0.25, ((0, 8),))
    w_output = heavy_noise(key_of[7], (HEADS, VDIM, D), (HEADS * VDIM) ** -0.5, 0.09375, ((0, 8), (1, 16)), (0, 2, 8, 2.0))
    return dict(query_latent=query_latent, key_rows=key_rows, key_cache=key_cache, prompt_start=prompt_start, w_query=w_query, w_key_up=w_key_up, w_value_up=w_value_up, w_output=w_output)


def rotate(values, positions):
    half_dim = values.shape[-1] // 2
    inverse = jnp.power(jnp.float32(10000.0), -jnp.arange(half_dim, dtype=jnp.float32) * (2.0 / values.shape[-1]))
    angles = positions[..., None] * inverse
    cosine = jnp.cos(angles)
    sines = jnp.sin(angles)
    lower_half = values[..., :half_dim]
    upper_half = values[..., half_dim:]
    return jnp.concatenate([lower_half * cosine - upper_half * sines, lower_half * sines + upper_half * cosine], -1)


def reference(query_latent, key_rows, key_cache, prompt_start, w_query, w_key_up, w_value_up, w_output):
    head_count, nope_dim, latent = w_key_up.shape
    value_dim = w_value_up.shape[2]
    rope_dim = key_rows.shape[1] - latent
    queries = jnp.dot(query_latent, w_query, preferred_element_type=jnp.float32).astype(jnp.bfloat16)
    queries = queries.reshape(TOKENS, head_count, nope_dim + rope_dim)
    query_lat = jnp.einsum("thn,hnl->thl", queries[..., :nope_dim].astype(jnp.float32), w_key_up.astype(jnp.float32)).astype(jnp.bfloat16)
    token_pos = jnp.arange(TOKENS, dtype=jnp.float32)
    query_rot = rotate(queries[..., nope_dim:].astype(jnp.float32), token_pos[:, None]).astype(jnp.bfloat16)
    key_rot = rotate(key_rows[:, latent:].astype(jnp.float32), token_pos).astype(jnp.bfloat16)
    all_keys = jnp.concatenate([key_cache, jnp.concatenate([key_rows[:, :latent], key_rot], 1)], 0)
    score_scale = (nope_dim + rope_dim) ** -0.5
    prompt_first = prompt_start[0]
    key_span = WINDOW + TOK_DEV

    def attend(block_index):
        first_row = block_index * TOK_DEV
        near_keys = lax.dynamic_slice_in_dim(all_keys, first_row, key_span, 0)
        query_block = lax.dynamic_slice_in_dim(query_lat, first_row, TOK_DEV, 0).astype(jnp.float32)
        rot_block = lax.dynamic_slice_in_dim(query_rot, first_row, TOK_DEV, 0).astype(jnp.float32)
        key_lat = near_keys[:, :latent].astype(jnp.float32)
        scores = jnp.einsum("thl,kl->htk", query_block, key_lat)
        scores = scores + jnp.einsum("thr,kr->htk", rot_block, near_keys[:, latent:].astype(jnp.float32))
        scores = scores * score_scale
        key_pos = jnp.arange(key_span, dtype=jnp.int32) - WINDOW
        row_ids = jnp.arange(TOK_DEV, dtype=jnp.int32)
        relative = key_pos[None, :] - row_ids[:, None]
        visible = (relative <= 0) & (relative > -WINDOW) & ((first_row + key_pos) >= -prompt_first)[None, :]
        scores = jnp.where(visible[None], scores, -1e30)
        row_max = jnp.max(scores, axis=-1, keepdims=True)
        powers = jnp.exp(scores - row_max)
        weights = (powers / jnp.sum(powers, axis=-1, keepdims=True)).astype(jnp.bfloat16)
        mixed_lat = jnp.einsum("htk,kl->thl", weights.astype(jnp.float32), key_lat).astype(jnp.bfloat16)
        return jnp.einsum("thl,hlv->thv", mixed_lat.astype(jnp.float32), w_value_up.astype(jnp.float32)).astype(jnp.bfloat16)

    attention = lax.map(attend, jnp.arange(TOKENS // TOK_DEV, dtype=jnp.int32))
    attention = attention.reshape(TOKENS, head_count * value_dim)
    projected = jnp.dot(attention, w_output.reshape(head_count * value_dim, D), preferred_element_type=jnp.float32)
    return projected.astype(jnp.bfloat16)
```

```python
import functools

import jax
import jax.numpy as jnp
from jax import lax
from jax.experimental import pallas as pl
from jax.experimental.pallas import tpu as pltpu
from jax.sharding import Mesh
from jax.sharding import PartitionSpec as P

AXES = ("yh", "z", "x", "c", "yl")
SIZES = (2, 8, 4, 2, 2)
CTX = ("yh", "z")
HEAD = ("x", "c")
BF = jnp.bfloat16
F32 = jnp.float32
VMEM = pltpu.MemorySpace.VMEM


def number_of(yh, z, x, c, yl):
    return (((yh * 8 + z) * 4 + x) * 2 + c) * 2 + yl


def moved(a, target):
    pairs = []
    for yh in range(2):
        for z in range(8):
            for x in range(4):
                for c in range(2):
                    for yl in range(2):
                        t = target(yh, z, x, c, yl)
                        pairs.append((number_of(yh, z, x, c, yl), number_of(*t)))
    return lax.ppermute(a, AXES, pairs)


def up_z(a):
    return moved(a, lambda yh, z, x, c, yl: (yh, (z + 1) % 8, x, c, yl))


def down_z(a):
    return moved(a, lambda yh, z, x, c, yl: (yh, (z - 1) % 8, x, c, yl))


def xor_y(a, q):
    return moved(a, lambda yh, z, x, c, yl: (yh ^ (q >> 1), z, x, c, yl ^ (q & 1)))


def other_core(a):
    return moved(a, lambda yh, z, x, c, yl: (yh, z, x, 1 - c, yl))


def along_x(a, d):
    return moved(a, lambda yh, z, x, c, yl: (yh, z, (x + d) % 4, c, yl))


def home(a, r):
    return moved(a, lambda yh, z, x, c, yl: (yh ^ c, z, x, yh, yl ^ r))


def passed_along(x, by):
    pairs = [(i, i + by) for i in range(16) if i + by < 16]
    return lax.ppermute(x, CTX, pairs)


def rotate(values, positions):
    half_dim = values.shape[-1] // 2
    inverse = jnp.power(
        jnp.float32(10000.0), -jnp.arange(half_dim, dtype=jnp.float32) * (2.0 / values.shape[-1])
    )
    angles = positions[..., None] * inverse
    cosine = jnp.cos(angles)
    sines = jnp.sin(angles)
    lower_half = values[..., :half_dim]
    upper_half = values[..., half_dim:]
    return jnp.concatenate(
        [lower_half * cosine - upper_half * sines, lower_half * sines + upper_half * cosine], -1
    )


def attention_of(query_latent, key_rows, key_cache, prompt_start, w_query, w_key_up, w_value_up):
    tok_rows = query_latent.shape[0]
    heads_dev, nope_dim, latent = w_key_up.shape
    rope_dim = key_rows.shape[1] - latent
    window = key_cache.shape[0]
    slab_index = lax.axis_index(CTX)
    queries = jnp.dot(query_latent, w_query, preferred_element_type=F32).astype(BF)
    queries = queries.reshape(tok_rows, heads_dev, nope_dim + rope_dim)
    query_lat = jnp.einsum(
        "thn,hnl->thl", queries[..., :nope_dim], w_key_up, preferred_element_type=F32
    ).astype(BF)
    token_pos = (slab_index * tok_rows + jnp.arange(tok_rows, dtype=jnp.int32)).astype(F32)
    query_rot = rotate(queries[..., nope_dim:].astype(F32), token_pos[:, None]).astype(BF)
    key_rot = rotate(key_rows[:, latent:].astype(F32), token_pos).astype(BF)
    own_keys = jnp.concatenate([key_rows[:, :latent], key_rot], 1)
    received = [passed_along(own_keys, 1), passed_along(own_keys, 2)]
    key_blocks = []
    for distance in (1, 2):
        cache_slot = jnp.clip(2 - distance + slab_index, 0, 1)
        cached = lax.dynamic_slice_in_dim(key_cache, cache_slot * tok_rows, tok_rows, 0)
        key_blocks.append(jnp.where(slab_index < distance, cached, received[distance - 1]))
    all_keys = jnp.concatenate(key_blocks[::-1] + [own_keys], 0)
    key_span = all_keys.shape[0]
    key_lat = all_keys[:, :latent]
    score_scale = (nope_dim + rope_dim) ** (-0.5)
    scores = jnp.einsum("thl,kl->htk", query_lat, key_lat, preferred_element_type=F32)
    scores = scores + jnp.einsum(
        "thr,kr->htk", query_rot, all_keys[:, latent:], preferred_element_type=F32
    )
    scores = scores * score_scale
    key_pos = jnp.arange(key_span, dtype=jnp.int32) - window
    row_ids = jnp.arange(tok_rows, dtype=jnp.int32)
    relative = key_pos[None, :] - row_ids[:, None]
    in_prompt = slab_index * tok_rows + key_pos >= -prompt_start[0]
    visible = (relative <= 0) & (relative > -window) & in_prompt[None, :]
    scores = jnp.where(visible[None], scores, -1e30)
    row_max = jnp.max(scores, axis=-1, keepdims=True)
    powers = jnp.exp(scores - row_max)
    weights = (powers / jnp.sum(powers, axis=-1, keepdims=True)).astype(BF)
    mixed_lat = jnp.einsum("htk,kl->thl", weights, key_lat, preferred_element_type=F32).astype(BF)
    attention = jnp.einsum("thl,hlv->thv", mixed_lat, w_value_up, preferred_element_type=F32)
    return attention.astype(BF).reshape(tok_rows, -1)


def quarter_kernel(place, rows, own, other):
    for out, flip in ((own, 0), (other, 3)):
        y = place[1] ^ flip
        odd = y % 2
        base = 896 * (y // 2) + 384 * odd
        pieces = []
        for d in range(4):
            start = pl.multiple_of(1792 * ((place[0] + d) % 4) + base, 128)
            wide = rows[:, pl.ds(start, 512)]
            pieces.append(jnp.where(odd == 1, wide[:, 64:], wide[:, :448]))
        out[...] = jnp.concatenate(pieces, 1)


def project_kernel(theirs, place, *refs):
    groups, blocks, (out, rows, total) = refs[:4], refs[4:20], refs[20:]
    first = 2 * (place[0] ^ theirs)
    for pick in (0, 2):

        @pl.when(first == pick)
        def _():
            for g in range(2):
                for p in range(2):
                    half = pl.ds(pl.multiple_of(512 * (place[1] ^ p), 512), 512)
                    rows[pl.ds(256 * g, 256), pl.ds(512 * p, 512)] = groups[pick + g][:, half]

    def step(n, carry):
        columns = pl.ds(pl.multiple_of(n * 256, 256), 256)
        weights = jnp.concatenate([block[:, columns] for block in blocks], 0)
        total[:, columns] = jnp.dot(rows[...], weights, preferred_element_type=F32)
        return carry

    lax.fori_loop(0, 7, step, 0)
    for d in range(4):
        span = slice(448 * d, 448 * d + 448)
        out[d] = jnp.concatenate([total[:256, span], total[256:, span]], 1).astype(out.dtype)


def whole(n):
    return [pl.BlockSpec(memory_space=VMEM)] * n


def scalars(n=1):
    return [pl.BlockSpec(memory_space=pltpu.MemorySpace.SMEM)] * n


def quarters(rows, x, y):
    return pl.pallas_call(
        quarter_kernel,
        out_shape=[jax.ShapeDtypeStruct((64, 1792), BF)] * 2,
        in_specs=scalars() + whole(1),
        out_specs=whole(2),
        name="quarters",
        cost_estimate=pl.CostEstimate(flops=0, bytes_accessed=2 << 20, transcendentals=0),
    )(jnp.stack([x, y]), rows)


def project(theirs, place, groups, blocks, kind):
    return pl.pallas_call(
        functools.partial(project_kernel, theirs),
        out_shape=jax.ShapeDtypeStruct((4, 256, 896), kind),
        in_specs=scalars() + whole(20),
        out_specs=whole(1)[0],
        scratch_shapes=[pltpu.VMEM((512, 1024), BF), pltpu.VMEM((512, 1792), F32)],
        compiler_params=pltpu.CompilerParams(vmem_limit_bytes=40 << 20),
        name="project",
        cost_estimate=pl.CostEstimate(
            flops=2 * 512 * 1024 * 1792, bytes_accessed=8 << 20, transcendentals=0
        ),
    )(place, *groups, *blocks)


def local(query_latent, key_rows, key_cache, prompt_start, w_query, w_key_up, w_value_up, w_output):
    yh, z, x, c, yl = (lax.axis_index(a) for a in AXES)
    y = 2 * yh + yl
    own, given = quarters(w_output.reshape(64, 7168), x, y)
    other = xor_y(given, 3)
    blocks = [[own] + [None] * 7, [other] + [None] * 7]
    for p in range(2):
        up = down = blocks[p][0]
        for s in range(1, 5):
            if s < 4 or p == 0:
                up = up_z(up)
                blocks[p][8 - s] = up
            if s < 4 or p == 1:
                down = down_z(down)
                blocks[p][s] = down
    attention = attention_of(
        query_latent, key_rows, key_cache, prompt_start, w_query, w_key_up, w_value_up
    )
    column = jnp.arange(1024, dtype=jnp.int32)
    source = (
        (column // 8 % 8) * 128 + (column // 512) * 64 + ((z + column // 64) % 8) * 8 + column % 8
    )
    reorder = (jnp.arange(1024, dtype=jnp.int32)[:, None] == source[None, :]).astype(BF)
    rows = jnp.dot(attention, reorder, preferred_element_type=F32).astype(BF)
    groups = [rows] + [xor_y(rows, q) for q in (1, 2, 3)]
    place = jnp.stack([c, yh])
    flat = blocks[0] + blocks[1]
    theirs = other_core(project(1, place, groups, flat, BF))
    mine = project(0, place, groups, flat, F32)
    sums = mine + theirs.astype(F32)
    result = sums[0]
    for d in (2, 1, 3):
        result = result + along_x(sums[d].astype(BF), d).astype(F32)
    result = result.astype(BF)
    pieces = [home(result[:, 448 * r : 448 * r + 448], r) for r in range(2)]
    even = yl == 0
    return jnp.concatenate(
        [jnp.where(even, pieces[0], pieces[1]), jnp.where(even, pieces[1], pieces[0])], 1
    )


def solution(mesh):
    cut = Mesh(mesh.devices.reshape(SIZES), AXES) if hasattr(mesh, "devices") else mesh
    tokens = ("yl", "yh", "z")
    return jax.shard_map(
        local,
        mesh=cut,
        in_specs=(
            P(tokens, None),
            P(tokens, None),
            P("yl", None),
            P("yl"),
            P(None, HEAD),
            P(HEAD, None, None),
            P(HEAD, None, None),
            P(HEAD, CTX, None),
        ),
        out_specs=P(tokens, HEAD),
        check_vma=False,
    )
```

```python
import functools

import jax
import jax.numpy as jnp
from jax import lax
from jax.experimental import pallas as pl
from jax.experimental.pallas import tpu as pltpu
from jax.sharding import Mesh
from jax.sharding import PartitionSpec as P

AXES = ("yh", "z", "x", "c", "yl")
SIZES = (2, 8, 4, 2, 2)
CTX = ("yh", "z")
HEAD = ("x", "c")
BF = jnp.bfloat16
F32 = jnp.float32
VMEM = pltpu.MemorySpace.VMEM


def number_of(yh, z, x, c, yl):
    return (((yh * 8 + z) * 4 + x) * 2 + c) * 2 + yl


def moved(a, target):
    pairs = []
    for yh in range(2):
        for z in range(8):
            for x in range(4):
                for c in range(2):
                    for yl in range(2):
                        t = target(yh, z, x, c, yl)
                        pairs.append((number_of(yh, z, x, c, yl), number_of(*t)))
    return lax.ppermute(a, AXES, pairs)


def up_z(a):
    return moved(a, lambda yh, z, x, c, yl: (yh, (z + 1) % 8, x, c, yl))


def down_z(a):
    return moved(a, lambda yh, z, x, c, yl: (yh, (z - 1) % 8, x, c, yl))


def xor_y(a, q):
    return moved(a, lambda yh, z, x, c, yl: (yh ^ (q >> 1), z, x, c, yl ^ (q & 1)))


def other_core(a):
    return moved(a, lambda yh, z, x, c, yl: (yh, z, x, 1 - c, yl))


def along_x(a, d):
    return moved(a, lambda yh, z, x, c, yl: (yh, z, (x + d) % 4, c, yl))


def home(a, r):
    return moved(a, lambda yh, z, x, c, yl: (yh ^ c, z, x, yh, yl ^ r))


def queries_kernel(rows, w_query, w_key_up, turn, out):
    cosine, sine = turn[:, :64], turn[:, 64:]
    for part in range(2):
        span = slice(768 * part, 768 * part + 768)
        queries = jnp.dot(rows[...], w_query[:, span], preferred_element_type=F32).astype(BF)
        for i in range(4):
            h = 4 * part + i
            plain = queries[:, 192 * i : 192 * i + 128]
            lat = jnp.dot(plain, w_key_up[h], preferred_element_type=F32)
            rot = queries[:, 192 * i + 128 : 192 * i + 192].astype(F32)
            other = jnp.concatenate([rot[:, 32:], rot[:, :32]], 1)
            rot = rot * cosine + other * sine
            tokens = slice(256 * h, 256 * h + 256)
            out[tokens, :512] = lat.astype(BF)
            out[tokens, 512:] = jnp.concatenate([rot, jnp.zeros_like(rot)], 1).astype(BF)


def keys_kernel(place, own, near, far, swapped, cache, turn, keys, hidden):
    c, slab, start = place[0], place[1], place[2]
    mine = pl.ds(pl.multiple_of(128 * c, 128), 128)
    theirs = pl.ds(pl.multiple_of(128 * (1 - c), 128), 128)
    keys[512:, :576] = own[...]
    keys[pl.ds(pl.multiple_of(256 + 128 * c, 128), 128), :576] = near[...]
    keys[pl.ds(pl.multiple_of(384 - 128 * c, 128), 128), :576] = swapped[:128]
    keys[mine, :576] = far[...]
    keys[theirs, :576] = swapped[128:]
    rot = keys[:, 512:576].astype(F32)
    other = jnp.concatenate([rot[:, 32:], rot[:, :32]], 1)
    rot = rot * turn[:, :64] + other * turn[:, 64:]
    keys[:, 512:] = jnp.concatenate([rot, jnp.zeros_like(rot)], 1).astype(BF)

    @pl.when(slab == 0)
    def _():
        keys[:512, :576] = cache[...]

    @pl.when(slab == 1)
    def _():
        keys[:256, :576] = cache[256:]

    row = lax.broadcasted_iota(jnp.int32, (256, 768), 0)
    col = lax.broadcasted_iota(jnp.int32, (256, 768), 1)
    relative = col - 512 - row
    visible = (relative <= 0) & (relative > -512) & (slab * 256 + col - 512 >= -start)
    hidden[...] = jnp.where(visible, 0.0, -1e30)


def attend_kernel(group, queries, keys, hidden, w_value_up, reorder, out):
    scale = 192.0**-0.5 * 1.4426950408889634
    latent = keys[:, :512]
    heads = []
    for pair in range(2):
        scores = lax.dot_general(
            queries[1024 * group + 512 * pair : 1024 * group + 512 * pair + 512, :],
            keys[...],
            (((1,), (1,)), ((), ())),
            preferred_element_type=F32,
        )
        for i in range(2):
            part = scores[256 * i : 256 * i + 256] * scale + hidden[...]
            top = jnp.max(part, axis=1, keepdims=True)
            powers = jnp.exp2(part - top)
            share = 1.0 / jnp.sum(powers, axis=1, keepdims=True)
            mixed = jnp.dot(powers.astype(BF), latent, preferred_element_type=F32) * share
            attention = jnp.dot(
                mixed.astype(BF), w_value_up[4 * group + 2 * pair + i], preferred_element_type=F32
            )
            heads.append(attention.astype(BF))
    rows = jnp.concatenate(heads, 1)
    out[...] = jnp.dot(rows, reorder[...], preferred_element_type=F32).astype(BF)


def turn_of(positions):
    inverse = jnp.power(jnp.float32(10000.0), -jnp.arange(32, dtype=F32) * (2.0 / 64))
    angles = positions.astype(F32)[:, None] * inverse
    cosine, sine = jnp.cos(angles), jnp.sin(angles)
    return jnp.concatenate([cosine, cosine, -sine, sine], 1)


def quarter_kernel(place, rows, own, other):
    for out, flip in ((own, 0), (other, 3)):
        y = place[1] ^ flip
        odd = y % 2
        base = 896 * (y // 2) + 384 * odd
        pieces = []
        for d in range(4):
            start = pl.multiple_of(1792 * ((place[0] + d) % 4) + base, 128)
            wide = rows[:, pl.ds(start, 512)]
            pieces.append(jnp.where(odd == 1, wide[:, 64:], wide[:, :448]))
        out[...] = jnp.concatenate(pieces, 1)


def project_kernel(theirs, place, *refs):
    groups, blocks, (out, rows, weights, total, sem) = refs[:8], refs[8:24], refs[24:]
    copies = []
    for p in range(2):
        for k in range(8):
            for g in range(2):
                at = 512 * g + 256 * p + 32 * k
                copies.append(
                    pltpu.make_async_copy(
                        blocks[8 * p + k].at[pl.ds(32 * g, 32)],
                        weights.at[pl.ds(at, 32)],
                        sem.at[len(copies)],
                    )
                )
    for copy in copies:
        copy.start()
    first = 2 * (place[0] ^ theirs)
    for pick in (0, 2):

        @pl.when(first == pick)
        def _():
            for g in range(2):
                for j in range(2):
                    for p in range(2):
                        half = pl.ds(pl.multiple_of(256 * (place[1] ^ p), 256), 256)
                        rows[256 * j : 256 * j + 256, 512 * g + 256 * p : 512 * g + 256 * p + 256] = (
                            groups[2 * (pick + j) + g][:, half]
                        )

    for copy in copies:
        copy.wait()

    def step(n, carry):
        columns = pl.ds(pl.multiple_of(n * 256, 256), 256)
        total[:, columns] = jnp.dot(rows[...], weights[:, columns], preferred_element_type=F32)
        return carry

    lax.fori_loop(0, 7, step, 0)
    for d in range(4):
        span = slice(448 * d, 448 * d + 448)
        out[d] = jnp.concatenate([total[:256, span], total[256:, span]], 1).astype(out.dtype)


def whole(n):
    return [pl.BlockSpec(memory_space=VMEM)] * n


def scalars(n=1):
    return [pl.BlockSpec(memory_space=pltpu.MemorySpace.SMEM)] * n


def quarters(rows, x, y):
    return pl.pallas_call(
        quarter_kernel,
        out_shape=[jax.ShapeDtypeStruct((64, 1792), BF)] * 2,
        in_specs=scalars() + whole(1),
        out_specs=whole(2),
        name="quarters",
        cost_estimate=pl.CostEstimate(flops=0, bytes_accessed=2 << 20, transcendentals=0),
    )(jnp.stack([x, y]), rows)


def call(kernel, shapes, specs, args, name, flops, moved_bytes, scratch=()):
    many = isinstance(shapes, list)
    return pl.pallas_call(
        kernel,
        out_shape=shapes,
        in_specs=specs,
        out_specs=whole(len(shapes)) if many else whole(1)[0],
        scratch_shapes=list(scratch),
        compiler_params=pltpu.CompilerParams(vmem_limit_bytes=40 << 20),
        name=name,
        cost_estimate=pl.CostEstimate(
            flops=flops, bytes_accessed=moved_bytes, transcendentals=0
        ),
    )(*args)


def array(shape, kind=BF):
    return jax.ShapeDtypeStruct(shape, kind)


def project(theirs, place, groups, blocks, kind):
    return call(
        functools.partial(project_kernel, theirs),
        array((4, 256, 896), kind),
        scalars() + whole(8) + [pl.BlockSpec(memory_space=pl.ANY)] * 16,
        (place, *groups, *blocks),
        "project",
        2 * 512 * 1024 * 1792,
        8 << 20,
        [
            pltpu.VMEM((512, 1024), BF),
            pltpu.VMEM((1024, 1792), BF),
            pltpu.VMEM((512, 1792), F32),
            pltpu.SemaphoreType.DMA((32,)),
        ],
    )


def local(query_latent, key_rows, key_cache, prompt_start, w_query, w_key_up, w_value_up, w_output):
    yh, z, x, c, yl = (lax.axis_index(a) for a in AXES)
    y = 2 * yh + yl
    slab = 8 * yh + z
    own, given = quarters(w_output.reshape(64, 7168), x, y)

    half = lax.dynamic_slice_in_dim(key_rows, 128 * c, 128, 0)
    near, far = (
        lax.ppermute(half, CTX, [(i, i + by) for i in range(16 - by)]) for by in (1, 2)
    )
    swapped = other_core(jnp.concatenate([near, far], 0))

    other = xor_y(given, 3)
    blocks = [[own] + [None] * 7, [other] + [None] * 7]
    for p in range(2):
        up = down = blocks[p][0]
        for s in range(1, 5):
            if s < 4 or p == 0:
                up = up_z(up)
                blocks[p][8 - s] = up
            if s < 4 or p == 1:
                down = down_z(down)
                blocks[p][s] = down

    turn = turn_of(slab * 256 + jnp.arange(768, dtype=jnp.int32) - 512)
    queries = call(
        queries_kernel,
        array((2048, 640)),
        whole(4),
        (query_latent, w_query, w_key_up, turn[512:]),
        "queries",
        2 * 256 * 1536 * 1536 + 2 * 2048 * 128 * 512,
        8 << 20,
    )
    keys, hidden = call(
        keys_kernel,
        [array((768, 640)), array((256, 768), F32)],
        scalars() + whole(6),
        (jnp.stack([c, slab, prompt_start[0]]), key_rows, near, far, swapped, key_cache, turn),
        "keys",
        768 * 640 * 8,
        4 << 20,
    )
    column = jnp.arange(512, dtype=jnp.int32)
    source = (
        (column // 8 % 4) * 128 + (column // 256) * 64 + ((z + column // 32) % 8) * 8 + column % 8
    )
    reorder = (column[:, None] == source[None, :]).astype(BF)
    groups = [[None] * 2 for _ in range(4)]
    for g in range(2):
        rows = call(
            functools.partial(attend_kernel, g),
            array((256, 512)),
            whole(5),
            (queries, keys, hidden, w_value_up, reorder),
            "attend",
            2 * 1024 * 768 * 1152 + 2 * 1024 * 512 * 128,
            5 << 20,
        )
        groups[0][g] = rows
        for q in (2, 1, 3):
            groups[q][g] = xor_y(rows, q)
    place = jnp.stack([c, yh])
    rows = [part for slot in groups for part in slot]
    flat = blocks[0] + blocks[1]
    theirs = other_core(project(1, place, rows, flat, BF))
    mine = project(0, place, rows, flat, F32)
    sums = mine + theirs.astype(F32)
    result = sums[0]
    for d in (2, 1, 3):
        result = result + along_x(sums[d].astype(BF), d).astype(F32)
    result = result.astype(BF)
    pieces = [home(result[:, 448 * r : 448 * r + 448], r) for r in range(2)]
    even = yl == 0
    return jnp.concatenate(
        [jnp.where(even, pieces[0], pieces[1]), jnp.where(even, pieces[1], pieces[0])], 1
    )


def solution(mesh):
    cut = Mesh(mesh.devices.reshape(SIZES), AXES) if hasattr(mesh, "devices") else mesh
    tokens = ("yl", "yh", "z")
    return jax.shard_map(
        local,
        mesh=cut,
        in_specs=(
            P(tokens, None),
            P(tokens, None),
            P("yl", None),
            P("yl"),
            P(None, HEAD),
            P(HEAD, None, None),
            P(HEAD, None, None),
            P(HEAD, CTX, None),
        ),
        out_specs=P(tokens, HEAD),
        check_vma=False,
    )
```

```python
import functools

import jax
import jax.numpy as jnp
from jax import lax
from jax.experimental import pallas as pl
from jax.experimental.pallas import tpu as pltpu
from jax.sharding import Mesh
from jax.sharding import PartitionSpec as P

AXES = ("yh", "z", "x", "c", "yl")
SIZES = (2, 8, 4, 2, 2)
CTX = ("yh", "z")
HEAD = ("x", "c")
BF = jnp.bfloat16
F32 = jnp.float32
VMEM = pltpu.MemorySpace.VMEM


def number_of(yh, z, x, c, yl):
    return (((yh * 8 + z) * 4 + x) * 2 + c) * 2 + yl


def moved(a, target):
    pairs = []
    for yh in range(2):
        for z in range(8):
            for x in range(4):
                for c in range(2):
                    for yl in range(2):
                        t = target(yh, z, x, c, yl)
                        pairs.append((number_of(yh, z, x, c, yl), number_of(*t)))
    return lax.ppermute(a, AXES, pairs)


def up_z(a):
    return moved(a, lambda yh, z, x, c, yl: (yh, (z + 1) % 8, x, c, yl))


def down_z(a):
    return moved(a, lambda yh, z, x, c, yl: (yh, (z - 1) % 8, x, c, yl))


def xor_y(a, q):
    return moved(a, lambda yh, z, x, c, yl: (yh ^ (q >> 1), z, x, c, yl ^ (q & 1)))


def other_core(a):
    return moved(a, lambda yh, z, x, c, yl: (yh, z, x, 1 - c, yl))


def along_x(a, d):
    return moved(a, lambda yh, z, x, c, yl: (yh, z, (x + d) % 4, c, yl))


def home(a, r):
    return moved(a, lambda yh, z, x, c, yl: (yh ^ c, z, x, yh, yl ^ r))


def queries_kernel(rows, w_query, w_key_up, turn, out):
    cosine, sine = turn[:, :64], turn[:, 64:]
    for part in range(2):
        span = slice(768 * part, 768 * part + 768)
        queries = jnp.dot(rows[...], w_query[:, span], preferred_element_type=F32).astype(BF)
        for i in range(4):
            h = 4 * part + i
            plain = queries[:, 192 * i : 192 * i + 128]
            lat = jnp.dot(plain, w_key_up[h], preferred_element_type=F32)
            rot = queries[:, 192 * i + 128 : 192 * i + 192].astype(F32)
            other = jnp.concatenate([rot[:, 32:], rot[:, :32]], 1)
            rot = rot * cosine + other * sine
            tokens = slice(256 * h, 256 * h + 256)
            out[tokens, :512] = lat.astype(BF)
            out[tokens, 512:] = jnp.concatenate([rot, jnp.zeros_like(rot)], 1).astype(BF)


def keys_kernel(place, own, near, far, swapped, cache, turn, keys, hidden):
    c, slab, start = place[0], place[1], place[2]
    mine = pl.ds(pl.multiple_of(128 * c, 128), 128)
    theirs = pl.ds(pl.multiple_of(128 * (1 - c), 128), 128)
    keys[512:, :576] = own[...]
    keys[pl.ds(pl.multiple_of(256 + 128 * c, 128), 128), :576] = near[...]
    keys[pl.ds(pl.multiple_of(384 - 128 * c, 128), 128), :576] = swapped[:128]
    keys[mine, :576] = far[...]
    keys[theirs, :576] = swapped[128:]
    rot = keys[:, 512:576].astype(F32)
    other = jnp.concatenate([rot[:, 32:], rot[:, :32]], 1)
    rot = rot * turn[:, :64] + other * turn[:, 64:]
    keys[:, 512:] = jnp.concatenate([rot, jnp.zeros_like(rot)], 1).astype(BF)

    @pl.when(slab == 0)
    def _():
        keys[:512, :576] = cache[...]

    @pl.when(slab == 1)
    def _():
        keys[:256, :576] = cache[256:]

    row = lax.broadcasted_iota(jnp.int32, (256, 768), 0)
    col = lax.broadcasted_iota(jnp.int32, (256, 768), 1)
    relative = col - 512 - row
    visible = (relative <= 0) & (relative > -512) & (slab * 256 + col - 512 >= -start)
    hidden[...] = jnp.where(visible, 0.0, -1e30)


def attend_kernel(queries, keys, hidden, w_value_up, reorder, out):
    scale = 192.0**-0.5 * 1.4426950408889634
    latent = keys[:, :512]
    for group in range(2):
        heads = []
        for pair in range(2):
            first = 1024 * group + 512 * pair
            scores = lax.dot_general(
                queries[first : first + 512, :],
                keys[...],
                (((1,), (1,)), ((), ())),
                preferred_element_type=F32,
            )
            for i in range(2):
                part = scores[256 * i : 256 * i + 256] * scale + hidden[...]
                top = jnp.max(part, axis=1, keepdims=True)
                powers = jnp.exp2(part - top)
                share = 1.0 / jnp.sum(powers, axis=1, keepdims=True)
                mixed = jnp.dot(powers.astype(BF), latent, preferred_element_type=F32) * share
                attention = jnp.dot(
                    mixed.astype(BF),
                    w_value_up[4 * group + 2 * pair + i],
                    preferred_element_type=F32,
                )
                heads.append(attention.astype(BF))
        rows = jnp.concatenate(heads, 1)
        out[:, 512 * group : 512 * group + 512] = jnp.dot(
            rows, reorder[...], preferred_element_type=F32
        ).astype(BF)


def turn_of(positions):
    inverse = jnp.power(jnp.float32(10000.0), -jnp.arange(32, dtype=F32) * (2.0 / 64))
    angles = positions.astype(F32)[:, None] * inverse
    cosine, sine = jnp.cos(angles), jnp.sin(angles)
    return jnp.concatenate([cosine, cosine, -sine, sine], 1)


def quarter_kernel(place, rows, own, other):
    for out, flip in ((own, 0), (other, 3)):
        y = place[1] ^ flip
        odd = y % 2
        base = 896 * (y // 2) + 384 * odd
        pieces = []
        for d in range(4):
            start = pl.multiple_of(1792 * ((place[0] + d) % 4) + base, 128)
            wide = rows[:, pl.ds(start, 512)]
            pieces.append(jnp.where(odd == 1, wide[:, 64:], wide[:, :448]))
        out[...] = jnp.concatenate(pieces, 1)


def project_kernel(theirs, place, *refs):
    groups, gathered, blocks, (out, rows, weights, total, sem) = (
        refs[:4],
        refs[4],
        refs[5:13],
        refs[13:],
    )
    copies = []
    for p in range(2):
        for k in range(8):
            slot = k if p == 0 else (place[2] + k) % 8
            for g in range(2):
                at = pl.multiple_of(512 * g + 256 * p + 32 * slot, 32)
                block = gathered.at[k] if p == 0 else blocks[k]
                copies.append(
                    pltpu.make_async_copy(
                        block.at[pl.ds(32 * g, 32)], weights.at[pl.ds(at, 32)], sem.at[len(copies)]
                    )
                )
    for copy in copies:
        copy.start()
    first = 2 * (place[0] ^ theirs)
    for pick in (0, 2):

        @pl.when(first == pick)
        def _():
            for g in range(2):
                for j in range(2):
                    for p in range(2):
                        half = pl.ds(pl.multiple_of(512 * g + 256 * (place[1] ^ p), 256), 256)
                        rows[256 * j : 256 * j + 256, 512 * g + 256 * p : 512 * g + 256 * p + 256] = (
                            groups[pick + j][:, half]
                        )

    for copy in copies:
        copy.wait()

    def step(n, carry):
        columns = pl.ds(pl.multiple_of(n * 256, 256), 256)
        total[:, columns] = jnp.dot(rows[...], weights[:, columns], preferred_element_type=F32)
        return carry

    lax.fori_loop(0, 7, step, 0)
    for d in range(4):
        span = slice(448 * d, 448 * d + 448)
        out[d] = jnp.concatenate([total[:256, span], total[256:, span]], 1).astype(out.dtype)


def whole(n):
    return [pl.BlockSpec(memory_space=VMEM)] * n


def scalars(n=1):
    return [pl.BlockSpec(memory_space=pltpu.MemorySpace.SMEM)] * n


def quarters(rows, x, y):
    return pl.pallas_call(
        quarter_kernel,
        out_shape=[jax.ShapeDtypeStruct((64, 1792), BF)] * 2,
        in_specs=scalars() + whole(1),
        out_specs=whole(2),
        name="quarters",
        cost_estimate=pl.CostEstimate(flops=0, bytes_accessed=2 << 20, transcendentals=0),
    )(jnp.stack([x, y]), rows)


def call(kernel, shapes, specs, args, name, flops, moved_bytes, room, scratch=()):
    many = isinstance(shapes, list)
    return pl.pallas_call(
        kernel,
        out_shape=shapes,
        in_specs=specs,
        out_specs=whole(len(shapes)) if many else whole(1)[0],
        scratch_shapes=list(scratch),
        compiler_params=pltpu.CompilerParams(vmem_limit_bytes=room << 20),
        name=name,
        cost_estimate=pl.CostEstimate(
            flops=flops, bytes_accessed=moved_bytes, transcendentals=0
        ),
    )(*args)


def array(shape, kind=BF):
    return jax.ShapeDtypeStruct(shape, kind)


def project(theirs, place, groups, gathered, blocks, kind):
    return call(
        functools.partial(project_kernel, theirs),
        array((4, 256, 896), kind),
        scalars() + whole(4) + [pl.BlockSpec(memory_space=pl.ANY)] * 9,
        (place, *groups, gathered, *blocks),
        "project",
        2 * 512 * 1024 * 1792,
        8 << 20,
        20,
        [
            pltpu.VMEM((512, 1024), BF),
            pltpu.VMEM((1024, 1792), BF),
            pltpu.VMEM((512, 1792), F32),
            pltpu.SemaphoreType.DMA((32,)),
        ],
    )


def local(query_latent, key_rows, key_cache, prompt_start, w_query, w_key_up, w_value_up, w_output):
    yh, z, x, c, yl = (lax.axis_index(a) for a in AXES)
    y = 2 * yh + yl
    slab = 8 * yh + z
    own, given = quarters(w_output.reshape(64, 7168), x, y)

    half = lax.dynamic_slice_in_dim(key_rows, 128 * c, 128, 0)
    near, far = (
        lax.ppermute(half, CTX, [(i, i + by) for i in range(16 - by)]) for by in (1, 2)
    )
    swapped = other_core(jnp.concatenate([near, far], 0))

    gathered = lax.all_gather(own, "z", axis=0)
    other = xor_y(given, 3)
    blocks = [other] + [None] * 7
    up = down = other
    for s in range(1, 5):
        up = up_z(up)
        blocks[8 - s] = up
        if s < 4:
            down = down_z(down)
            blocks[s] = down

    turn = turn_of(slab * 256 + jnp.arange(768, dtype=jnp.int32) - 512)
    queries = call(
        queries_kernel,
        array((2048, 640)),
        whole(4),
        (query_latent, w_query, w_key_up, turn[512:]),
        "queries",
        2 * 256 * 1536 * 1536 + 2 * 2048 * 128 * 512,
        8 << 20,
        14,
    )
    keys, hidden = call(
        keys_kernel,
        [array((768, 640)), array((256, 768), F32)],
        scalars() + whole(6),
        (jnp.stack([c, slab, prompt_start[0]]), key_rows, near, far, swapped, key_cache, turn),
        "keys",
        768 * 640 * 8,
        4 << 20,
        8,
    )
    column = jnp.arange(512, dtype=jnp.int32)
    source = (
        (column // 8 % 4) * 128 + (column // 256) * 64 + (column // 32 % 8) * 8 + column % 8
    )
    reorder = (column[:, None] == source[None, :]).astype(BF)
    rows = call(
        attend_kernel,
        array((256, 1024)),
        whole(5),
        (queries, keys, hidden, w_value_up, reorder),
        "attend",
        4 * 1024 * 768 * 1152 + 4 * 1024 * 512 * 128,
        9 << 20,
        18,
    )
    groups = [rows] + [xor_y(rows, q) for q in (1, 2, 3)]
    place = jnp.stack([c, yh, z])
    theirs = other_core(project(1, place, groups, gathered, blocks, BF))
    mine = project(0, place, groups, gathered, blocks, F32)
    sums = mine + theirs.astype(F32)
    result = sums[0]
    for d in (1, 3, 2):
        result = result + along_x(sums[d].astype(BF), d).astype(F32)
    result = result.astype(BF)
    pieces = [home(result[:, 448 * r : 448 * r + 448], r) for r in range(2)]
    even = yl == 0
    return jnp.concatenate(
        [jnp.where(even, pieces[0], pieces[1]), jnp.where(even, pieces[1], pieces[0])], 1
    )


def solution(mesh):
    cut = Mesh(mesh.devices.reshape(SIZES), AXES) if hasattr(mesh, "devices") else mesh
    tokens = ("yl", "yh", "z")
    return jax.shard_map(
        local,
        mesh=cut,
        in_specs=(
            P(tokens, None),
            P(tokens, None),
            P("yl", None),
            P("yl"),
            P(None, HEAD),
            P(HEAD, None, None),
            P(HEAD, None, None),
            P(HEAD, CTX, None),
        ),
        out_specs=P(tokens, HEAD),
        check_vma=False,
    )
```

```python
import functools

import jax
import jax.numpy as jnp
from jax import lax
from jax.experimental import pallas as pl
from jax.experimental.pallas import tpu as pltpu
from jax.sharding import Mesh
from jax.sharding import PartitionSpec as P

AXES = ("yh", "z", "x", "c", "yl")
SIZES = (2, 8, 4, 2, 2)
CTX = ("yh", "z")
HEAD = ("x", "c")
BF = jnp.bfloat16
F32 = jnp.float32
VMEM = pltpu.MemorySpace.VMEM


def number_of(yh, z, x, c, yl):
    return (((yh * 8 + z) * 4 + x) * 2 + c) * 2 + yl


def moved(a, target):
    pairs = []
    for yh in range(2):
        for z in range(8):
            for x in range(4):
                for c in range(2):
                    for yl in range(2):
                        t = target(yh, z, x, c, yl)
                        pairs.append((number_of(yh, z, x, c, yl), number_of(*t)))
    return lax.ppermute(a, AXES, pairs)


def up_z(a):
    return moved(a, lambda yh, z, x, c, yl: (yh, (z + 1) % 8, x, c, yl))


def down_z(a):
    return moved(a, lambda yh, z, x, c, yl: (yh, (z - 1) % 8, x, c, yl))


def xor_y(a, q):
    return moved(a, lambda yh, z, x, c, yl: (yh ^ (q >> 1), z, x, c, yl ^ (q & 1)))


def other_core(a):
    return moved(a, lambda yh, z, x, c, yl: (yh, z, x, 1 - c, yl))


def along_x(a, d):
    return moved(a, lambda yh, z, x, c, yl: (yh, z, (x + d) % 4, c, yl))


def home(a, r):
    return moved(a, lambda yh, z, x, c, yl: (yh ^ c, z, x, yh, yl ^ r))


def queries_kernel(rows, w_query, w_key_up, turn, out, held, sem):
    copies = [
        pltpu.make_async_copy(w_query.at[:, pl.ds(768 * part, 768)], held.at[part], sem.at[part])
        for part in range(2)
    ]
    for copy in copies:
        copy.start()
    cosine, sine = turn[512:, :64], turn[512:, 64:]
    for part in range(2):
        copies[part].wait()
        queries = jnp.dot(rows[...], held[part], preferred_element_type=F32).astype(BF)
        for i in range(4):
            h = 4 * part + i
            plain = queries[:, 192 * i : 192 * i + 128]
            lat = jnp.dot(plain, w_key_up[h], preferred_element_type=F32)
            rot = queries[:, 192 * i + 128 : 192 * i + 192].astype(F32)
            other = jnp.concatenate([rot[:, 32:], rot[:, :32]], 1)
            rot = rot * cosine + other * sine
            tokens = slice(256 * h, 256 * h + 256)
            out[tokens, :512] = lat.astype(BF)
            out[tokens, 512:] = jnp.concatenate([rot, jnp.zeros_like(rot)], 1).astype(BF)


def keys_kernel(start, own, near, far, swapped, cache, turn, keys, hidden, raw, sem):
    c = lax.axis_index("c")
    slab = 8 * lax.axis_index("yh") + lax.axis_index("z")

    def at(row, rows):
        return raw.at[pl.ds(pl.multiple_of(row, 128), rows)]

    copies = [
        pltpu.make_async_copy(own, at(512, 256), sem.at[0]),
        pltpu.make_async_copy(near, at(256 + 128 * c, 128), sem.at[1]),
        pltpu.make_async_copy(swapped.at[pl.ds(0, 128)], at(384 - 128 * c, 128), sem.at[2]),
        pltpu.make_async_copy(far, at(128 * c, 128), sem.at[3]),
        pltpu.make_async_copy(swapped.at[pl.ds(128, 128)], at(128 - 128 * c, 128), sem.at[4]),
    ]
    for copy in copies:
        copy.start()
    row = lax.broadcasted_iota(jnp.int32, (256, 768), 0)
    col = lax.broadcasted_iota(jnp.int32, (256, 768), 1)
    relative = col - 512 - row
    visible = (relative <= 0) & (relative > -512) & (slab * 256 + col - 512 >= -start[0])
    hidden[...] = jnp.where(visible, 0.0, -1e30)
    for copy in copies:
        copy.wait()
    rot = raw[:, 512:].astype(F32)
    other = jnp.concatenate([rot[:, 32:], rot[:, :32]], 1)
    rot = rot * turn[:, :64] + other * turn[:, 64:]
    keys[:, :512] = raw[:, :512]
    keys[:, 512:] = jnp.concatenate([rot, jnp.zeros_like(rot)], 1).astype(BF)

    @pl.when(slab < 2)
    def _():
        copy = pltpu.make_async_copy(cache, at(0, 512), sem.at[0])
        copy.start()
        copy.wait()

    @pl.when(slab == 0)
    def _():
        keys[:512, :576] = raw[:512]

    @pl.when(slab == 1)
    def _():
        keys[:256, :576] = raw[256:512]


def attend_kernel(queries, keys, hidden, w_value_up, reorder, out):
    scale = 192.0**-0.5 * 1.4426950408889634
    latent = keys[:, :512]

    def step(group, carry):
        heads = []
        for pair in range(2):
            first = pl.multiple_of(1024 * group + 512 * pair, 512)
            scores = lax.dot_general(
                queries[pl.ds(first, 512), :],
                keys[...],
                (((1,), (1,)), ((), ())),
                preferred_element_type=F32,
            )
            for i in range(2):
                part = scores[256 * i : 256 * i + 256] * scale + hidden[...]
                top = jnp.max(part, axis=1, keepdims=True)
                powers = jnp.exp2(part - top)
                share = 1.0 / jnp.sum(powers, axis=1, keepdims=True)
                mixed = jnp.dot(powers.astype(BF), latent, preferred_element_type=F32) * share
                attention = jnp.dot(
                    mixed.astype(BF),
                    w_value_up[4 * group + 2 * pair + i],
                    preferred_element_type=F32,
                )
                heads.append(attention.astype(BF))
        rows = jnp.concatenate(heads, 1)
        columns = pl.ds(pl.multiple_of(512 * group, 512), 512)
        out[:, columns] = jnp.dot(rows, reorder[...], preferred_element_type=F32).astype(BF)
        return carry

    lax.fori_loop(0, 2, step, 0)


def turn_of(positions):
    inverse = jnp.power(jnp.float32(10000.0), -jnp.arange(32, dtype=F32) * (2.0 / 64))
    angles = positions.astype(F32)[:, None] * inverse
    cosine, sine = jnp.cos(angles), jnp.sin(angles)
    return jnp.concatenate([cosine, cosine, -sine, sine], 1)


def quarter_kernel(rows, own, other):
    x = lax.axis_index("x")
    for out, flip in ((own, 0), (other, 1)):
        odd = lax.axis_index("yl") ^ flip
        base = 896 * (lax.axis_index("yh") ^ flip) + 384 * odd
        pieces = []
        for d in range(4):
            start = pl.multiple_of(1792 * ((x + d) % 4) + base, 128)
            wide = rows[:, pl.ds(start, 512)]
            pieces.append(jnp.where(odd == 1, wide[:, 64:], wide[:, :448]))
        out[...] = jnp.concatenate(pieces, 1)


def project_kernel(theirs, *refs):
    groups, blocks, (out, rows, total) = refs[:4], refs[4:20], refs[20:]
    first = 2 * (lax.axis_index("c") ^ theirs)
    yh = lax.axis_index("yh")
    for pick in (0, 2):

        @pl.when(first == pick)
        def _():
            for g in range(2):
                for j in range(2):
                    for p in range(2):
                        half = pl.ds(pl.multiple_of(512 * g + 256 * (yh ^ p), 256), 256)
                        rows[256 * j : 256 * j + 256, 512 * g + 256 * p : 512 * g + 256 * p + 256] = (
                            groups[pick + j][:, half]
                        )

    for n in range(7):
        columns = slice(256 * n, 256 * n + 256)
        weights = jnp.concatenate(
            [
                block[32 * g : 32 * g + 32, columns]
                for g in range(2)
                for block in blocks
            ],
            0,
        )
        total[:, columns] = jnp.dot(rows[...], weights, preferred_element_type=F32)
    for d in range(4):
        span = slice(448 * d, 448 * d + 448)
        for j in range(2):
            top = total[256 * j : 256 * j + 128, span]
            low = total[256 * j + 128 : 256 * j + 256, span]
            out[d, 128 * j : 128 * j + 128] = jnp.concatenate([top, low], 1).astype(out.dtype)


def whole(n):
    return [pl.BlockSpec(memory_space=VMEM)] * n


def placed(n):
    return [pl.BlockSpec(memory_space=pl.ANY)] * n


def scalars(n=1):
    return [pl.BlockSpec(memory_space=pltpu.MemorySpace.SMEM)] * n


def quarters(rows):
    return pl.pallas_call(
        quarter_kernel,
        out_shape=[jax.ShapeDtypeStruct((64, 1792), BF)] * 2,
        in_specs=whole(1),
        out_specs=whole(2),
        name="quarters",
        cost_estimate=pl.CostEstimate(flops=0, bytes_accessed=2 << 20, transcendentals=0),
    )(rows)


def call(kernel, shapes, specs, args, name, flops, moved_bytes, room, scratch=()):
    many = isinstance(shapes, list)
    return pl.pallas_call(
        kernel,
        out_shape=shapes,
        in_specs=specs,
        out_specs=whole(len(shapes)) if many else whole(1)[0],
        scratch_shapes=list(scratch),
        compiler_params=pltpu.CompilerParams(vmem_limit_bytes=room << 20),
        name=name,
        cost_estimate=pl.CostEstimate(
            flops=flops, bytes_accessed=moved_bytes, transcendentals=0
        ),
    )(*args)


def array(shape, kind=BF):
    return jax.ShapeDtypeStruct(shape, kind)


def after(value, *others):
    return lax.optimization_barrier((value, *others))[0]


def project(theirs, groups, blocks, kind):
    return call(
        functools.partial(project_kernel, theirs),
        array((4, 256, 896), kind),
        whole(20),
        (*groups, *blocks),
        "project",
        2 * 512 * 1024 * 1792,
        8 << 20,
        12,
        [pltpu.VMEM((512, 1024), BF), pltpu.VMEM((512, 1792), F32)],
    )


def local(query_latent, key_rows, key_cache, prompt_start, w_query, w_key_up, w_value_up, w_output):
    yh, z, x, c, yl = (lax.axis_index(a) for a in AXES)
    slab = 8 * yh + z
    own, given = quarters(w_output.reshape(64, 7168))
    other = xor_y(given, 3)
    ups, downs = [up_z(own)], [down_z(own)]

    half = lax.dynamic_slice_in_dim(key_rows, 128 * c, 128, 0)
    near, far = (
        lax.ppermute(half, CTX, [(i, i + by) for i in range(16 - by)]) for by in (1, 2)
    )
    turn = turn_of(slab * 256 + jnp.arange(768, dtype=jnp.int32) - 512)
    queries = call(
        queries_kernel,
        array((2048, 640)),
        whole(1) + placed(1) + whole(2),
        (query_latent, w_query, w_key_up, turn),
        "queries",
        2 * 256 * 1536 * 1536 + 2 * 2048 * 128 * 512,
        8 << 20,
        14,
        [pltpu.VMEM((2, 1536, 768), BF), pltpu.SemaphoreType.DMA((2,))],
    )
    swapped = other_core(jnp.concatenate([near, far], 0))
    ups.append(up_z(after(ups[0], queries)))
    downs.append(down_z(after(downs[0], queries)))
    ups_other, downs_other = [up_z(other)], [down_z(other)]

    keys, hidden = call(
        keys_kernel,
        [array((768, 640)), array((256, 768), F32)],
        scalars() + placed(5) + whole(1),
        (prompt_start, key_rows, near, far, swapped, key_cache, turn),
        "keys",
        768 * 640 * 8,
        4 << 20,
        8,
        [pltpu.VMEM((768, 576), BF), pltpu.SemaphoreType.DMA((5,))],
    )
    column = jnp.arange(512, dtype=jnp.int32)
    source = (
        (column // 8 % 4) * 128 + (column // 256) * 64 + ((z + column // 32) % 8) * 8 + column % 8
    )
    reorder = (column[:, None] == source[None, :]).astype(BF)
    rows = call(
        attend_kernel,
        array((256, 1024)),
        whole(5),
        (queries, keys, hidden, w_value_up, reorder),
        "attend",
        4 * 1024 * 768 * 1152 + 4 * 1024 * 512 * 128,
        9 << 20,
        18,
    )
    groups = [rows] + [xor_y(rows, q) for q in (2, 1, 3)]
    groups = [groups[i] for i in (0, 2, 1, 3)]
    ups.append(up_z(after(ups[1], rows)))
    downs.append(down_z(after(downs[1], rows)))
    ups_other.append(up_z(after(ups_other[0], rows)))
    downs_other.append(down_z(after(downs_other[0], rows)))
    ups.append(up_z(ups[2]))
    ups_other.append(up_z(ups_other[1]))
    downs_other.append(down_z(downs_other[1]))
    downs_other.append(down_z(downs_other[2]))
    blocks = [own, *downs, *ups[::-1], other, *downs_other, *ups_other[::-1]]

    theirs = project(1, groups, blocks, BF)
    first = other_core(theirs[2])
    rest = other_core(jnp.concatenate([theirs[:2], theirs[3:]], 0))
    mine = project(0, groups, blocks, F32)
    sums = [None] * 4
    sums[2] = (mine[2] + first.astype(F32)).astype(BF)
    for i, d in enumerate((0, 1, 3)):
        sums[d] = mine[d] + rest[i].astype(F32)
    passing_up = along_x(sums[2][:128], 1)
    passing_down = along_x(sums[2][128:], 3)
    early_up = along_x(sums[1][128:].astype(BF), 1)
    early_down = along_x(sums[3][:128].astype(BF), 3)
    late_up = along_x((sums[1][:128] + passing_up.astype(F32)).astype(BF), 1)
    late_down = along_x((sums[3][128:] + passing_down.astype(F32)).astype(BF), 3)
    pieces = [
        home((sums[0][:128] + late_up.astype(F32) + early_down.astype(F32)).astype(BF), 0),
        home((sums[0][128:] + early_up.astype(F32) + late_down.astype(F32)).astype(BF), 1),
    ]
    even = yl == 0
    pair = jnp.where(even, pieces[0], pieces[1]), jnp.where(even, pieces[1], pieces[0])
    return jnp.concatenate(
        [jnp.concatenate([p[:, 448 * i : 448 * i + 448] for p in pair], 1) for i in range(2)], 0
    )


def solution(mesh):
    cut = Mesh(mesh.devices.reshape(SIZES), AXES) if hasattr(mesh, "devices") else mesh
    tokens = ("yl", "yh", "z")
    return jax.shard_map(
        local,
        mesh=cut,
        in_specs=(
            P(tokens, None),
            P(tokens, None),
            P("yl", None),
            P("yl"),
            P(None, HEAD),
            P(HEAD, None, None),
            P(HEAD, None, None),
            P(HEAD, CTX, None),
        ),
        out_specs=P(tokens, HEAD),
        check_vma=False,
    )
```

```python
import functools

import jax
import jax.numpy as jnp
from jax import lax
from jax.experimental import pallas as pl
from jax.experimental.pallas import tpu as pltpu
from jax.sharding import Mesh
from jax.sharding import PartitionSpec as P

AXES = ("yh", "z", "x", "c", "yl")
SIZES = (2, 8, 4, 2, 2)
CTX = ("yh", "z")
HEAD = ("x", "c")
BF = jnp.bfloat16
F32 = jnp.float32
VMEM = pltpu.MemorySpace.VMEM


def number_of(yh, z, x, c, yl):
    return (((yh * 8 + z) * 4 + x) * 2 + c) * 2 + yl


def moved(a, target):
    pairs = []
    for yh in range(2):
        for z in range(8):
            for x in range(4):
                for c in range(2):
                    for yl in range(2):
                        t = target(yh, z, x, c, yl)
                        pairs.append((number_of(yh, z, x, c, yl), number_of(*t)))
    return lax.ppermute(a, AXES, pairs)


def up_z(a):
    return moved(a, lambda yh, z, x, c, yl: (yh, (z + 1) % 8, x, c, yl))


def down_z(a):
    return moved(a, lambda yh, z, x, c, yl: (yh, (z - 1) % 8, x, c, yl))


def xor_y(a, q):
    return moved(a, lambda yh, z, x, c, yl: (yh ^ (q >> 1), z, x, c, yl ^ (q & 1)))


def other_core(a):
    return moved(a, lambda yh, z, x, c, yl: (yh, z, x, 1 - c, yl))


def along_x(a, d):
    return moved(a, lambda yh, z, x, c, yl: (yh, z, (x + d) % 4, c, yl))


def home(a, r):
    return moved(a, lambda yh, z, x, c, yl: (yh ^ c, z, x, yh, yl ^ r))


def turn_of(table, block):
    rows = slice(64 * block, 64 * block + 64)
    return jnp.concatenate([table[rows, 32 * i : 32 * i + 32] for i in range(4)], 0)


def turned(rot, cosine, sine):
    other = jnp.concatenate([rot[:, 32:], rot[:, :32]], 1)
    cosine = jnp.concatenate([cosine, cosine], 1)
    sine = jnp.concatenate([-sine, sine], 1)
    rot = rot * cosine + other * sine
    return jnp.concatenate([rot, jnp.zeros_like(rot)], 1).astype(BF)


def queries_kernel(rows, w_query, w_key_up, cosines, sines, out, held, rows_held, sem):
    copies = [
        pltpu.make_async_copy(w_query.at[:, pl.ds(768 * part, 768)], held.at[part], sem.at[part])
        for part in range(2)
    ]
    copies.append(pltpu.make_async_copy(rows, rows_held, sem.at[2]))
    for i in (2, 0, 1):
        copies[i].start()
    cosine, sine = turn_of(cosines, 2), turn_of(sines, 2)
    copies[2].wait()
    for part in range(2):
        copies[part].wait()
        queries = jnp.dot(rows_held[...], held[part], preferred_element_type=F32).astype(BF)
        for i in range(4):
            h = 4 * part + i
            plain = queries[:, 192 * i : 192 * i + 128]
            lat = jnp.dot(plain, w_key_up[h], preferred_element_type=F32)
            rot = queries[:, 192 * i + 128 : 192 * i + 192].astype(F32)
            tokens = slice(256 * h, 256 * h + 256)
            out[tokens, :512] = lat.astype(BF)
            out[tokens, 512:] = turned(rot, cosine, sine)


def keys_kernel(start, own, near, far, swapped, cache, cosines, sines, keys, hidden, raw, sem):
    c = lax.axis_index("c")
    slab = 8 * lax.axis_index("yh") + lax.axis_index("z")

    def at(row, rows):
        return raw.at[pl.ds(pl.multiple_of(row, 128), rows)]

    copies = [
        pltpu.make_async_copy(own, at(512, 256), sem.at[0]),
        pltpu.make_async_copy(near, at(256 + 128 * c, 128), sem.at[1]),
        pltpu.make_async_copy(swapped.at[pl.ds(0, 128)], at(384 - 128 * c, 128), sem.at[2]),
        pltpu.make_async_copy(far, at(128 * c, 128), sem.at[3]),
        pltpu.make_async_copy(swapped.at[pl.ds(128, 128)], at(128 - 128 * c, 128), sem.at[4]),
    ]
    for copy in copies:
        copy.start()
    row = lax.broadcasted_iota(jnp.int32, (256, 768), 0)
    col = lax.broadcasted_iota(jnp.int32, (256, 768), 1)
    relative = col - 512 - row
    visible = (relative <= 0) & (relative > -512) & (slab * 256 + col - 512 >= -start[0])
    hidden[...] = jnp.where(visible, 0.0, -1e30)
    for copy in copies:
        copy.wait()
    keys[:, :512] = raw[:, :512]
    for block in range(3):
        tokens = slice(256 * block, 256 * block + 256)
        keys[tokens, 512:] = turned(
            raw[tokens, 512:].astype(F32), turn_of(cosines, block), turn_of(sines, block)
        )

    @pl.when(slab < 2)
    def _():
        copy = pltpu.make_async_copy(cache, at(0, 512), sem.at[0])
        copy.start()
        copy.wait()

    @pl.when(slab == 0)
    def _():
        keys[:512, :576] = raw[:512]

    @pl.when(slab == 1)
    def _():
        keys[:256, :576] = raw[256:512]


def attend_kernel(queries, keys, hidden, w_value_up, reorder, out):
    scale = 192.0**-0.5 * 1.4426950408889634
    latent = keys[:, :512]

    def step(group, carry):
        heads = []
        for pair in range(2):
            first = pl.multiple_of(1024 * group + 512 * pair, 512)
            scores = lax.dot_general(
                queries[pl.ds(first, 512), :],
                keys[...],
                (((1,), (1,)), ((), ())),
                preferred_element_type=F32,
            )
            for i in range(2):
                part = scores[256 * i : 256 * i + 256] * scale + hidden[...]
                top = jnp.max(part, axis=1, keepdims=True)
                powers = jnp.exp2(part - top)
                share = 1.0 / jnp.sum(powers, axis=1, keepdims=True)
                mixed = jnp.dot(powers.astype(BF), latent, preferred_element_type=F32) * share
                attention = jnp.dot(
                    mixed.astype(BF),
                    w_value_up[4 * group + 2 * pair + i],
                    preferred_element_type=F32,
                )
                heads.append(attention.astype(BF))
        rows = jnp.concatenate(heads, 1)
        columns = pl.ds(pl.multiple_of(512 * group, 512), 512)
        out[:, columns] = jnp.dot(rows, reorder[...], preferred_element_type=F32).astype(BF)
        return carry

    lax.fori_loop(0, 2, step, 0)


def turns(first):
    inverse = jnp.power(jnp.float32(10000.0), -jnp.arange(32, dtype=F32) * (2.0 / 64))
    row = lax.broadcasted_iota(jnp.int32, (192, 128), 0)
    lane = lax.broadcasted_iota(jnp.int32, (192, 128), 1)
    place = first + (row // 64) * 256 + (lane // 32) * 64 + row % 64
    angles = place.astype(F32) * jnp.tile(inverse, 4)[None, :]
    return jnp.cos(angles), jnp.sin(angles)


def quarter_kernel(rows, own, other):
    x = lax.axis_index("x")
    for out, flip in ((own, 0), (other, 1)):
        odd = lax.axis_index("yl") ^ flip
        base = 896 * (lax.axis_index("yh") ^ flip) + 384 * odd
        pieces = []
        for d in range(4):
            start = pl.multiple_of(1792 * ((x + d) % 4) + base, 128)
            wide = rows[:, pl.ds(start, 512)]
            pieces.append(jnp.where(odd == 1, wide[:, 64:], wide[:, :448]))
        out[...] = jnp.concatenate(pieces, 1)


def project_kernel(theirs, *refs):
    groups, held, (out, rows, total) = refs[:4], refs[4:17], refs[17:]
    own, d1, d2, d3, u4, u3, u2, u1, other, e1, e3, e4, v1 = held
    blocks = [own, d1, d2, d3.at[:64], u4.at[:64], u3.at[:64], u2, u1]
    blocks += [other, e1, d3.at[64:], e3, e4, u4.at[64:], u3.at[64:], v1]
    first = 2 * (lax.axis_index("c") ^ theirs)
    yh = lax.axis_index("yh")
    for pick in (0, 2):

        @pl.when(first == pick)
        def _():
            for g in range(2):
                for j in range(2):
                    for p in range(2):
                        half = pl.ds(pl.multiple_of(512 * g + 256 * (yh ^ p), 256), 256)
                        rows[256 * j : 256 * j + 256, 512 * g + 256 * p : 512 * g + 256 * p + 256] = (
                            groups[pick + j][:, half]
                        )

    for n in range(7):
        columns = slice(256 * n, 256 * n + 256)
        weights = jnp.concatenate(
            [
                block[32 * g : 32 * g + 32, columns]
                for g in range(2)
                for block in blocks
            ],
            0,
        )
        total[:, columns] = jnp.dot(rows[...], weights, preferred_element_type=F32)
    for d in range(4):
        span = slice(448 * d, 448 * d + 448)
        for j in range(2):
            top = total[256 * j : 256 * j + 128, span]
            low = total[256 * j + 128 : 256 * j + 256, span]
            out[d, 128 * j : 128 * j + 128] = jnp.concatenate([top, low], 1).astype(out.dtype)


def whole(n):
    return [pl.BlockSpec(memory_space=VMEM)] * n


def placed(n):
    return [pl.BlockSpec(memory_space=pl.ANY)] * n


def kept(n=1):
    return [pl.BlockSpec(memory_space=pltpu.MemorySpace.HBM)] * n


def scalars(n=1):
    return [pl.BlockSpec(memory_space=pltpu.MemorySpace.SMEM)] * n


def quarters(rows):
    return pl.pallas_call(
        quarter_kernel,
        out_shape=[jax.ShapeDtypeStruct((64, 1792), BF)] * 2,
        in_specs=whole(1),
        out_specs=whole(2),
        name="quarters",
        cost_estimate=pl.CostEstimate(flops=0, bytes_accessed=2 << 20, transcendentals=0),
    )(rows)


def call(kernel, shapes, specs, args, name, flops, moved_bytes, room, scratch=()):
    many = isinstance(shapes, list)
    return pl.pallas_call(
        kernel,
        out_shape=shapes,
        in_specs=specs,
        out_specs=whole(len(shapes)) if many else whole(1)[0],
        scratch_shapes=list(scratch),
        compiler_params=pltpu.CompilerParams(vmem_limit_bytes=room << 20),
        name=name,
        cost_estimate=pl.CostEstimate(
            flops=flops, bytes_accessed=moved_bytes, transcendentals=0
        ),
    )(*args)


def array(shape, kind=BF):
    return jax.ShapeDtypeStruct(shape, kind)


def after(value, *others):
    return lax.optimization_barrier((value, *others))[0]


def project(theirs, groups, blocks, kind):
    return call(
        functools.partial(project_kernel, theirs),
        array((4, 256, 896), kind),
        whole(17),
        (*groups, *blocks),
        "project",
        2 * 512 * 1024 * 1792,
        8 << 20,
        12,
        [pltpu.VMEM((512, 1024), BF), pltpu.VMEM((512, 1792), F32)],
    )


def local(query_latent, key_rows, key_cache, prompt_start, w_query, w_key_up, w_value_up, w_output):
    yh, z, x, c, yl = (lax.axis_index(a) for a in AXES)
    slab = 8 * yh + z
    own, given = quarters(w_output.reshape(64, 7168))
    other = xor_y(given, 3)
    u1, d1 = up_z(own), down_z(own)

    half = lax.dynamic_slice_in_dim(key_rows, 128 * c, 128, 0)
    near, far = (
        lax.ppermute(half, CTX, [(i, i + by) for i in range(16 - by)]) for by in (1, 2)
    )
    cosines, sines = turns(slab * 256 - 512)
    queries = call(
        queries_kernel,
        array((2048, 640)),
        kept(2) + whole(3),
        (query_latent, w_query, w_key_up, cosines, sines),
        "queries",
        2 * 256 * 1536 * 1536 + 2 * 2048 * 128 * 512,
        8 << 20,
        14,
        [
            pltpu.VMEM((2, 1536, 768), BF),
            pltpu.VMEM((256, 1536), BF),
            pltpu.SemaphoreType.DMA((3,)),
        ],
    )
    swapped = other_core(jnp.concatenate([near, far], 0))
    u2, d2 = up_z(after(u1, queries)), down_z(after(d1, queries))
    v1, e1 = up_z(other), down_z(other)

    keys, hidden = call(
        keys_kernel,
        [array((768, 640)), array((256, 768), F32)],
        scalars() + kept() + placed(3) + kept() + whole(2),
        (prompt_start, key_rows, near, far, swapped, key_cache, cosines, sines),
        "keys",
        768 * 640 * 8,
        4 << 20,
        8,
        [pltpu.VMEM((768, 576), BF), pltpu.SemaphoreType.DMA((5,))],
    )
    column = jnp.arange(512, dtype=jnp.int32)
    source = (
        (column // 8 % 4) * 128 + (column // 256) * 64 + ((z + column // 32) % 8) * 8 + column % 8
    )
    reorder = (column[:, None] == source[None, :]).astype(BF)
    rows = call(
        attend_kernel,
        array((256, 1024)),
        whole(5),
        (queries, keys, hidden, w_value_up, reorder),
        "attend",
        4 * 1024 * 768 * 1152 + 4 * 1024 * 512 * 128,
        9 << 20,
        18,
    )
    groups = [rows] + [xor_y(rows, q) for q in (2, 1, 3)]
    groups = [groups[i] for i in (0, 2, 1, 3)]
    u3 = up_z(after(jnp.concatenate([u2, v1], 0), rows))
    d3 = down_z(after(jnp.concatenate([d2, e1], 0), rows))
    u4 = up_z(u3)
    e3 = down_z(d3[64:])
    e4 = down_z(e3)
    blocks = [own, d1, d2, d3, u4, u3, u2, u1, other, e1, e3, e4, v1]

    theirs = other_core(project(1, groups, blocks, BF))
    mine = project(0, groups, blocks, F32)
    far_sum = (mine[2] + theirs[2].astype(F32)).astype(BF)
    passing_up = along_x(far_sum[:128], 1)
    passing_down = along_x(far_sum[128:], 3)
    sums = [mine[d] + theirs[d].astype(F32) for d in (0, 1, 3)]
    early_up, early_down = lax.optimization_barrier(
        (sums[1][128:].astype(BF), sums[2][:128].astype(BF))
    )
    early_up, early_down = along_x(early_up, 1), along_x(early_down, 3)
    late_up = along_x((sums[1][:128] + passing_up.astype(F32)).astype(BF), 1)
    late_down = along_x((sums[2][128:] + passing_down.astype(F32)).astype(BF), 3)
    pieces = [
        home((sums[0][:128] + late_up.astype(F32) + early_down.astype(F32)).astype(BF), 0),
        home((sums[0][128:] + early_up.astype(F32) + late_down.astype(F32)).astype(BF), 1),
    ]
    even = yl == 0
    pair = jnp.where(even, pieces[0], pieces[1]), jnp.where(even, pieces[1], pieces[0])
    return jnp.concatenate(
        [jnp.concatenate([p[:, 448 * i : 448 * i + 448] for p in pair], 1) for i in range(2)], 0
    )


def solution(mesh):
    cut = Mesh(mesh.devices.reshape(SIZES), AXES) if hasattr(mesh, "devices") else mesh
    tokens = ("yl", "yh", "z")
    return jax.shard_map(
        local,
        mesh=cut,
        in_specs=(
            P(tokens, None),
            P(tokens, None),
            P("yl", None),
            P("yl"),
            P(None, HEAD),
            P(HEAD, None, None),
            P(HEAD, None, None),
            P(HEAD, CTX, None),
        ),
        out_specs=P(tokens, HEAD),
        check_vma=False,
    )
```

```python
import functools

import jax
import jax.numpy as jnp
from jax import lax
from jax.experimental import pallas as pl
from jax.experimental.pallas import tpu as pltpu
from jax.sharding import Mesh
from jax.sharding import PartitionSpec as P

AXES = ("yh", "z", "x", "c", "yl")
SIZES = (2, 8, 4, 2, 2)
CTX = ("yh", "z")
HEAD = ("x", "c")
BF = jnp.bfloat16
F32 = jnp.float32
VMEM = pltpu.MemorySpace.VMEM


def number_of(yh, z, x, c, yl):
    return (((yh * 8 + z) * 4 + x) * 2 + c) * 2 + yl


def moved(a, target):
    pairs = []
    for yh in range(2):
        for z in range(8):
            for x in range(4):
                for c in range(2):
                    for yl in range(2):
                        t = target(yh, z, x, c, yl)
                        pairs.append((number_of(yh, z, x, c, yl), number_of(*t)))
    return lax.ppermute(a, AXES, pairs)


def up_z(a):
    return moved(a, lambda yh, z, x, c, yl: (yh, (z + 1) % 8, x, c, yl))


def down_z(a):
    return moved(a, lambda yh, z, x, c, yl: (yh, (z - 1) % 8, x, c, yl))


def xor_y(a, q):
    return moved(a, lambda yh, z, x, c, yl: (yh ^ (q >> 1), z, x, c, yl ^ (q & 1)))


def other_core(a):
    return moved(a, lambda yh, z, x, c, yl: (yh, z, x, 1 - c, yl))


def along_x(a, d):
    return moved(a, lambda yh, z, x, c, yl: (yh, z, (x + d) % 4, c, yl))


def home(a, r):
    return moved(a, lambda yh, z, x, c, yl: (yh ^ c, z, x, yh, yl ^ r))


def turn_of(table):
    return jnp.concatenate([table[:, 32 * i : 32 * i + 32] for i in range(4)], 0)


def turned(rot, cosine, sine):
    other = jnp.concatenate([rot[:, 32:], rot[:, :32]], 1)
    cosine = jnp.concatenate([cosine, cosine], 1)
    sine = jnp.concatenate([-sine, sine], 1)
    rot = rot * cosine + other * sine
    return jnp.concatenate([rot, jnp.zeros_like(rot)], 1).astype(BF)


def queries_kernel(rows, w_query, w_key_up, cosines, sines, out, out_next, held, rows_held, sem):
    copies = [
        pltpu.make_async_copy(w_query.at[:, pl.ds(768 * part, 768)], held.at[part], sem.at[part])
        for part in range(2)
    ]
    copies.append(pltpu.make_async_copy(rows, rows_held, sem.at[2]))
    for i in (2, 0, 1):
        copies[i].start()
    cosine, sine = turn_of(cosines), turn_of(sines)
    copies[2].wait()
    for part in range(2):
        copies[part].wait()
        queries = jnp.dot(rows_held[...], held[part], preferred_element_type=F32).astype(BF)
        for i in range(4):
            h = 4 * part + i
            plain = queries[:, 192 * i : 192 * i + 128]
            lat = jnp.dot(plain, w_key_up[h], preferred_element_type=F32)
            rot = queries[:, 192 * i + 128 : 192 * i + 192].astype(F32)
            tokens = slice(256 * i, 256 * i + 256)
            to = out_next if part else out
            to[tokens, :512] = lat.astype(BF)
            to[tokens, 512:] = turned(rot, cosine, sine)


def keys_kernel(start, own, near, far, swapped, cache, cosines, sines, keys, hidden, raw, sem):
    c = lax.axis_index("c")
    slab = 8 * lax.axis_index("yh") + lax.axis_index("z")

    def at(column, columns):
        return raw.at[:, pl.ds(pl.multiple_of(column, 128), columns)]

    copies = [
        pltpu.make_async_copy(own, at(512, 256), sem.at[0]),
        pltpu.make_async_copy(near, at(256 + 128 * c, 128), sem.at[1]),
        pltpu.make_async_copy(swapped.at[:, pl.ds(0, 128)], at(384 - 128 * c, 128), sem.at[2]),
        pltpu.make_async_copy(far, at(128 * c, 128), sem.at[3]),
        pltpu.make_async_copy(swapped.at[:, pl.ds(128, 128)], at(128 - 128 * c, 128), sem.at[4]),
    ]
    for copy in copies:
        copy.start()
    row = lax.broadcasted_iota(jnp.int32, (256, 768), 0)
    col = lax.broadcasted_iota(jnp.int32, (256, 768), 1)
    relative = col - 512 - row
    visible = (relative <= 0) & (relative > -512) & (slab * 256 + col - 512 >= -start[0])
    hidden[...] = jnp.where(visible, 0.0, -1e30)
    for copy in copies:
        copy.wait()
    low, high = raw[512:544, :].astype(F32), raw[544:, :].astype(F32)
    cosine, sine = cosines[...], sines[...]
    keys[:512, :] = raw[:512, :]
    keys[512:544, :] = (low * cosine - high * sine).astype(BF)
    keys[544:576, :] = (low * sine + high * cosine).astype(BF)
    keys[576:, :] = jnp.zeros((64, 768), BF)

    @pl.when(slab < 2)
    def _():
        copy = pltpu.make_async_copy(cache, at(0, 512), sem.at[0])
        copy.start()
        copy.wait()

    @pl.when(slab == 0)
    def _():
        keys[:576, :512] = raw[:, :512]

    @pl.when(slab == 1)
    def _():
        keys[:576, :256] = raw[:, 256:512]


def attend_kernel(group, queries, keys, hidden, w_value_up, reorder, out):
    scale = 192.0**-0.5 * 1.4426950408889634
    heads = []
    for pair in range(2):
        scores = jnp.dot(
            queries[512 * pair : 512 * pair + 512, :], keys[...], preferred_element_type=F32
        )
        for i in range(2):
            part = scores[256 * i : 256 * i + 256] * scale + hidden[...]
            top = jnp.max(part, axis=1, keepdims=True)
            powers = jnp.exp2(part - top)
            share = 1.0 / jnp.sum(powers, axis=1, keepdims=True)
            mixed = lax.dot_general(
                powers.astype(BF),
                keys[:512, :],
                (((1,), (1,)), ((), ())),
                preferred_element_type=F32,
            )
            attention = jnp.dot(
                (mixed * share).astype(BF),
                w_value_up[4 * group + 2 * pair + i],
                preferred_element_type=F32,
            )
            heads.append(attention.astype(BF))
    rows = jnp.concatenate(heads, 1)
    out[...] = jnp.dot(rows, reorder[...], preferred_element_type=F32).astype(BF)


def turns(first):
    inverse = jnp.power(jnp.float32(10000.0), -jnp.arange(32, dtype=F32) * (2.0 / 64))
    row = lax.broadcasted_iota(jnp.int32, (64, 128), 0)
    lane = lax.broadcasted_iota(jnp.int32, (64, 128), 1)
    own = (first + (lane // 32) * 64 + row).astype(F32) * jnp.tile(inverse, 4)[None, :]
    place = first - 512 + lax.broadcasted_iota(jnp.int32, (32, 768), 1)
    every = place.astype(F32) * inverse[:, None]
    return jnp.cos(own), jnp.sin(own), jnp.cos(every), jnp.sin(every)


def quarter_kernel(rows, own, other):
    x = lax.axis_index("x")
    for out, flip in ((own, 0), (other, 1)):
        odd = lax.axis_index("yl") ^ flip
        base = 896 * (lax.axis_index("yh") ^ flip) + 384 * odd
        pieces = []
        for d in range(4):
            start = pl.multiple_of(1792 * ((x + d) % 4) + base, 128)
            wide = rows[:, pl.ds(start, 512)]
            pieces.append(jnp.where(odd == 1, wide[:, 64:], wide[:, :448]))
        out[...] = jnp.concatenate(pieces, 1)


def project_kernel(theirs, *refs):
    groups, held, outs, (rows, total) = refs[:8], refs[8:21], refs[21:-2], refs[-2:]
    own, d1, d2, d3, u4, u3, u2, u1, other, e1, e3, e4, v1 = held
    blocks = [own, d1, d2, d3.at[:64], u4.at[:64], u3.at[:64], u2, u1]
    blocks += [other, e1, d3.at[64:], e3, e4, u4.at[64:], u3.at[64:], v1]
    first = 2 * (lax.axis_index("c") ^ theirs)
    yh = lax.axis_index("yh")
    for pick in (0, 2):

        @pl.when(first == pick)
        def _():
            for g in range(2):
                for j in range(2):
                    for p in range(2):
                        half = pl.ds(pl.multiple_of(256 * (yh ^ p), 256), 256)
                        rows[256 * j : 256 * j + 256, 512 * g + 256 * p : 512 * g + 256 * p + 256] = (
                            groups[2 * (pick + j) + g][:, half]
                        )

    for n in range(7):
        columns = slice(256 * n, 256 * n + 256)
        weights = jnp.concatenate(
            [
                block[32 * g : 32 * g + 32, columns]
                for g in range(2)
                for block in blocks
            ],
            0,
        )
        total[:, columns] = jnp.dot(rows[...], weights, preferred_element_type=F32)
    for out, d in zip((outs[0], *(outs[1].at[i] for i in range(3))), (2, 0, 1, 3)):
        span = slice(448 * d, 448 * d + 448)
        for j in range(2):
            top = total[256 * j : 256 * j + 128, span]
            low = total[256 * j + 128 : 256 * j + 256, span]
            out[128 * j : 128 * j + 128, :] = jnp.concatenate([top, low], 1).astype(out.dtype)


def whole(n):
    return [pl.BlockSpec(memory_space=VMEM)] * n


def placed(n):
    return [pl.BlockSpec(memory_space=pl.ANY)] * n


def kept(n=1):
    return [pl.BlockSpec(memory_space=pltpu.MemorySpace.HBM)] * n


def scalars(n=1):
    return [pl.BlockSpec(memory_space=pltpu.MemorySpace.SMEM)] * n


def quarters(rows):
    return pl.pallas_call(
        quarter_kernel,
        out_shape=[jax.ShapeDtypeStruct((64, 1792), BF)] * 2,
        in_specs=whole(1),
        out_specs=whole(2),
        name="quarters",
        cost_estimate=pl.CostEstimate(flops=0, bytes_accessed=2 << 20, transcendentals=0),
    )(rows)


def call(kernel, shapes, specs, args, name, flops, moved_bytes, room, scratch=()):
    many = isinstance(shapes, list)
    return pl.pallas_call(
        kernel,
        out_shape=shapes,
        in_specs=specs,
        out_specs=whole(len(shapes)) if many else whole(1)[0],
        scratch_shapes=list(scratch),
        compiler_params=pltpu.CompilerParams(vmem_limit_bytes=room << 20),
        name=name,
        cost_estimate=pl.CostEstimate(
            flops=flops, bytes_accessed=moved_bytes, transcendentals=0
        ),
    )(*args)


def array(shape, kind=BF):
    return jax.ShapeDtypeStruct(shape, kind)


def after(value, *others):
    return lax.optimization_barrier((value, *others))[0]


def project(theirs, groups, blocks, kind):
    return call(
        functools.partial(project_kernel, theirs),
        [array((256, 896), kind), array((3, 256, 896), kind)],
        whole(21),
        (*groups, *blocks),
        "project",
        2 * 512 * 1024 * 1792,
        8 << 20,
        12,
        [pltpu.VMEM((512, 1024), BF), pltpu.VMEM((512, 1792), F32)],
    )


def local(query_latent, key_rows, key_cache, prompt_start, w_query, w_key_up, w_value_up, w_output):
    yh, z, x, c, yl = (lax.axis_index(a) for a in AXES)
    slab = 8 * yh + z
    own, given = quarters(w_output.reshape(64, 7168))
    other = xor_y(given, 3)
    u1, d1 = up_z(own), down_z(own)

    own_keys = key_rows.T
    half = lax.dynamic_slice_in_dim(own_keys, 128 * c, 128, 1)
    near, far = (
        lax.ppermute(half, CTX, [(i, i + by) for i in range(16 - by)]) for by in (1, 2)
    )
    cosines, sines, all_cosines, all_sines = turns(slab * 256)
    queries = call(
        queries_kernel,
        [array((1024, 640))] * 2,
        kept(2) + whole(3),
        (query_latent, w_query, w_key_up, cosines, sines),
        "queries",
        2 * 256 * 1536 * 1536 + 2 * 2048 * 128 * 512,
        8 << 20,
        60,
        [
            pltpu.VMEM((2, 1536, 768), BF),
            pltpu.VMEM((256, 1536), BF),
            pltpu.SemaphoreType.DMA((3,)),
        ],
    )
    swapped = other_core(jnp.concatenate([near, far], 1))
    u2, d2 = up_z(after(u1, queries[0])), down_z(after(d1, queries[0]))
    v1, e1 = up_z(other), down_z(other)

    keys, hidden = call(
        keys_kernel,
        [array((640, 768)), array((256, 768), F32)],
        scalars() + kept() + placed(3) + kept() + whole(2),
        (prompt_start, own_keys, near, far, swapped, key_cache.T, all_cosines, all_sines),
        "keys",
        768 * 640 * 8,
        4 << 20,
        8,
        [pltpu.VMEM((576, 768), BF), pltpu.SemaphoreType.DMA((5,))],
    )
    column = jnp.arange(512, dtype=jnp.int32)
    source = (
        (column // 8 % 4) * 128 + (column // 256) * 64 + ((z + column // 32) % 8) * 8 + column % 8
    )
    reorder = (column[:, None] == source[None, :]).astype(BF)
    rows = [
        call(
            functools.partial(attend_kernel, g),
            array((256, 512)),
            whole(5),
            (queries[g], keys, hidden, w_value_up, reorder),
            "attend",
            2 * 1024 * 768 * 1152 + 2 * 1024 * 512 * 128,
            5 << 20,
            14,
        )
        for g in range(2)
    ]
    one = [xor_y(part, 1) for part in rows]
    three = [xor_y(part, 3) for part in rows]
    two = [xor_y(one[0], 3), xor_y(three[1], 1)]
    groups = [*rows, *one, *two, *three]
    u3 = up_z(after(jnp.concatenate([u2, v1], 0), rows[0]))
    d3 = down_z(after(jnp.concatenate([d2, e1], 0), rows[0]))
    u4 = up_z(u3)
    e3 = down_z(d3[64:])
    e4 = down_z(e3)
    blocks = [own, d1, d2, d3, u4, u3, u2, u1, other, e1, e3, e4, v1]

    first, rest = project(1, groups, blocks, BF)
    first, rest = other_core(first), other_core(rest)
    mine, mine_rest = project(0, groups, blocks, F32)
    far_sum = (mine + first.astype(F32)).astype(BF)
    passing_up = along_x(far_sum[:128], 1)
    passing_down = along_x(far_sum[128:], 3)
    sums = [mine_rest[i] + rest[i].astype(F32) for i in range(3)]
    early_up, early_down = lax.optimization_barrier(
        (sums[1][128:].astype(BF), sums[2][:128].astype(BF))
    )
    early_up, early_down = along_x(early_up, 1), along_x(early_down, 3)
    late_up = along_x((sums[1][:128] + passing_up.astype(F32)).astype(BF), 1)
    late_down = along_x((sums[2][128:] + passing_down.astype(F32)).astype(BF), 3)
    pieces = [
        home((sums[0][:128] + late_up.astype(F32) + early_down.astype(F32)).astype(BF), 0),
        home((sums[0][128:] + early_up.astype(F32) + late_down.astype(F32)).astype(BF), 1),
    ]
    even = yl == 0
    pair = jnp.where(even, pieces[0], pieces[1]), jnp.where(even, pieces[1], pieces[0])
    return jnp.concatenate(
        [jnp.concatenate([p[:, 448 * i : 448 * i + 448] for p in pair], 1) for i in range(2)], 0
    )


def solution(mesh):
    cut = Mesh(mesh.devices.reshape(SIZES), AXES) if hasattr(mesh, "devices") else mesh
    tokens = ("yl", "yh", "z")
    return jax.shard_map(
        local,
        mesh=cut,
        in_specs=(
            P(tokens, None),
            P(tokens, None),
            P("yl", None),
            P("yl"),
            P(None, HEAD),
            P(HEAD, None, None),
            P(HEAD, None, None),
            P(HEAD, CTX, None),
        ),
        out_specs=P(tokens, HEAD),
        check_vma=False,
    )
```

```python
import functools

import jax
import jax.numpy as jnp
from jax import lax
from jax.experimental import pallas as pl
from jax.experimental.pallas import tpu as pltpu
from jax.sharding import Mesh
from jax.sharding import PartitionSpec as P

AXES = ("yh", "z", "x", "c", "yl")
SIZES = (2, 8, 4, 2, 2)
CTX = ("yh", "z")
HEAD = ("x", "c")
BF = jnp.bfloat16
F32 = jnp.float32
VMEM = pltpu.MemorySpace.VMEM


def number_of(yh, z, x, c, yl):
    return (((yh * 8 + z) * 4 + x) * 2 + c) * 2 + yl


def moved(a, target):
    pairs = []
    for yh in range(2):
        for z in range(8):
            for x in range(4):
                for c in range(2):
                    for yl in range(2):
                        t = target(yh, z, x, c, yl)
                        pairs.append((number_of(yh, z, x, c, yl), number_of(*t)))
    return lax.ppermute(a, AXES, pairs)


def up_z(a):
    return moved(a, lambda yh, z, x, c, yl: (yh, (z + 1) % 8, x, c, yl))


def down_z(a):
    return moved(a, lambda yh, z, x, c, yl: (yh, (z - 1) % 8, x, c, yl))


def xor_y(a, q):
    return moved(a, lambda yh, z, x, c, yl: (yh ^ (q >> 1), z, x, c, yl ^ (q & 1)))


def other_core(a):
    return moved(a, lambda yh, z, x, c, yl: (yh, z, x, 1 - c, yl))


def along_x(a, d):
    return moved(a, lambda yh, z, x, c, yl: (yh, z, (x + d) % 4, c, yl))


def home(a, r):
    return moved(a, lambda yh, z, x, c, yl: (yh ^ c, z, x, yh, yl ^ r))


def turn_of(table):
    return jnp.concatenate([table[:, 32 * i : 32 * i + 32] for i in range(4)], 0)


def turned(rot, cosine, sine):
    other = jnp.concatenate([rot[:, 32:], rot[:, :32]], 1)
    cosine = jnp.concatenate([cosine, cosine], 1)
    sine = jnp.concatenate([-sine, sine], 1)
    rot = rot * cosine + other * sine
    return jnp.concatenate([rot, jnp.zeros_like(rot)], 1).astype(BF)


def queries_kernel(
    rows, w_query, w_key_up, cosines, sines, out, out_next, w_held, rows_held, up_held, total, sem
):
    copies = [
        pltpu.make_async_copy(
            w_query.at[pl.ds(384 * part, 384)], w_held.at[pl.ds(384 * part, 384)], sem.at[part]
        )
        for part in range(4)
    ]
    copies.append(pltpu.make_async_copy(rows, rows_held, sem.at[4]))
    copies.append(pltpu.make_async_copy(w_key_up, up_held, sem.at[5]))
    for i in (4, 0, 1, 2, 3, 5):
        copies[i].start()
    cosine, sine = turn_of(cosines), turn_of(sines)
    copies[4].wait()
    for part in range(4):
        copies[part].wait()
        span = slice(384 * part, 384 * part + 384)
        sums = jnp.dot(rows_held[:, span], w_held[span, :], preferred_element_type=F32)
        total[...] = total[...] + sums if part else sums
    copies[5].wait()
    for h in range(8):
        queries = total[:, 192 * h : 192 * h + 192]
        lat = jnp.dot(queries[:, :128].astype(BF), up_held[h], preferred_element_type=F32)
        rot = queries[:, 128:].astype(BF).astype(F32)
        i = h % 4
        tokens = slice(256 * i, 256 * i + 256)
        to = out_next if h >= 4 else out
        to[tokens, :512] = lat.astype(BF)
        to[tokens, 512:] = turned(rot, cosine, sine)


def keys_kernel(start, own, near, far, swapped, cache, cosines, sines, keys, hidden, raw, sem):
    c = lax.axis_index("c")
    slab = 8 * lax.axis_index("yh") + lax.axis_index("z")

    def at(column, columns):
        return raw.at[:, pl.ds(pl.multiple_of(column, 128), columns)]

    copies = [
        pltpu.make_async_copy(own, at(512, 256), sem.at[0]),
        pltpu.make_async_copy(near, at(256 + 128 * c, 128), sem.at[1]),
        pltpu.make_async_copy(swapped.at[:, pl.ds(0, 128)], at(384 - 128 * c, 128), sem.at[2]),
        pltpu.make_async_copy(far, at(128 * c, 128), sem.at[3]),
        pltpu.make_async_copy(swapped.at[:, pl.ds(128, 128)], at(128 - 128 * c, 128), sem.at[4]),
    ]
    for copy in copies:
        copy.start()
    row = lax.broadcasted_iota(jnp.int32, (256, 768), 0)
    col = lax.broadcasted_iota(jnp.int32, (256, 768), 1)
    relative = col - 512 - row
    visible = (relative <= 0) & (relative > -512) & (slab * 256 + col - 512 >= -start[0])
    hidden[...] = jnp.where(visible, 0.0, -1e30)
    for copy in copies:
        copy.wait()
    low, high = raw[512:544, :].astype(F32), raw[544:, :].astype(F32)
    cosine, sine = cosines[...], sines[...]
    keys[:512, :] = raw[:512, :]
    keys[512:544, :] = (low * cosine - high * sine).astype(BF)
    keys[544:576, :] = (low * sine + high * cosine).astype(BF)
    keys[576:, :] = jnp.zeros((64, 768), BF)

    @pl.when(slab < 2)
    def _():
        copy = pltpu.make_async_copy(cache, at(0, 512), sem.at[0])
        copy.start()
        copy.wait()

    @pl.when(slab == 0)
    def _():
        keys[:576, :512] = raw[:, :512]

    @pl.when(slab == 1)
    def _():
        keys[:576, :256] = raw[:, 256:512]


def attend_kernel(group, queries, keys, hidden, w_value_up, reorder, out):
    scale = 192.0**-0.5 * 1.4426950408889634
    heads = []
    for pair in range(2):
        scores = jnp.dot(
            queries[512 * pair : 512 * pair + 512, :], keys[...], preferred_element_type=F32
        )
        for i in range(2):
            part = scores[256 * i : 256 * i + 256] * scale + hidden[...]
            top = jnp.max(part, axis=1, keepdims=True)
            powers = jnp.exp2(part - top)
            share = 1.0 / jnp.sum(powers, axis=1, keepdims=True)
            mixed = lax.dot_general(
                powers.astype(BF),
                keys[:512, :],
                (((1,), (1,)), ((), ())),
                preferred_element_type=F32,
            )
            attention = jnp.dot(
                (mixed * share).astype(BF),
                w_value_up[4 * group + 2 * pair + i],
                preferred_element_type=F32,
            )
            heads.append(attention.astype(BF))
    rows = jnp.concatenate(heads, 1)
    out[...] = jnp.dot(rows, reorder[...], preferred_element_type=F32).astype(BF)


def turns(first):
    inverse = jnp.power(jnp.float32(10000.0), -jnp.arange(32, dtype=F32) * (2.0 / 64))
    row = lax.broadcasted_iota(jnp.int32, (64, 128), 0)
    lane = lax.broadcasted_iota(jnp.int32, (64, 128), 1)
    own = (first + (lane // 32) * 64 + row).astype(F32) * jnp.tile(inverse, 4)[None, :]
    place = first - 512 + lax.broadcasted_iota(jnp.int32, (32, 768), 1)
    every = place.astype(F32) * inverse[:, None]
    return jnp.cos(own), jnp.sin(own), jnp.cos(every), jnp.sin(every)


def quarter_kernel(flip, rows, out, wide, sem):
    x = lax.axis_index("x")
    odd = lax.axis_index("yl") ^ flip
    base = 896 * (lax.axis_index("yh") ^ flip) + 384 * odd
    copies = [
        pltpu.make_async_copy(
            rows.at[:, pl.ds(pl.multiple_of(1792 * ((x + d) % 4) + base, 128), 512)],
            wide.at[d],
            sem.at[d],
        )
        for d in range(4)
    ]
    for copy in copies:
        copy.start()
    for copy in copies:
        copy.wait()
    pieces = [jnp.where(odd == 1, wide[d, :, 64:], wide[d, :, :448]) for d in range(4)]
    out[...] = jnp.concatenate(pieces, 1)


def project_kernel(theirs, *refs):
    groups, held, outs, (rows, total) = refs[:8], refs[8:19], refs[19:-2], refs[-2:]
    own, d1, d2, d3, u4, u3, u2, u1, other, e3, e4 = held
    blocks = [own, d1, *(both.at[:64] for both in (d2, d3, u4, u3, u2)), u1]
    blocks += [other, d2.at[64:], d3.at[64:], e3, e4, *(both.at[64:] for both in (u4, u3, u2))]
    first = 2 * (lax.axis_index("c") ^ theirs)
    yh = lax.axis_index("yh")
    for pick in (0, 2):

        @pl.when(first == pick)
        def _():
            for g in range(2):
                for j in range(2):
                    for p in range(2):
                        half = pl.ds(pl.multiple_of(256 * (yh ^ p), 256), 256)
                        rows[256 * j : 256 * j + 256, 512 * g + 256 * p : 512 * g + 256 * p + 256] = (
                            groups[2 * (pick + j) + g][:, half]
                        )

    for n in range(7):
        columns = slice(256 * n, 256 * n + 256)
        weights = jnp.concatenate(
            [
                block[32 * g : 32 * g + 32, columns]
                for g in range(2)
                for block in blocks
            ],
            0,
        )
        total[:, columns] = jnp.dot(rows[...], weights, preferred_element_type=F32)
    for out, d in zip((outs[0], *(outs[1].at[i] for i in range(3))), (2, 0, 1, 3)):
        span = slice(448 * d, 448 * d + 448)
        for j in range(2):
            top = total[256 * j : 256 * j + 128, span]
            low = total[256 * j + 128 : 256 * j + 256, span]
            out[128 * j : 128 * j + 128, :] = jnp.concatenate([top, low], 1).astype(out.dtype)


def whole(n):
    return [pl.BlockSpec(memory_space=VMEM)] * n


def placed(n):
    return [pl.BlockSpec(memory_space=pl.ANY)] * n


def kept(n=1):
    return [pl.BlockSpec(memory_space=pltpu.MemorySpace.HBM)] * n


def scalars(n=1):
    return [pl.BlockSpec(memory_space=pltpu.MemorySpace.SMEM)] * n


def call(kernel, shapes, specs, args, name, flops, moved_bytes, room, scratch=()):
    many = isinstance(shapes, list)
    return pl.pallas_call(
        kernel,
        out_shape=shapes,
        in_specs=specs,
        out_specs=whole(len(shapes)) if many else whole(1)[0],
        scratch_shapes=list(scratch),
        compiler_params=pltpu.CompilerParams(vmem_limit_bytes=room << 20),
        name=name,
        cost_estimate=pl.CostEstimate(
            flops=flops, bytes_accessed=moved_bytes, transcendentals=0
        ),
    )(*args)


def array(shape, kind=BF):
    return jax.ShapeDtypeStruct(shape, kind)


def quarter(flip, rows):
    return call(
        functools.partial(quarter_kernel, flip),
        array((64, 1792)),
        kept(),
        (rows,),
        "quarter",
        0,
        1 << 19,
        62,
        [pltpu.VMEM((4, 64, 512), BF), pltpu.SemaphoreType.DMA((4,))],
    )


def after(value, *others):
    return lax.optimization_barrier((value, *others))[0]


def project(theirs, groups, blocks, kind):
    return call(
        functools.partial(project_kernel, theirs),
        [array((256, 896), kind), array((3, 256, 896), kind)],
        whole(19),
        (*groups, *blocks),
        "project",
        2 * 512 * 1024 * 1792,
        8 << 20,
        12,
        [pltpu.VMEM((512, 1024), BF), pltpu.VMEM((512, 1792), F32)],
    )


def local(query_latent, key_rows, key_cache, prompt_start, w_query, w_key_up, w_value_up, w_output):
    yh, z, x, c, yl = (lax.axis_index(a) for a in AXES)
    slab = 8 * yh + z
    weight_rows = w_output.reshape(64, 7168)
    given = quarter(1, weight_rows)
    other = xor_y(given, 3)
    own_keys = key_rows.T
    half = lax.dynamic_slice_in_dim(after(own_keys, given), 128 * c, 128, 1)
    own = quarter(0, after(weight_rows, half))
    u1, d1 = up_z(own), down_z(own)
    near, far = (
        lax.ppermute(half, CTX, [(i, i + by) for i in range(16 - by)]) for by in (1, 2)
    )
    cosines, sines, all_cosines, all_sines = turns(slab * 256)
    queries = call(
        queries_kernel,
        [array((1024, 640))] * 2,
        kept(3) + whole(2),
        (query_latent, w_query, w_key_up, cosines, sines),
        "queries",
        2 * 256 * 1536 * 1536 + 2 * 2048 * 128 * 512,
        8 << 20,
        60,
        [
            pltpu.VMEM((1536, 1536), BF),
            pltpu.VMEM((256, 1536), BF),
            pltpu.VMEM((8, 128, 512), BF),
            pltpu.VMEM((256, 1536), F32),
            pltpu.SemaphoreType.DMA((6,)),
        ],
    )
    swapped = other_core(jnp.concatenate([near, far], 1))
    u2 = up_z(jnp.concatenate([u1, other], 0))
    d2 = down_z(jnp.concatenate([d1, other], 0))

    keys, hidden = call(
        keys_kernel,
        [array((640, 768)), array((256, 768), F32)],
        scalars() + kept() + placed(3) + kept() + whole(2),
        (prompt_start, own_keys, near, far, swapped, key_cache.T, all_cosines, all_sines),
        "keys",
        768 * 640 * 8,
        4 << 20,
        8,
        [pltpu.VMEM((576, 768), BF), pltpu.SemaphoreType.DMA((5,))],
    )
    column = jnp.arange(512, dtype=jnp.int32)
    source = (
        (column // 8 % 4) * 128 + (column // 256) * 64 + ((z + column // 32) % 8) * 8 + column % 8
    )
    reorder = (column[:, None] == source[None, :]).astype(BF)
    rows = [
        call(
            functools.partial(attend_kernel, g),
            array((256, 512)),
            whole(5),
            (queries[g], keys, hidden, w_value_up, reorder),
            "attend",
            2 * 1024 * 768 * 1152 + 2 * 1024 * 512 * 128,
            5 << 20,
            14,
        )
        for g in range(2)
    ]
    one = [xor_y(part, 1) for part in rows]
    three = [xor_y(part, 3) for part in rows]
    two = [xor_y(one[0], 3), xor_y(three[1], 1)]
    groups = [*rows, *one, *two, *three]
    u3, d3 = up_z(after(u2, rows[0])), down_z(after(d2, rows[0]))
    u4 = up_z(u3)
    e3 = down_z(d3[64:])
    e4 = down_z(e3)
    blocks = [own, d1, d2, d3, u4, u3, u2, u1, other, e3, e4]

    first, rest = project(1, groups, blocks, BF)
    first, rest = other_core(first), other_core(rest)
    mine, mine_rest = project(0, groups, blocks, F32)
    far_sum = (mine + first.astype(F32)).astype(BF)
    passing_up = along_x(far_sum[:128], 1)
    passing_down = along_x(far_sum[128:], 3)
    sums = [mine_rest[i] + rest[i].astype(F32) for i in range(3)]
    early_up, early_down = lax.optimization_barrier(
        (sums[1][128:].astype(BF), sums[2][:128].astype(BF))
    )
    early_up, early_down = along_x(early_up, 1), along_x(early_down, 3)
    late_up = along_x((sums[1][:128] + passing_up.astype(F32)).astype(BF), 1)
    late_down = along_x((sums[2][128:] + passing_down.astype(F32)).astype(BF), 3)
    pieces = [
        home((sums[0][:128] + late_up.astype(F32) + early_down.astype(F32)).astype(BF), 0),
        home((sums[0][128:] + early_up.astype(F32) + late_down.astype(F32)).astype(BF), 1),
    ]
    even = yl == 0
    pair = jnp.where(even, pieces[0], pieces[1]), jnp.where(even, pieces[1], pieces[0])
    return jnp.concatenate(
        [jnp.concatenate([p[:, 448 * i : 448 * i + 448] for p in pair], 1) for i in range(2)], 0
    )


def solution(mesh):
    cut = Mesh(mesh.devices.reshape(SIZES), AXES) if hasattr(mesh, "devices") else mesh
    tokens = ("yl", "yh", "z")
    return jax.shard_map(
        local,
        mesh=cut,
        in_specs=(
            P(tokens, None),
            P(tokens, None),
            P("yl", None),
            P("yl"),
            P(None, HEAD),
            P(HEAD, None, None),
            P(HEAD, None, None),
            P(HEAD, CTX, None),
        ),
        out_specs=P(tokens, HEAD),
        check_vma=False,
    )
```

```python
import functools

import jax
import jax.numpy as jnp
from jax import lax
from jax.experimental import pallas as pl
from jax.experimental.pallas import tpu as pltpu
from jax.sharding import Mesh
from jax.sharding import PartitionSpec as P

AXES = ("yh", "z", "x", "c", "yl")
SIZES = (2, 8, 4, 2, 2)
CTX = ("yh", "z")
HEAD = ("x", "c")
BF = jnp.bfloat16
F32 = jnp.float32
VMEM = pltpu.MemorySpace.VMEM


def number_of(yh, z, x, c, yl):
    return (((yh * 8 + z) * 4 + x) * 2 + c) * 2 + yl


def moved(a, target):
    pairs = []
    for yh in range(2):
        for z in range(8):
            for x in range(4):
                for c in range(2):
                    for yl in range(2):
                        t = target(yh, z, x, c, yl)
                        pairs.append((number_of(yh, z, x, c, yl), number_of(*t)))
    return lax.ppermute(a, AXES, pairs)


def up_z(a):
    return moved(a, lambda yh, z, x, c, yl: (yh, (z + 1) % 8, x, c, yl))


def down_z(a):
    return moved(a, lambda yh, z, x, c, yl: (yh, (z - 1) % 8, x, c, yl))


def xor_y(a, q):
    return moved(a, lambda yh, z, x, c, yl: (yh ^ (q >> 1), z, x, c, yl ^ (q & 1)))


def other_core(a):
    return moved(a, lambda yh, z, x, c, yl: (yh, z, x, 1 - c, yl))


def along_x(a, d):
    return moved(a, lambda yh, z, x, c, yl: (yh, z, (x + d) % 4, c, yl))


def home(a, r):
    return moved(a, lambda yh, z, x, c, yl: (yh ^ c, z, x, yh, yl ^ r))


def turn_of(table):
    return jnp.concatenate([table[:, 32 * i : 32 * i + 32] for i in range(4)], 0)


def turned(rot, cosine, sine):
    other = jnp.concatenate([rot[:, 32:], rot[:, :32]], 1)
    cosine = jnp.concatenate([cosine, cosine], 1)
    sine = jnp.concatenate([-sine, sine], 1)
    rot = rot * cosine + other * sine
    return jnp.concatenate([rot, jnp.zeros_like(rot)], 1).astype(BF)


def queries_kernel(rows, w_query, w_key_up, cosines, sines, out, out_next):
    cosine, sine = turn_of(cosines), turn_of(sines)
    for part in range(2):
        span = slice(768 * part, 768 * part + 768)
        queries = jnp.dot(rows[...], w_query[:, span], preferred_element_type=F32).astype(BF)
        for i in range(4):
            plain = queries[:, 192 * i : 192 * i + 128]
            lat = jnp.dot(plain, w_key_up[4 * part + i], preferred_element_type=F32)
            rot = queries[:, 192 * i + 128 : 192 * i + 192].astype(F32)
            tokens = slice(256 * i, 256 * i + 256)
            to = out_next if part else out
            to[tokens, :512] = lat.astype(BF)
            to[tokens, 512:] = turned(rot, cosine, sine)


def keys_kernel(start, own, near, far, swapped, cache, cosines, sines, keys, hidden, raw, sem):
    c = lax.axis_index("c")
    slab = 8 * lax.axis_index("yh") + lax.axis_index("z")

    def at(column, columns):
        return raw.at[:, pl.ds(pl.multiple_of(column, 128), columns)]

    copies = [
        pltpu.make_async_copy(own, at(512, 256), sem.at[0]),
        pltpu.make_async_copy(near, at(256 + 128 * c, 128), sem.at[1]),
        pltpu.make_async_copy(swapped.at[:, pl.ds(0, 128)], at(384 - 128 * c, 128), sem.at[2]),
        pltpu.make_async_copy(far, at(128 * c, 128), sem.at[3]),
        pltpu.make_async_copy(swapped.at[:, pl.ds(128, 128)], at(128 - 128 * c, 128), sem.at[4]),
    ]
    for copy in copies:
        copy.start()
    row = lax.broadcasted_iota(jnp.int32, (256, 768), 0)
    col = lax.broadcasted_iota(jnp.int32, (256, 768), 1)
    relative = col - 512 - row
    visible = (relative <= 0) & (relative > -512) & (slab * 256 + col - 512 >= -start[0])
    hidden[...] = jnp.where(visible, 0.0, -1e30)
    for copy in copies:
        copy.wait()
    low, high = raw[512:544, :].astype(F32), raw[544:, :].astype(F32)
    cosine, sine = cosines[...], sines[...]
    keys[:512, :] = raw[:512, :]
    keys[512:544, :] = (low * cosine - high * sine).astype(BF)
    keys[544:576, :] = (low * sine + high * cosine).astype(BF)
    keys[576:, :] = jnp.zeros((64, 768), BF)

    @pl.when(slab < 2)
    def _():
        copy = pltpu.make_async_copy(cache, at(0, 512), sem.at[0])
        copy.start()
        copy.wait()

    @pl.when(slab == 0)
    def _():
        keys[:576, :512] = raw[:, :512]

    @pl.when(slab == 1)
    def _():
        keys[:576, :256] = raw[:, 256:512]


def attend_kernel(group, queries, keys, hidden, w_value_up, reorder, out):
    scale = 192.0**-0.5 * 1.4426950408889634
    heads = []
    for pair in range(2):
        scores = jnp.dot(
            queries[512 * pair : 512 * pair + 512, :], keys[...], preferred_element_type=F32
        )
        for i in range(2):
            part = scores[256 * i : 256 * i + 256] * scale + hidden[...]
            top = jnp.max(part, axis=1, keepdims=True)
            powers = jnp.exp2(part - top)
            share = 1.0 / jnp.sum(powers, axis=1, keepdims=True)
            mixed = lax.dot_general(
                powers.astype(BF),
                keys[:512, :],
                (((1,), (1,)), ((), ())),
                preferred_element_type=F32,
            )
            attention = jnp.dot(
                (mixed * share).astype(BF),
                w_value_up[4 * group + 2 * pair + i],
                preferred_element_type=F32,
            )
            heads.append(attention.astype(BF))
    rows = jnp.concatenate(heads, 1)
    out[...] = jnp.dot(rows, reorder[...], preferred_element_type=F32).astype(BF)


def turns(first):
    inverse = jnp.power(jnp.float32(10000.0), -jnp.arange(32, dtype=F32) * (2.0 / 64))
    row = lax.broadcasted_iota(jnp.int32, (64, 128), 0)
    lane = lax.broadcasted_iota(jnp.int32, (64, 128), 1)
    own = (first + (lane // 32) * 64 + row).astype(F32) * jnp.tile(inverse, 4)[None, :]
    place = first - 512 + lax.broadcasted_iota(jnp.int32, (32, 768), 1)
    every = place.astype(F32) * inverse[:, None]
    return jnp.cos(own), jnp.sin(own), jnp.cos(every), jnp.sin(every)


def quarter_kernel(rows, own, other):
    x = lax.axis_index("x")
    for out, flip in ((own, 0), (other, 1)):
        odd = lax.axis_index("yl") ^ flip
        base = 896 * (lax.axis_index("yh") ^ flip) + 384 * odd
        pieces = []
        for d in range(4):
            start = pl.multiple_of(1792 * ((x + d) % 4) + base, 128)
            wide = rows[:, pl.ds(start, 512)]
            pieces.append(jnp.where(odd == 1, wide[:, 64:], wide[:, :448]))
        out[...] = jnp.concatenate(pieces, 1)


def project_kernel(theirs, *refs):
    groups, held, outs, (rows, total) = refs[:8], refs[8:23], refs[23:-2], refs[-2:]
    both = held[4]
    blocks = [*held[:4], both.at[:64], *held[5:14], both.at[64:], held[14]]
    first = 2 * (lax.axis_index("c") ^ theirs)
    yh = lax.axis_index("yh")
    for pick in (0, 2):

        @pl.when(first == pick)
        def _():
            for g in range(2):
                for j in range(2):
                    for p in range(2):
                        half = pl.ds(pl.multiple_of(256 * (yh ^ p), 256), 256)
                        rows[256 * j : 256 * j + 256, 512 * g + 256 * p : 512 * g + 256 * p + 256] = (
                            groups[2 * (pick + j) + g][:, half]
                        )

    for n in range(7):
        columns = slice(256 * n, 256 * n + 256)
        weights = jnp.concatenate(
            [
                block[32 * g : 32 * g + 32, columns]
                for g in range(2)
                for block in blocks
            ],
            0,
        )
        total[:, columns] = jnp.dot(rows[...], weights, preferred_element_type=F32)
    for out, d in zip((outs[0], *(outs[1].at[i] for i in range(3))), (2, 0, 1, 3)):
        span = slice(448 * d, 448 * d + 448)
        for j in range(2):
            top = total[256 * j : 256 * j + 128, span]
            low = total[256 * j + 128 : 256 * j + 256, span]
            out[128 * j : 128 * j + 128, :] = jnp.concatenate([top, low], 1).astype(out.dtype)


def whole(n):
    return [pl.BlockSpec(memory_space=VMEM)] * n


def placed(n):
    return [pl.BlockSpec(memory_space=pl.ANY)] * n


def kept(n=1):
    return [pl.BlockSpec(memory_space=pltpu.MemorySpace.HBM)] * n


def scalars(n=1):
    return [pl.BlockSpec(memory_space=pltpu.MemorySpace.SMEM)] * n


def quarters(rows):
    return pl.pallas_call(
        quarter_kernel,
        out_shape=[jax.ShapeDtypeStruct((64, 1792), BF)] * 2,
        in_specs=whole(1),
        out_specs=whole(2),
        name="quarters",
        cost_estimate=pl.CostEstimate(flops=0, bytes_accessed=2 << 20, transcendentals=0),
    )(rows)


def call(kernel, shapes, specs, args, name, flops, moved_bytes, room, scratch=()):
    many = isinstance(shapes, list)
    return pl.pallas_call(
        kernel,
        out_shape=shapes,
        in_specs=specs,
        out_specs=whole(len(shapes)) if many else whole(1)[0],
        scratch_shapes=list(scratch),
        compiler_params=pltpu.CompilerParams(vmem_limit_bytes=room << 20),
        name=name,
        cost_estimate=pl.CostEstimate(
            flops=flops, bytes_accessed=moved_bytes, transcendentals=0
        ),
    )(*args)


def array(shape, kind=BF):
    return jax.ShapeDtypeStruct(shape, kind)


def after(value, *others):
    return lax.optimization_barrier((value, *others))[0]


def project(theirs, groups, blocks, kind):
    return call(
        functools.partial(project_kernel, theirs),
        [array((256, 896), kind), array((3, 256, 896), kind)],
        whole(23),
        (*groups, *blocks),
        "project",
        2 * 512 * 1024 * 1792,
        8 << 20,
        12,
        [pltpu.VMEM((512, 1024), BF), pltpu.VMEM((512, 1792), F32)],
    )


def local(query_latent, key_rows, key_cache, prompt_start, w_query, w_key_up, w_value_up, w_output):
    yh, z, x, c, yl = (lax.axis_index(a) for a in AXES)
    slab = 8 * yh + z
    own, given = quarters(w_output.reshape(64, 7168))
    other = xor_y(given, 3)
    u1, d1 = up_z(own), down_z(own)

    own_keys = key_rows.T
    half = lax.dynamic_slice_in_dim(own_keys, 128 * c, 128, 1)
    near, far = (
        lax.ppermute(half, CTX, [(i, i + by) for i in range(16 - by)]) for by in (1, 2)
    )
    cosines, sines, all_cosines, all_sines = turns(slab * 256)
    queries = call(
        queries_kernel,
        [array((1024, 640))] * 2,
        whole(5),
        (query_latent, w_query, w_key_up, cosines, sines),
        "queries",
        2 * 256 * 1536 * 1536 + 2 * 2048 * 128 * 512,
        8 << 20,
        10,
    )
    swapped = other_core(jnp.concatenate([near, far], 1))
    u2, d2 = up_z(after(u1, queries[0])), down_z(after(d1, queries[0]))
    v1, e1 = up_z(other), down_z(other)

    keys, hidden = call(
        keys_kernel,
        [array((640, 768)), array((256, 768), F32)],
        scalars() + kept() + placed(3) + kept() + whole(2),
        (prompt_start, own_keys, near, far, swapped, key_cache.T, all_cosines, all_sines),
        "keys",
        768 * 640 * 8,
        4 << 20,
        8,
        [pltpu.VMEM((576, 768), BF), pltpu.SemaphoreType.DMA((5,))],
    )
    column = jnp.arange(512, dtype=jnp.int32)
    source = (
        (column // 8 % 4) * 128 + (column // 256) * 64 + ((z + column // 32) % 8) * 8 + column % 8
    )
    reorder = (column[:, None] == source[None, :]).astype(BF)
    rows = [
        call(
            functools.partial(attend_kernel, g),
            array((256, 512)),
            whole(5),
            (queries[g], keys, hidden, w_value_up, reorder),
            "attend",
            2 * 1024 * 768 * 1152 + 2 * 1024 * 512 * 128,
            5 << 20,
            14,
        )
        for g in range(2)
    ]
    one = [xor_y(part, 1) for part in rows]
    three = [xor_y(part, 3) for part in rows]
    two = [xor_y(one[0], 3), xor_y(three[1], 1)]
    groups = [*rows, *one, *two, *three]
    u3, d3 = up_z(after(u2, rows[0])), down_z(after(d2, rows[0]))
    u4 = up_z(after(jnp.concatenate([u3, v1], 0), *rows))
    e2 = down_z(after(e1, *rows))
    v3 = up_z(u4[64:])
    e3 = down_z(e2)
    e4 = down_z(e3)
    blocks = [own, d1, d2, d3, u4, u3, u2, u1, other, e1, e2, e3, e4, v3, v1]

    first, rest = project(1, groups, blocks, BF)
    first, rest = other_core(first), other_core(rest)
    mine, mine_rest = project(0, groups, blocks, F32)
    far_sum = (mine + first.astype(F32)).astype(BF)
    passing_up = along_x(far_sum[:128], 1)
    passing_down = along_x(far_sum[128:], 3)
    sums = [mine_rest[i] + rest[i].astype(F32) for i in range(3)]
    early_up, early_down = lax.optimization_barrier(
        (sums[1][128:].astype(BF), sums[2][:128].astype(BF))
    )
    early_up, early_down = along_x(early_up, 1), along_x(early_down, 3)
    late_up = along_x((sums[1][:128] + passing_up.astype(F32)).astype(BF), 1)
    late_down = along_x((sums[2][128:] + passing_down.astype(F32)).astype(BF), 3)
    pieces = [
        home((sums[0][:128] + late_up.astype(F32) + early_down.astype(F32)).astype(BF), 0),
        home((sums[0][128:] + early_up.astype(F32) + late_down.astype(F32)).astype(BF), 1),
    ]
    even = yl == 0
    pair = jnp.where(even, pieces[0], pieces[1]), jnp.where(even, pieces[1], pieces[0])
    return jnp.concatenate(
        [jnp.concatenate([p[:, 448 * i : 448 * i + 448] for p in pair], 1) for i in range(2)], 0
    )


def solution(mesh):
    cut = Mesh(mesh.devices.reshape(SIZES), AXES) if hasattr(mesh, "devices") else mesh
    tokens = ("yl", "yh", "z")
    return jax.shard_map(
        local,
        mesh=cut,
        in_specs=(
            P(tokens, None),
            P(tokens, None),
            P("yl", None),
            P("yl"),
            P(None, HEAD),
            P(HEAD, None, None),
            P(HEAD, None, None),
            P(HEAD, CTX, None),
        ),
        out_specs=P(tokens, HEAD),
        check_vma=False,
    )
```

```python
import functools

import jax
import jax.numpy as jnp
from jax import lax
from jax.experimental import pallas as pl
from jax.experimental.pallas import tpu as pltpu
from jax.sharding import Mesh
from jax.sharding import PartitionSpec as P

AXES = ("yh", "z", "x", "c", "yl")
SIZES = (2, 8, 4, 2, 2)
CTX = ("yh", "z")
HEAD = ("x", "c")
BF = jnp.bfloat16
F32 = jnp.float32
VMEM = pltpu.MemorySpace.VMEM


def number_of(yh, z, x, c, yl):
    return (((yh * 8 + z) * 4 + x) * 2 + c) * 2 + yl


def moved(a, target):
    pairs = []
    for yh in range(2):
        for z in range(8):
            for x in range(4):
                for c in range(2):
                    for yl in range(2):
                        t = target(yh, z, x, c, yl)
                        pairs.append((number_of(yh, z, x, c, yl), number_of(*t)))
    return lax.ppermute(a, AXES, pairs)


def up_z(a):
    return moved(a, lambda yh, z, x, c, yl: (yh, (z + 1) % 8, x, c, yl))


def down_z(a):
    return moved(a, lambda yh, z, x, c, yl: (yh, (z - 1) % 8, x, c, yl))


def xor_y(a, q):
    return moved(a, lambda yh, z, x, c, yl: (yh ^ (q >> 1), z, x, c, yl ^ (q & 1)))


def other_core(a):
    return moved(a, lambda yh, z, x, c, yl: (yh, z, x, 1 - c, yl))


def along_x(a, d):
    return moved(a, lambda yh, z, x, c, yl: (yh, z, (x + d) % 4, c, yl))


def home(a, r, d=0):
    return moved(a, lambda yh, z, x, c, yl: (yh ^ c, z, (x + d) % 4, yh, yl ^ r))


def turn_of(table):
    return jnp.concatenate([table[:, 32 * i : 32 * i + 32] for i in range(4)], 0)


def turned(rot, cosine, sine):
    other = jnp.concatenate([rot[:, 32:], rot[:, :32]], 1)
    cosine = jnp.concatenate([cosine, cosine], 1)
    sine = jnp.concatenate([-sine, sine], 1)
    rot = rot * cosine + other * sine
    return jnp.concatenate([rot, jnp.zeros_like(rot)], 1).astype(BF)


def queries_kernel(rows, w_query, w_key_up, cosines, sines, out, out_next, held, rows_held, sem):
    copies = [
        pltpu.make_async_copy(w_query.at[:, pl.ds(768 * part, 768)], held.at[part], sem.at[part])
        for part in range(2)
    ]
    copies.append(pltpu.make_async_copy(rows, rows_held, sem.at[2]))
    for i in (2, 0, 1):
        copies[i].start()
    cosine, sine = turn_of(cosines), turn_of(sines)
    copies[2].wait()
    for part in range(2):
        copies[part].wait()
        queries = jnp.dot(rows_held[...], held[part], preferred_element_type=F32).astype(BF)
        for i in range(4):
            h = 4 * part + i
            plain = queries[:, 192 * i : 192 * i + 128]
            lat = jnp.dot(plain, w_key_up[h], preferred_element_type=F32)
            rot = queries[:, 192 * i + 128 : 192 * i + 192].astype(F32)
            tokens = slice(256 * i, 256 * i + 256)
            to = out_next if part else out
            to[tokens, :512] = lat.astype(BF)
            to[tokens, 512:] = turned(rot, cosine, sine)


def keys_kernel(start, own, near, far, swapped, cache, cosines, sines, keys, hidden, raw, sem):
    c = lax.axis_index("c")
    slab = 8 * lax.axis_index("yh") + lax.axis_index("z")

    def at(column, columns):
        return raw.at[:, pl.ds(pl.multiple_of(column, 128), columns)]

    copies = [
        pltpu.make_async_copy(own, at(512, 256), sem.at[0]),
        pltpu.make_async_copy(near, at(256 + 128 * c, 128), sem.at[1]),
        pltpu.make_async_copy(swapped.at[:, pl.ds(0, 128)], at(384 - 128 * c, 128), sem.at[2]),
        pltpu.make_async_copy(far, at(128 * c, 128), sem.at[3]),
        pltpu.make_async_copy(swapped.at[:, pl.ds(128, 128)], at(128 - 128 * c, 128), sem.at[4]),
    ]
    for copy in copies:
        copy.start()
    row = lax.broadcasted_iota(jnp.int32, (256, 768), 0)
    col = lax.broadcasted_iota(jnp.int32, (256, 768), 1)
    relative = col - 512 - row
    visible = (relative <= 0) & (relative > -512) & (slab * 256 + col - 512 >= -start[0])
    hidden[...] = jnp.where(visible, 0.0, -1e30)
    for copy in copies:
        copy.wait()
    low, high = raw[512:544, :].astype(F32), raw[544:, :].astype(F32)
    cosine, sine = cosines[...], sines[...]
    keys[:512, :] = raw[:512, :]
    keys[512:544, :] = (low * cosine - high * sine).astype(BF)
    keys[544:576, :] = (low * sine + high * cosine).astype(BF)
    keys[576:, :] = jnp.zeros((64, 768), BF)

    @pl.when(slab < 2)
    def _():
        copy = pltpu.make_async_copy(cache, at(0, 512), sem.at[0])
        copy.start()
        copy.wait()

    @pl.when(slab == 0)
    def _():
        keys[:576, :512] = raw[:, :512]

    @pl.when(slab == 1)
    def _():
        keys[:576, :256] = raw[:, 256:512]


def attend_kernel(group, queries, keys, hidden, w_value_up, reorder, out):
    scale = 192.0**-0.5 * 1.4426950408889634
    heads = []
    for pair in range(2):
        scores = jnp.dot(
            queries[512 * pair : 512 * pair + 512, :], keys[...], preferred_element_type=F32
        )
        for i in range(2):
            part = scores[256 * i : 256 * i + 256] * scale + hidden[...]
            top = jnp.max(part, axis=1, keepdims=True)
            powers = jnp.exp2(part - top)
            share = 1.0 / jnp.sum(powers, axis=1, keepdims=True)
            mixed = lax.dot_general(
                powers.astype(BF),
                keys[:512, :],
                (((1,), (1,)), ((), ())),
                preferred_element_type=F32,
            )
            attention = jnp.dot(
                (mixed * share).astype(BF),
                w_value_up[4 * group + 2 * pair + i],
                preferred_element_type=F32,
            )
            heads.append(attention.astype(BF))
    rows = jnp.concatenate(heads, 1)
    out[...] = jnp.dot(rows, reorder[...], preferred_element_type=F32).astype(BF)


def turns(first):
    inverse = jnp.power(jnp.float32(10000.0), -jnp.arange(32, dtype=F32) * (2.0 / 64))
    row = lax.broadcasted_iota(jnp.int32, (64, 128), 0)
    lane = lax.broadcasted_iota(jnp.int32, (64, 128), 1)
    own = (first + (lane // 32) * 64 + row).astype(F32) * jnp.tile(inverse, 4)[None, :]
    place = first - 512 + lax.broadcasted_iota(jnp.int32, (32, 768), 1)
    every = place.astype(F32) * inverse[:, None]
    return jnp.cos(own), jnp.sin(own), jnp.cos(every), jnp.sin(every)


def quarter_kernel(rows, own, other):
    x = lax.axis_index("x")
    for out, flip in ((own, 0), (other, 1)):
        odd = lax.axis_index("yl") ^ flip
        base = 896 * (lax.axis_index("yh") ^ flip) + 384 * odd
        pieces = []
        for d in range(4):
            start = pl.multiple_of(1792 * ((x + d) % 4) + base, 128)
            wide = rows[:, pl.ds(start, 512)]
            pieces.append(jnp.where(odd == 1, wide[:, 64:], wide[:, :448]))
        out[...] = jnp.concatenate(pieces, 1)


def project_kernel(theirs, *refs):
    groups, held, outs, (rows, total) = refs[:8], refs[8:21], refs[21:-2], refs[-2:]
    own, d1, d2, d3, u4, u3, u2, u1, other, e1, e3, e4, v1 = held
    blocks = [own, d1, d2, d3.at[:64], u4.at[:64], u3.at[:64], u2, u1]
    blocks += [other, e1, d3.at[64:], e3, e4, u4.at[64:], u3.at[64:], v1]
    first = 2 * (lax.axis_index("c") ^ theirs)
    yh = lax.axis_index("yh")
    for pick in (0, 2):

        @pl.when(first == pick)
        def _():
            for g in range(2):
                for j in range(2):
                    for p in range(2):
                        half = pl.ds(pl.multiple_of(256 * (yh ^ p), 256), 256)
                        rows[256 * j : 256 * j + 256, 512 * g + 256 * p : 512 * g + 256 * p + 256] = (
                            groups[2 * (pick + j) + g][:, half]
                        )

    for n in range(7):
        columns = slice(256 * n, 256 * n + 256)
        weights = jnp.concatenate(
            [
                block[32 * g : 32 * g + 32, columns]
                for g in range(2)
                for block in blocks
            ],
            0,
        )
        total[:, columns] = jnp.dot(rows[...], weights, preferred_element_type=F32)
    for out, d in zip((outs[0], *(outs[1].at[i] for i in range(3))), (2, 0, 1, 3)):
        span = slice(448 * d, 448 * d + 448)
        for j in range(2):
            top = total[256 * j : 256 * j + 128, span]
            low = total[256 * j + 128 : 256 * j + 256, span]
            out[128 * j : 128 * j + 128, :] = jnp.concatenate([top, low], 1).astype(out.dtype)


def whole(n):
    return [pl.BlockSpec(memory_space=VMEM)] * n


def placed(n):
    return [pl.BlockSpec(memory_space=pl.ANY)] * n


def kept(n=1):
    return [pl.BlockSpec(memory_space=pltpu.MemorySpace.HBM)] * n


def scalars(n=1):
    return [pl.BlockSpec(memory_space=pltpu.MemorySpace.SMEM)] * n


def quarters(rows):
    return pl.pallas_call(
        quarter_kernel,
        out_shape=[jax.ShapeDtypeStruct((64, 1792), BF)] * 2,
        in_specs=whole(1),
        out_specs=whole(2),
        name="quarters",
        cost_estimate=pl.CostEstimate(flops=0, bytes_accessed=2 << 20, transcendentals=0),
    )(rows)


def call(kernel, shapes, specs, args, name, flops, moved_bytes, room, scratch=()):
    many = isinstance(shapes, list)
    return pl.pallas_call(
        kernel,
        out_shape=shapes,
        in_specs=specs,
        out_specs=whole(len(shapes)) if many else whole(1)[0],
        scratch_shapes=list(scratch),
        compiler_params=pltpu.CompilerParams(vmem_limit_bytes=room << 20),
        name=name,
        cost_estimate=pl.CostEstimate(
            flops=flops, bytes_accessed=moved_bytes, transcendentals=0
        ),
    )(*args)


def array(shape, kind=BF):
    return jax.ShapeDtypeStruct(shape, kind)


def after(value, *others):
    return lax.optimization_barrier((value, *others))[0]


def project(theirs, groups, blocks, kind):
    return call(
        functools.partial(project_kernel, theirs),
        [array((256, 896), kind), array((3, 256, 896), kind)],
        whole(21),
        (*groups, *blocks),
        "project",
        2 * 512 * 1024 * 1792,
        8 << 20,
        12,
        [pltpu.VMEM((512, 1024), BF), pltpu.VMEM((512, 1792), F32)],
    )


def local(query_latent, key_rows, key_cache, prompt_start, w_query, w_key_up, w_value_up, w_output):
    yh, z, x, c, yl = (lax.axis_index(a) for a in AXES)
    slab = 8 * yh + z
    own, given = quarters(w_output.reshape(64, 7168))
    other = xor_y(given, 3)
    u1, d1 = up_z(own), down_z(own)

    own_keys = key_rows.T
    half = lax.dynamic_slice_in_dim(own_keys, 128 * c, 128, 1)
    near, far = (
        lax.ppermute(half, CTX, [(i, i + by) for i in range(16 - by)]) for by in (1, 2)
    )
    cosines, sines, all_cosines, all_sines = turns(slab * 256)
    queries = call(
        queries_kernel,
        [array((1024, 640))] * 2,
        kept(2) + whole(3),
        (query_latent, w_query, w_key_up, cosines, sines),
        "queries",
        2 * 256 * 1536 * 1536 + 2 * 2048 * 128 * 512,
        8 << 20,
        60,
        [
            pltpu.VMEM((2, 1536, 768), BF),
            pltpu.VMEM((256, 1536), BF),
            pltpu.SemaphoreType.DMA((3,)),
        ],
    )
    swapped = other_core(jnp.concatenate([near, far], 1))
    u2, d2 = up_z(after(u1, queries[0])), down_z(after(d1, queries[0]))
    v1, e1 = up_z(other), down_z(other)

    keys, hidden = call(
        keys_kernel,
        [array((640, 768)), array((256, 768), F32)],
        scalars() + kept() + placed(3) + kept() + whole(2),
        (prompt_start, own_keys, near, far, swapped, key_cache.T, all_cosines, all_sines),
        "keys",
        768 * 640 * 8,
        4 << 20,
        8,
        [pltpu.VMEM((576, 768), BF), pltpu.SemaphoreType.DMA((5,))],
    )
    column = jnp.arange(512, dtype=jnp.int32)
    source = (
        (column // 8 % 4) * 128 + (column // 256) * 64 + ((z + column // 32) % 8) * 8 + column % 8
    )
    reorder = (column[:, None] == source[None, :]).astype(BF)
    rows = [
        call(
            functools.partial(attend_kernel, g),
            array((256, 512)),
            whole(5),
            (queries[g], keys, hidden, w_value_up, reorder),
            "attend",
            2 * 1024 * 768 * 1152 + 2 * 1024 * 512 * 128,
            5 << 20,
            14,
        )
        for g in range(2)
    ]
    one = [xor_y(part, 1) for part in rows]
    three = [xor_y(part, 3) for part in rows]
    two = [xor_y(one[0], 3), xor_y(three[1], 1)]
    groups = [*rows, *one, *two, *three]
    u3 = up_z(after(jnp.concatenate([u2, v1], 0), rows[0]))
    d3 = down_z(after(jnp.concatenate([d2, e1], 0), rows[0]))
    u4 = up_z(u3)
    e3 = down_z(d3[64:])
    e4 = down_z(e3)
    blocks = [own, d1, d2, d3, u4, u3, u2, u1, other, e1, e3, e4, v1]

    first, rest = project(1, groups, blocks, BF)
    first, rest = other_core(first), other_core(rest)
    mine, mine_rest = project(0, groups, blocks, F32)
    far_sum = (mine + first.astype(F32)).astype(BF)
    passing_up = along_x(far_sum[:128], 1)
    passing_down = along_x(far_sum[128:], 3)
    sums = [mine_rest[i] + rest[i].astype(F32) for i in range(3)]
    early_up, early_down, *own_sum = lax.optimization_barrier(
        (
            sums[1][128:].astype(BF),
            sums[2][:128].astype(BF),
            sums[0][:128].astype(BF),
            sums[0][128:].astype(BF),
        )
    )
    parts = [
        [home(own_sum[0], 0), home(early_down, 0, 3)],
        [home(own_sum[1], 1), home(early_up, 1, 1)],
    ]
    parts[0].append(home((sums[1][:128] + passing_up.astype(F32)).astype(BF), 0, 1))
    parts[1].append(home((sums[2][128:] + passing_down.astype(F32)).astype(BF), 1, 3))
    pieces = [sum(part.astype(F32) for part in piece).astype(BF) for piece in parts]
    even = yl == 0
    pair = jnp.where(even, pieces[0], pieces[1]), jnp.where(even, pieces[1], pieces[0])
    return jnp.concatenate(
        [jnp.concatenate([p[:, 448 * i : 448 * i + 448] for p in pair], 1) for i in range(2)], 0
    )


def solution(mesh):
    cut = Mesh(mesh.devices.reshape(SIZES), AXES) if hasattr(mesh, "devices") else mesh
    tokens = ("yl", "yh", "z")
    return jax.shard_map(
        local,
        mesh=cut,
        in_specs=(
            P(tokens, None),
            P(tokens, None),
            P("yl", None),
            P("yl"),
            P(None, HEAD),
            P(HEAD, None, None),
            P(HEAD, None, None),
            P(HEAD, CTX, None),
        ),
        out_specs=P(tokens, HEAD),
        check_vma=False,
    )
```

```python
import functools

import jax
import jax.numpy as jnp
from jax import lax
from jax.experimental import pallas as pl
from jax.experimental.pallas import tpu as pltpu
from jax.sharding import Mesh
from jax.sharding import PartitionSpec as P

AXES = ("yh", "z", "x", "c", "yl")
SIZES = (2, 8, 4, 2, 2)
CTX = ("yh", "z")
HEAD = ("x", "c")
BF = jnp.bfloat16
F32 = jnp.float32
VMEM = pltpu.MemorySpace.VMEM


def number_of(yh, z, x, c, yl):
    return (((yh * 8 + z) * 4 + x) * 2 + c) * 2 + yl


def moved(a, target):
    pairs = []
    for yh in range(2):
        for z in range(8):
            for x in range(4):
                for c in range(2):
                    for yl in range(2):
                        t = target(yh, z, x, c, yl)
                        pairs.append((number_of(yh, z, x, c, yl), number_of(*t)))
    return lax.ppermute(a, AXES, pairs)


def up_z(a):
    return moved(a, lambda yh, z, x, c, yl: (yh, (z + 1) % 8, x, c, yl))


def down_z(a):
    return moved(a, lambda yh, z, x, c, yl: (yh, (z - 1) % 8, x, c, yl))


def xor_y(a, q):
    return moved(a, lambda yh, z, x, c, yl: (yh ^ (q >> 1), z, x, c, yl ^ (q & 1)))


def other_core(a):
    return moved(a, lambda yh, z, x, c, yl: (yh, z, x, 1 - c, yl))


def along_x(a, d):
    return moved(a, lambda yh, z, x, c, yl: (yh, z, (x + d) % 4, c, yl))


def home(a, r, d=0):
    return moved(a, lambda yh, z, x, c, yl: (yh ^ c, z, (x + d) % 4, yh, yl ^ r))


def turn_of(table):
    return jnp.concatenate([table[:, 32 * i : 32 * i + 32] for i in range(4)], 0)


def turned(rot, cosine, sine):
    other = jnp.concatenate([rot[:, 32:], rot[:, :32]], 1)
    cosine = jnp.concatenate([cosine, cosine], 1)
    sine = jnp.concatenate([-sine, sine], 1)
    rot = rot * cosine + other * sine
    return jnp.concatenate([rot, jnp.zeros_like(rot)], 1).astype(BF)


def queries_kernel(rows, w_query, w_key_up, cosines, sines, out, out_next, held, rows_held, sem):
    copies = [
        pltpu.make_async_copy(w_query.at[:, pl.ds(768 * part, 768)], held.at[part], sem.at[part])
        for part in range(2)
    ]
    copies.append(pltpu.make_async_copy(rows, rows_held, sem.at[2]))
    for i in (2, 0, 1):
        copies[i].start()
    cosine, sine = turn_of(cosines), turn_of(sines)
    copies[2].wait()
    for part in range(2):
        copies[part].wait()
        queries = jnp.dot(rows_held[...], held[part], preferred_element_type=F32).astype(BF)
        for i in range(4):
            h = 4 * part + i
            plain = queries[:, 192 * i : 192 * i + 128]
            lat = jnp.dot(plain, w_key_up[h], preferred_element_type=F32)
            rot = queries[:, 192 * i + 128 : 192 * i + 192].astype(F32)
            tokens = slice(256 * i, 256 * i + 256)
            to = out_next if part else out
            to[tokens, :512] = lat.astype(BF)
            to[tokens, 512:] = turned(rot, cosine, sine)


def keys_kernel(start, own, near, far, swapped, cache, cosines, sines, keys, hidden, raw, sem):
    c = lax.axis_index("c")
    slab = 8 * lax.axis_index("yh") + lax.axis_index("z")

    def at(column, columns):
        return raw.at[:, pl.ds(pl.multiple_of(column, 128), columns)]

    copies = [
        pltpu.make_async_copy(own, at(512, 256), sem.at[0]),
        pltpu.make_async_copy(near, at(256 + 128 * c, 128), sem.at[1]),
        pltpu.make_async_copy(swapped.at[:, pl.ds(0, 128)], at(384 - 128 * c, 128), sem.at[2]),
        pltpu.make_async_copy(far, at(128 * c, 128), sem.at[3]),
        pltpu.make_async_copy(swapped.at[:, pl.ds(128, 128)], at(128 - 128 * c, 128), sem.at[4]),
    ]
    for copy in copies:
        copy.start()
    row = lax.broadcasted_iota(jnp.int32, (256, 768), 0)
    col = lax.broadcasted_iota(jnp.int32, (256, 768), 1)
    relative = col - 512 - row
    visible = (relative <= 0) & (relative > -512) & (slab * 256 + col - 512 >= -start[0])
    hidden[...] = jnp.where(visible, 0.0, -1e30)
    for copy in copies:
        copy.wait()
    low, high = raw[512:544, :].astype(F32), raw[544:, :].astype(F32)
    cosine, sine = cosines[...], sines[...]
    keys[:512, :] = raw[:512, :]
    keys[512:544, :] = (low * cosine - high * sine).astype(BF)
    keys[544:576, :] = (low * sine + high * cosine).astype(BF)
    keys[576:, :] = jnp.zeros((64, 768), BF)

    @pl.when(slab < 2)
    def _():
        copy = pltpu.make_async_copy(cache, at(0, 512), sem.at[0])
        copy.start()
        copy.wait()

    @pl.when(slab == 0)
    def _():
        keys[:576, :512] = raw[:, :512]

    @pl.when(slab == 1)
    def _():
        keys[:576, :256] = raw[:, 256:512]


def attend_kernel(group, queries, keys, hidden, w_value_up, reorder, out):
    scale = 192.0**-0.5 * 1.4426950408889634
    heads = []
    for pair in range(2):
        scores = jnp.dot(
            queries[512 * pair : 512 * pair + 512, :], keys[...], preferred_element_type=F32
        )
        for i in range(2):
            part = scores[256 * i : 256 * i + 256] * scale + hidden[...]
            top = jnp.max(part, axis=1, keepdims=True)
            powers = jnp.exp2(part - top)
            share = 1.0 / jnp.sum(powers, axis=1, keepdims=True)
            mixed = lax.dot_general(
                powers.astype(BF),
                keys[:512, :],
                (((1,), (1,)), ((), ())),
                preferred_element_type=F32,
            )
            attention = jnp.dot(
                (mixed * share).astype(BF),
                w_value_up[4 * group + 2 * pair + i],
                preferred_element_type=F32,
            )
            heads.append(attention.astype(BF))
    rows = jnp.concatenate(heads, 1)
    out[...] = jnp.dot(rows, reorder[...], preferred_element_type=F32).astype(BF)


def turns(first):
    inverse = jnp.power(jnp.float32(10000.0), -jnp.arange(32, dtype=F32) * (2.0 / 64))
    row = lax.broadcasted_iota(jnp.int32, (64, 128), 0)
    lane = lax.broadcasted_iota(jnp.int32, (64, 128), 1)
    own = (first + (lane // 32) * 64 + row).astype(F32) * jnp.tile(inverse, 4)[None, :]
    place = first - 512 + lax.broadcasted_iota(jnp.int32, (32, 768), 1)
    every = place.astype(F32) * inverse[:, None]
    return jnp.cos(own), jnp.sin(own), jnp.cos(every), jnp.sin(every)


def quarter_kernel(rows, own, other):
    x = lax.axis_index("x")
    for out, flip in ((own, 0), (other, 1)):
        odd = lax.axis_index("yl") ^ flip
        base = 896 * (lax.axis_index("yh") ^ flip) + 384 * odd
        pieces = []
        for d in range(4):
            start = pl.multiple_of(1792 * ((x + d) % 4) + base, 128)
            wide = rows[:, pl.ds(start, 512)]
            pieces.append(jnp.where(odd == 1, wide[:, 64:], wide[:, :448]))
        out[...] = jnp.concatenate(pieces, 1)


def project_kernel(theirs, *refs):
    groups, held, outs, (rows, total) = refs[:8], refs[8:21], refs[21:-2], refs[-2:]
    own, d1, d2, d3, u4, u3, u2, u1, other, e1, e3, e4, v1 = held
    blocks = [own, d1, d2, d3.at[:64], u4.at[:64], u3.at[:64], u2, u1]
    blocks += [other, e1, d3.at[64:], e3, e4, u4.at[64:], u3.at[64:], v1]
    first = 2 * (lax.axis_index("c") ^ theirs)
    yh = lax.axis_index("yh")
    for pick in (0, 2):

        @pl.when(first == pick)
        def _():
            for g in range(2):
                for j in range(2):
                    for p in range(2):
                        half = pl.ds(pl.multiple_of(256 * (yh ^ p), 256), 256)
                        rows[256 * j : 256 * j + 256, 512 * g + 256 * p : 512 * g + 256 * p + 256] = (
                            groups[2 * (pick + j) + g][:, half]
                        )

    for n in range(7):
        columns = slice(256 * n, 256 * n + 256)
        weights = jnp.concatenate(
            [
                block[32 * g : 32 * g + 32, columns]
                for g in range(2)
                for block in blocks
            ],
            0,
        )
        total[:, columns] = jnp.dot(rows[...], weights, preferred_element_type=F32)
    for out, d in zip((outs[0], *(outs[1].at[i] for i in range(3))), (2, 0, 1, 3)):
        span = slice(448 * d, 448 * d + 448)
        for j in range(2):
            top = total[256 * j : 256 * j + 128, span]
            low = total[256 * j + 128 : 256 * j + 256, span]
            out[128 * j : 128 * j + 128, :] = jnp.concatenate([top, low], 1).astype(out.dtype)


def whole(n):
    return [pl.BlockSpec(memory_space=VMEM)] * n


def placed(n):
    return [pl.BlockSpec(memory_space=pl.ANY)] * n


def kept(n=1):
    return [pl.BlockSpec(memory_space=pltpu.MemorySpace.HBM)] * n


def scalars(n=1):
    return [pl.BlockSpec(memory_space=pltpu.MemorySpace.SMEM)] * n


def quarters(rows):
    return pl.pallas_call(
        quarter_kernel,
        out_shape=[jax.ShapeDtypeStruct((64, 1792), BF)] * 2,
        in_specs=whole(1),
        out_specs=whole(2),
        name="quarters",
        cost_estimate=pl.CostEstimate(flops=0, bytes_accessed=2 << 20, transcendentals=0),
    )(rows)


def call(kernel, shapes, specs, args, name, flops, moved_bytes, room, scratch=()):
    many = isinstance(shapes, list)
    return pl.pallas_call(
        kernel,
        out_shape=shapes,
        in_specs=specs,
        out_specs=whole(len(shapes)) if many else whole(1)[0],
        scratch_shapes=list(scratch),
        compiler_params=pltpu.CompilerParams(vmem_limit_bytes=room << 20),
        name=name,
        cost_estimate=pl.CostEstimate(
            flops=flops, bytes_accessed=moved_bytes, transcendentals=0
        ),
    )(*args)


def array(shape, kind=BF):
    return jax.ShapeDtypeStruct(shape, kind)


def after(value, *others):
    return lax.optimization_barrier((value, *others))[0]


def project(theirs, groups, blocks, kind):
    return call(
        functools.partial(project_kernel, theirs),
        [array((256, 896), kind), array((3, 256, 896), kind)],
        whole(21),
        (*groups, *blocks),
        "project",
        2 * 512 * 1024 * 1792,
        8 << 20,
        12,
        [pltpu.VMEM((512, 1024), BF), pltpu.VMEM((512, 1792), F32)],
    )


def local(query_latent, key_rows, key_cache, prompt_start, w_query, w_key_up, w_value_up, w_output):
    yh, z, x, c, yl = (lax.axis_index(a) for a in AXES)
    slab = 8 * yh + z
    own, given = quarters(w_output.reshape(64, 7168))
    other = xor_y(given, 3)
    u1, d1 = up_z(own), down_z(own)

    own_keys = key_rows.T
    half = lax.dynamic_slice_in_dim(own_keys, 128 * c, 128, 1)
    near, far = (
        lax.ppermute(half, CTX, [(i, i + by) for i in range(16 - by)]) for by in (1, 2)
    )
    cosines, sines, all_cosines, all_sines = turns(slab * 256)
    queries = call(
        queries_kernel,
        [array((1024, 640))] * 2,
        kept(2) + whole(3),
        (query_latent, w_query, w_key_up, cosines, sines),
        "queries",
        2 * 256 * 1536 * 1536 + 2 * 2048 * 128 * 512,
        8 << 20,
        60,
        [
            pltpu.VMEM((2, 1536, 768), BF),
            pltpu.VMEM((256, 1536), BF),
            pltpu.SemaphoreType.DMA((3,)),
        ],
    )
    swapped = other_core(jnp.concatenate([near, far], 1))
    u2, d2 = up_z(after(u1, queries[0])), down_z(after(d1, queries[0]))
    v1, e1 = up_z(other), down_z(other)

    keys, hidden = call(
        keys_kernel,
        [array((640, 768)), array((256, 768), F32)],
        scalars() + kept() + placed(3) + kept() + whole(2),
        (prompt_start, own_keys, near, far, swapped, key_cache.T, all_cosines, all_sines),
        "keys",
        768 * 640 * 8,
        4 << 20,
        8,
        [pltpu.VMEM((576, 768), BF), pltpu.SemaphoreType.DMA((5,))],
    )
    column = jnp.arange(512, dtype=jnp.int32)
    source = (
        (column // 8 % 4) * 128 + (column // 256) * 64 + ((z + column // 32) % 8) * 8 + column % 8
    )
    reorder = (column[:, None] == source[None, :]).astype(BF)
    rows = [
        call(
            functools.partial(attend_kernel, g),
            array((256, 512)),
            whole(5),
            (queries[g], keys, hidden, w_value_up, reorder),
            "attend",
            2 * 1024 * 768 * 1152 + 2 * 1024 * 512 * 128,
            5 << 20,
            14,
        )
        for g in range(2)
    ]
    one = [xor_y(part, 1) for part in rows]
    three = [xor_y(part, 3) for part in rows]
    two = [xor_y(one[0], 3), xor_y(three[1], 1)]
    groups = [*rows, *one, *two, *three]
    u3 = up_z(after(jnp.concatenate([u2, v1], 0), rows[0]))
    d3 = down_z(after(jnp.concatenate([d2, e1], 0), rows[0]))
    u4 = up_z(u3)
    e3 = down_z(d3[64:])
    e4 = down_z(e3)
    blocks = [own, d1, d2, d3, u4, u3, u2, u1, other, e1, e3, e4, v1]

    first, rest = project(1, groups, blocks, BF)
    first, rest = other_core(first), other_core(rest)
    mine, mine_rest = project(0, groups, blocks, F32)
    far_sum = (mine + first.astype(F32)).astype(BF)
    passing_up = along_x(far_sum[:128], 1)
    passing_down = along_x(far_sum[128:], 3)
    sums = [mine_rest[i] + rest[i].astype(F32) for i in range(3)]
    early_up, early_down = lax.optimization_barrier(
        (sums[1][128:].astype(BF), sums[2][:128].astype(BF))
    )
    early_up, early_down = along_x(early_up, 1), along_x(early_down, 3)
    late_up = home((sums[1][:128] + passing_up.astype(F32)).astype(BF), 0, 1)
    late_down = home((sums[2][128:] + passing_down.astype(F32)).astype(BF), 1, 3)
    parts = [
        [home((sums[0][:128] + early_down.astype(F32)).astype(BF), 0), late_up],
        [home((sums[0][128:] + early_up.astype(F32)).astype(BF), 1), late_down],
    ]
    pieces = [sum(part.astype(F32) for part in piece).astype(BF) for piece in parts]
    even = yl == 0
    pair = jnp.where(even, pieces[0], pieces[1]), jnp.where(even, pieces[1], pieces[0])
    return jnp.concatenate(
        [jnp.concatenate([p[:, 448 * i : 448 * i + 448] for p in pair], 1) for i in range(2)], 0
    )


def solution(mesh):
    cut = Mesh(mesh.devices.reshape(SIZES), AXES) if hasattr(mesh, "devices") else mesh
    tokens = ("yl", "yh", "z")
    return jax.shard_map(
        local,
        mesh=cut,
        in_specs=(
            P(tokens, None),
            P(tokens, None),
            P("yl", None),
            P("yl"),
            P(None, HEAD),
            P(HEAD, None, None),
            P(HEAD, None, None),
            P(HEAD, CTX, None),
        ),
        out_specs=P(tokens, HEAD),
        check_vma=False,
    )
```

```python
import functools

import jax
import jax.numpy as jnp
from jax import lax
from jax.experimental import pallas as pl
from jax.experimental.pallas import tpu as pltpu
from jax.sharding import Mesh
from jax.sharding import PartitionSpec as P

AXES = ("yh", "z", "x", "c", "yl")
SIZES = (2, 8, 4, 2, 2)
CTX = ("yh", "z")
HEAD = ("x", "c")
BF = jnp.bfloat16
F32 = jnp.float32
VMEM = pltpu.MemorySpace.VMEM


def number_of(yh, z, x, c, yl):
    return (((yh * 8 + z) * 4 + x) * 2 + c) * 2 + yl


def moved(a, target):
    pairs = []
    for yh in range(2):
        for z in range(8):
            for x in range(4):
                for c in range(2):
                    for yl in range(2):
                        t = target(yh, z, x, c, yl)
                        pairs.append((number_of(yh, z, x, c, yl), number_of(*t)))
    return lax.ppermute(a, AXES, pairs)


def up_z(a):
    return moved(a, lambda yh, z, x, c, yl: (yh, (z + 1) % 8, x, c, yl))


def down_z(a):
    return moved(a, lambda yh, z, x, c, yl: (yh, (z - 1) % 8, x, c, yl))


def xor_y(a, q):
    return moved(a, lambda yh, z, x, c, yl: (yh ^ (q >> 1), z, x, c, yl ^ (q & 1)))


def other_core(a):
    return moved(a, lambda yh, z, x, c, yl: (yh, z, x, 1 - c, yl))


def along_x(a, d):
    return moved(a, lambda yh, z, x, c, yl: (yh, z, (x + d) % 4, c, yl))


def home(a, r, d=0):
    return moved(a, lambda yh, z, x, c, yl: (yh ^ c, z, (x + d) % 4, yh, yl ^ r))


def turn_of(table):
    return jnp.concatenate([table[:, 32 * i : 32 * i + 32] for i in range(4)], 0)


def turned(rot, cosine, sine):
    other = jnp.concatenate([rot[:, 32:], rot[:, :32]], 1)
    cosine = jnp.concatenate([cosine, cosine], 1)
    sine = jnp.concatenate([-sine, sine], 1)
    rot = rot * cosine + other * sine
    return jnp.concatenate([rot, jnp.zeros_like(rot)], 1).astype(BF)


def queries_kernel(rows, w_query, w_key_up, cosines, sines, out, out_next, held, rows_held, sem):
    copies = [
        pltpu.make_async_copy(w_query.at[:, pl.ds(768 * part, 768)], held.at[part], sem.at[part])
        for part in range(2)
    ]
    copies.append(pltpu.make_async_copy(rows, rows_held, sem.at[2]))
    for i in (2, 0, 1):
        copies[i].start()
    cosine, sine = turn_of(cosines), turn_of(sines)
    copies[2].wait()
    for part in range(2):
        copies[part].wait()
        queries = jnp.dot(rows_held[...], held[part], preferred_element_type=F32).astype(BF)
        for i in range(4):
            h = 4 * part + i
            plain = queries[:, 192 * i : 192 * i + 128]
            lat = jnp.dot(plain, w_key_up[h], preferred_element_type=F32)
            rot = queries[:, 192 * i + 128 : 192 * i + 192].astype(F32)
            tokens = slice(256 * i, 256 * i + 256)
            to = out_next if part else out
            to[tokens, :512] = lat.astype(BF)
            to[tokens, 512:] = turned(rot, cosine, sine)


def keys_kernel(start, own, near, far, swapped, cache, cosines, sines, keys, hidden, raw, sem):
    c = lax.axis_index("c")
    slab = 8 * lax.axis_index("yh") + lax.axis_index("z")

    def at(column, columns):
        return raw.at[:, pl.ds(pl.multiple_of(column, 128), columns)]

    copies = [
        pltpu.make_async_copy(own, at(512, 256), sem.at[0]),
        pltpu.make_async_copy(near, at(256 + 128 * c, 128), sem.at[1]),
        pltpu.make_async_copy(swapped.at[:, pl.ds(0, 128)], at(384 - 128 * c, 128), sem.at[2]),
        pltpu.make_async_copy(far, at(128 * c, 128), sem.at[3]),
        pltpu.make_async_copy(swapped.at[:, pl.ds(128, 128)], at(128 - 128 * c, 128), sem.at[4]),
    ]
    for copy in copies:
        copy.start()
    row = lax.broadcasted_iota(jnp.int32, (256, 768), 0)
    col = lax.broadcasted_iota(jnp.int32, (256, 768), 1)
    relative = col - 512 - row
    visible = (relative <= 0) & (relative > -512) & (slab * 256 + col - 512 >= -start[0])
    hidden[...] = jnp.where(visible, 0.0, -1e30)
    for copy in copies:
        copy.wait()
    low, high = raw[512:544, :].astype(F32), raw[544:, :].astype(F32)
    cosine, sine = cosines[...], sines[...]
    keys[:512, :] = raw[:512, :]
    keys[512:544, :] = (low * cosine - high * sine).astype(BF)
    keys[544:576, :] = (low * sine + high * cosine).astype(BF)
    keys[576:, :] = jnp.zeros((64, 768), BF)

    @pl.when(slab < 2)
    def _():
        copy = pltpu.make_async_copy(cache, at(0, 512), sem.at[0])
        copy.start()
        copy.wait()

    @pl.when(slab == 0)
    def _():
        keys[:576, :512] = raw[:, :512]

    @pl.when(slab == 1)
    def _():
        keys[:576, :256] = raw[:, 256:512]


def attend_kernel(group, queries, keys, hidden, w_value_up, reorder, out):
    scale = 192.0**-0.5 * 1.4426950408889634
    heads = []
    for pair in range(2):
        scores = jnp.dot(
            queries[512 * pair : 512 * pair + 512, :], keys[...], preferred_element_type=F32
        )
        for i in range(2):
            part = scores[256 * i : 256 * i + 256] * scale + hidden[...]
            top = jnp.max(part, axis=1, keepdims=True)
            powers = jnp.exp2(part - top)
            share = 1.0 / jnp.sum(powers, axis=1, keepdims=True)
            mixed = lax.dot_general(
                powers.astype(BF),
                keys[:512, :],
                (((1,), (1,)), ((), ())),
                preferred_element_type=F32,
            )
            attention = jnp.dot(
                (mixed * share).astype(BF),
                w_value_up[4 * group + 2 * pair + i],
                preferred_element_type=F32,
            )
            heads.append(attention.astype(BF))
    rows = jnp.concatenate(heads, 1)
    out[...] = jnp.dot(rows, reorder[...], preferred_element_type=F32).astype(BF)


def turns(first):
    inverse = jnp.power(jnp.float32(10000.0), -jnp.arange(32, dtype=F32) * (2.0 / 64))
    row = lax.broadcasted_iota(jnp.int32, (64, 128), 0)
    lane = lax.broadcasted_iota(jnp.int32, (64, 128), 1)
    own = (first + (lane // 32) * 64 + row).astype(F32) * jnp.tile(inverse, 4)[None, :]
    place = first - 512 + lax.broadcasted_iota(jnp.int32, (32, 768), 1)
    every = place.astype(F32) * inverse[:, None]
    return jnp.cos(own), jnp.sin(own), jnp.cos(every), jnp.sin(every)


def quarter_kernel(rows, own, other):
    x = lax.axis_index("x")
    for out, flip in ((own, 0), (other, 1)):
        odd = lax.axis_index("yl") ^ flip
        base = 896 * (lax.axis_index("yh") ^ flip) + 384 * odd
        pieces = []
        for d in range(4):
            start = pl.multiple_of(1792 * ((x + d) % 4) + base, 128)
            wide = rows[:, pl.ds(start, 512)]
            pieces.append(jnp.where(odd == 1, wide[:, 64:], wide[:, :448]))
        out[...] = jnp.concatenate(pieces, 1)


def project_kernel(theirs, *refs):
    groups, held, outs, (rows, total) = refs[:8], refs[8:19], refs[19:-2], refs[-2:]
    own, d1, d2, d3, u4, u3, u2, u1, other, e3, e4 = held
    blocks = [own, d1, *(both.at[:64] for both in (d2, d3, u4, u3, u2)), u1]
    blocks += [other, d2.at[64:], d3.at[64:], e3, e4, *(both.at[64:] for both in (u4, u3, u2))]
    first = 2 * (lax.axis_index("c") ^ theirs)
    yh = lax.axis_index("yh")
    for pick in (0, 2):

        @pl.when(first == pick)
        def _():
            for g in range(2):
                for j in range(2):
                    for p in range(2):
                        half = pl.ds(pl.multiple_of(256 * (yh ^ p), 256), 256)
                        rows[256 * j : 256 * j + 256, 512 * g + 256 * p : 512 * g + 256 * p + 256] = (
                            groups[2 * (pick + j) + g][:, half]
                        )

    for n in range(7):
        columns = slice(256 * n, 256 * n + 256)
        weights = jnp.concatenate(
            [
                block[32 * g : 32 * g + 32, columns]
                for g in range(2)
                for block in blocks
            ],
            0,
        )
        total[:, columns] = jnp.dot(rows[...], weights, preferred_element_type=F32)
    for out, d in zip((outs[0], *(outs[1].at[i] for i in range(3))), (2, 0, 1, 3)):
        span = slice(448 * d, 448 * d + 448)
        for j in range(2):
            top = total[256 * j : 256 * j + 128, span]
            low = total[256 * j + 128 : 256 * j + 256, span]
            out[128 * j : 128 * j + 128, :] = jnp.concatenate([top, low], 1).astype(out.dtype)


def whole(n):
    return [pl.BlockSpec(memory_space=VMEM)] * n


def placed(n):
    return [pl.BlockSpec(memory_space=pl.ANY)] * n


def kept(n=1):
    return [pl.BlockSpec(memory_space=pltpu.MemorySpace.HBM)] * n


def scalars(n=1):
    return [pl.BlockSpec(memory_space=pltpu.MemorySpace.SMEM)] * n


def quarters(rows):
    return pl.pallas_call(
        quarter_kernel,
        out_shape=[jax.ShapeDtypeStruct((64, 1792), BF)] * 2,
        in_specs=whole(1),
        out_specs=whole(2),
        name="quarters",
        cost_estimate=pl.CostEstimate(flops=0, bytes_accessed=2 << 20, transcendentals=0),
    )(rows)


def call(kernel, shapes, specs, args, name, flops, moved_bytes, room, scratch=()):
    many = isinstance(shapes, list)
    return pl.pallas_call(
        kernel,
        out_shape=shapes,
        in_specs=specs,
        out_specs=whole(len(shapes)) if many else whole(1)[0],
        scratch_shapes=list(scratch),
        compiler_params=pltpu.CompilerParams(vmem_limit_bytes=room << 20),
        name=name,
        cost_estimate=pl.CostEstimate(
            flops=flops, bytes_accessed=moved_bytes, transcendentals=0
        ),
    )(*args)


def array(shape, kind=BF):
    return jax.ShapeDtypeStruct(shape, kind)


def after(value, *others):
    return lax.optimization_barrier((value, *others))[0]


def project(theirs, groups, blocks, kind):
    return call(
        functools.partial(project_kernel, theirs),
        [array((256, 896), kind), array((3, 256, 896), kind)],
        whole(19),
        (*groups, *blocks),
        "project",
        2 * 512 * 1024 * 1792,
        8 << 20,
        12,
        [pltpu.VMEM((512, 1024), BF), pltpu.VMEM((512, 1792), F32)],
    )


def local(query_latent, key_rows, key_cache, prompt_start, w_query, w_key_up, w_value_up, w_output):
    yh, z, x, c, yl = (lax.axis_index(a) for a in AXES)
    slab = 8 * yh + z
    own, given = quarters(w_output.reshape(64, 7168))
    other = xor_y(given, 3)
    u1, d1 = up_z(own), down_z(own)

    own_keys = key_rows.T
    half = lax.dynamic_slice_in_dim(own_keys, 128 * c, 128, 1)
    near, far = (
        lax.ppermute(half, CTX, [(i, i + by) for i in range(16 - by)]) for by in (1, 2)
    )
    cosines, sines, all_cosines, all_sines = turns(slab * 256)
    queries = call(
        queries_kernel,
        [array((1024, 640))] * 2,
        kept(2) + whole(3),
        (query_latent, w_query, w_key_up, cosines, sines),
        "queries",
        2 * 256 * 1536 * 1536 + 2 * 2048 * 128 * 512,
        8 << 20,
        60,
        [
            pltpu.VMEM((2, 1536, 768), BF),
            pltpu.VMEM((256, 1536), BF),
            pltpu.SemaphoreType.DMA((3,)),
        ],
    )
    swapped = other_core(jnp.concatenate([near, far], 1))
    u2 = up_z(after(jnp.concatenate([u1, other], 0), queries[0]))
    d2 = down_z(after(jnp.concatenate([d1, other], 0), queries[0]))

    keys, hidden = call(
        keys_kernel,
        [array((640, 768)), array((256, 768), F32)],
        scalars() + kept() + placed(3) + kept() + whole(2),
        (prompt_start, own_keys, near, far, swapped, key_cache.T, all_cosines, all_sines),
        "keys",
        768 * 640 * 8,
        4 << 20,
        8,
        [pltpu.VMEM((576, 768), BF), pltpu.SemaphoreType.DMA((5,))],
    )
    column = jnp.arange(512, dtype=jnp.int32)
    source = (
        (column // 8 % 4) * 128 + (column // 256) * 64 + ((z + column // 32) % 8) * 8 + column % 8
    )
    reorder = (column[:, None] == source[None, :]).astype(BF)
    rows = [
        call(
            functools.partial(attend_kernel, g),
            array((256, 512)),
            whole(5),
            (queries[g], keys, hidden, w_value_up, reorder),
            "attend",
            2 * 1024 * 768 * 1152 + 2 * 1024 * 512 * 128,
            5 << 20,
            14,
        )
        for g in range(2)
    ]
    one = [xor_y(part, 1) for part in rows]
    three = [xor_y(part, 3) for part in rows]
    two = [xor_y(one[0], 3), xor_y(three[1], 1)]
    groups = [*rows, *one, *two, *three]
    u3, d3 = up_z(after(u2, *rows)), down_z(after(d2, *rows))
    u4 = up_z(u3)
    e3 = down_z(d3[64:])
    e4 = down_z(e3)
    blocks = [own, d1, d2, d3, u4, u3, u2, u1, other, e3, e4]

    first, rest = project(1, groups, blocks, BF)
    first, rest = other_core(first), other_core(rest)
    mine, mine_rest = project(0, groups, blocks, F32)
    sums = [mine_rest[i] + rest[i].astype(F32) for i in range(3)]
    early_up, early_down, first, mine = lax.optimization_barrier(
        (sums[1][128:].astype(BF), sums[2][:128].astype(BF), first, mine)
    )
    far_sum = (mine + first.astype(F32)).astype(BF)
    passing_up = along_x(far_sum[:128], 1)
    passing_down = along_x(far_sum[128:], 3)
    early_up, early_down = along_x(early_up, 1), along_x(early_down, 3)
    late_up = home((sums[1][:128] + passing_up.astype(F32)).astype(BF), 0, 1)
    late_down = home((sums[2][128:] + passing_down.astype(F32)).astype(BF), 1, 3)
    parts = [
        [home((sums[0][:128] + early_down.astype(F32)).astype(BF), 0), late_up],
        [home((sums[0][128:] + early_up.astype(F32)).astype(BF), 1), late_down],
    ]
    pieces = [sum(part.astype(F32) for part in piece).astype(BF) for piece in parts]
    even = yl == 0
    pair = jnp.where(even, pieces[0], pieces[1]), jnp.where(even, pieces[1], pieces[0])
    return jnp.concatenate(
        [jnp.concatenate([p[:, 448 * i : 448 * i + 448] for p in pair], 1) for i in range(2)], 0
    )


def solution(mesh):
    cut = Mesh(mesh.devices.reshape(SIZES), AXES) if hasattr(mesh, "devices") else mesh
    tokens = ("yl", "yh", "z")
    return jax.shard_map(
        local,
        mesh=cut,
        in_specs=(
            P(tokens, None),
            P(tokens, None),
            P("yl", None),
            P("yl"),
            P(None, HEAD),
            P(HEAD, None, None),
            P(HEAD, None, None),
            P(HEAD, CTX, None),
        ),
        out_specs=P(tokens, HEAD),
        check_vma=False,
    )
```

```python
import functools

import jax
import jax.numpy as jnp
import numpy as np
from jax import lax
from jax.experimental import pallas as pl
from jax.experimental.pallas import tpu as pltpu
from jax.sharding import Mesh
from jax.sharding import PartitionSpec as P

AXES = ("yh", "z", "x", "c", "yl")
SIZES = (2, 8, 4, 2, 2)
CTX = ("yh", "z")
HEAD = ("x", "c")
BF = jnp.bfloat16
F32 = jnp.float32
VMEM = pltpu.MemorySpace.VMEM


def number_of(yh, z, x, c, yl):
    return (((yh * 8 + z) * 4 + x) * 2 + c) * 2 + yl


def moved(a, target):
    pairs = []
    for yh in range(2):
        for z in range(8):
            for x in range(4):
                for c in range(2):
                    for yl in range(2):
                        t = target(yh, z, x, c, yl)
                        pairs.append((number_of(yh, z, x, c, yl), number_of(*t)))
    return lax.ppermute(a, AXES, pairs)


def up_z(a):
    return moved(a, lambda yh, z, x, c, yl: (yh, (z + 1) % 8, x, c, yl))


def down_z(a):
    return moved(a, lambda yh, z, x, c, yl: (yh, (z - 1) % 8, x, c, yl))


def xor_y(a, q):
    return moved(a, lambda yh, z, x, c, yl: (yh ^ (q >> 1), z, x, c, yl ^ (q & 1)))


def other_core(a):
    return moved(a, lambda yh, z, x, c, yl: (yh, z, x, 1 - c, yl))


def along_x(a, d):
    return moved(a, lambda yh, z, x, c, yl: (yh, z, (x + d) % 4, c, yl))


def home(a, r, d=0):
    return moved(a, lambda yh, z, x, c, yl: (yh ^ c, z, (x + d) % 4, yh, yl ^ r))


def turn_of(table):
    return jnp.concatenate([table[:, 32 * i : 32 * i + 32] for i in range(4)], 0)


def turned(rot, cosine, sine):
    other = jnp.concatenate([rot[:, 32:], rot[:, :32]], 1)
    cosine = jnp.concatenate([cosine, cosine], 1)
    sine = jnp.concatenate([-sine, sine], 1)
    rot = rot * cosine + other * sine
    return jnp.concatenate([rot, jnp.zeros_like(rot)], 1).astype(BF)


def queries_kernel(rows, w_query, w_key_up, cosines, sines, out, out_next, held, rows_held, sem):
    copies = [
        pltpu.make_async_copy(w_query.at[:, pl.ds(768 * part, 768)], held.at[part], sem.at[part])
        for part in range(2)
    ]
    copies.append(pltpu.make_async_copy(rows, rows_held, sem.at[2]))
    for i in (2, 0, 1):
        copies[i].start()
    cosine, sine = turn_of(cosines), turn_of(sines)
    copies[2].wait()
    for part in range(2):
        copies[part].wait()
        queries = jnp.dot(rows_held[...], held[part], preferred_element_type=F32).astype(BF)
        for i in range(4):
            h = 4 * part + i
            plain = queries[:, 192 * i : 192 * i + 128]
            lat = jnp.dot(plain, w_key_up[h], preferred_element_type=F32)
            rot = queries[:, 192 * i + 128 : 192 * i + 192].astype(F32)
            tokens = slice(256 * i, 256 * i + 256)
            to = out_next if part else out
            to[tokens, :512] = lat.astype(BF)
            to[tokens, 512:] = turned(rot, cosine, sine)


def keys_kernel(start, own, near, far, swapped, cache, cosines, sines, keys, hidden, raw, sem):
    c = lax.axis_index("c")
    slab = 8 * lax.axis_index("yh") + lax.axis_index("z")

    def at(column, columns):
        return raw.at[:, pl.ds(pl.multiple_of(column, 128), columns)]

    copies = [
        pltpu.make_async_copy(own, at(512, 256), sem.at[0]),
        pltpu.make_async_copy(near, at(256 + 128 * c, 128), sem.at[1]),
        pltpu.make_async_copy(swapped.at[:, pl.ds(0, 128)], at(384 - 128 * c, 128), sem.at[2]),
        pltpu.make_async_copy(far, at(128 * c, 128), sem.at[3]),
        pltpu.make_async_copy(swapped.at[:, pl.ds(128, 128)], at(128 - 128 * c, 128), sem.at[4]),
    ]
    for copy in copies:
        copy.start()
    row = lax.broadcasted_iota(jnp.int32, (256, 768), 0)
    col = lax.broadcasted_iota(jnp.int32, (256, 768), 1)
    relative = col - 512 - row
    visible = (relative <= 0) & (relative > -512) & (slab * 256 + col - 512 >= -start[0])
    hidden[...] = jnp.where(visible, 0.0, -1e30)
    for copy in copies:
        copy.wait()
    low, high = raw[512:544, :].astype(F32), raw[544:, :].astype(F32)
    cosine, sine = cosines[...], sines[...]
    keys[:512, :] = raw[:512, :]
    keys[512:544, :] = (low * cosine - high * sine).astype(BF)
    keys[544:576, :] = (low * sine + high * cosine).astype(BF)
    keys[576:, :] = jnp.zeros((64, 768), BF)

    @pl.when(slab < 2)
    def _():
        copy = pltpu.make_async_copy(cache, at(0, 512), sem.at[0])
        copy.start()
        copy.wait()

    @pl.when(slab == 0)
    def _():
        keys[:576, :512] = raw[:, :512]

    @pl.when(slab == 1)
    def _():
        keys[:576, :256] = raw[:, 256:512]


def attend_kernel(queries, queries_next, keys, hidden, w_value_up, reorder, out):
    scale = 192.0**-0.5 * 1.4426950408889634
    for group, held in enumerate((queries, queries_next)):
        heads = []
        for pair in range(2):
            scores = jnp.dot(
                held[512 * pair : 512 * pair + 512, :], keys[...], preferred_element_type=F32
            )
            for i in range(2):
                part = scores[256 * i : 256 * i + 256] * scale + hidden[...]
                top = jnp.max(part, axis=1, keepdims=True)
                powers = jnp.exp2(part - top)
                share = 1.0 / jnp.sum(powers, axis=1, keepdims=True)
                mixed = lax.dot_general(
                    powers.astype(BF),
                    keys[:512, :],
                    (((1,), (1,)), ((), ())),
                    preferred_element_type=F32,
                )
                attention = jnp.dot(
                    (mixed * share).astype(BF),
                    w_value_up[4 * group + 2 * pair + i],
                    preferred_element_type=F32,
                )
                heads.append(attention.astype(BF))
        rows = jnp.concatenate(heads, 1)
        out[:, 512 * group : 512 * group + 512] = jnp.dot(
            rows, reorder[...], preferred_element_type=F32
        ).astype(BF)


def turns(first):
    inverse = (10000.0 ** (-np.arange(32) * (2.0 / 64))).astype(np.float32)
    lane = np.arange(128)[None, :]
    place = (np.arange(64)[:, None] + (lane // 32) * 64).astype(np.float32)
    start = first.astype(F32)
    own = (start + place) * np.tile(inverse, 4)[None, :]
    every = (start - 512 + np.arange(768, dtype=np.float32)[None, :]) * inverse[:, None]
    return jnp.cos(own), jnp.sin(own), jnp.cos(every), jnp.sin(every)


def quarter_kernel(rows, own, other):
    x = lax.axis_index("x")
    for out, flip in ((own, 0), (other, 1)):
        odd = lax.axis_index("yl") ^ flip
        base = 896 * (lax.axis_index("yh") ^ flip) + 384 * odd
        pieces = []
        for d in range(4):
            start = pl.multiple_of(1792 * ((x + d) % 4) + base, 128)
            wide = rows[:, pl.ds(start, 512)]
            pieces.append(jnp.where(odd == 1, wide[:, 64:], wide[:, :448]))
        out[...] = jnp.concatenate(pieces, 1)


def project_kernel(theirs, *refs):
    groups, held, outs, (rows, total) = refs[:5], refs[5:16], refs[16:-2], refs[-2:]
    own, d1, d2, d3, u4, u3, u2, u1, other, e3, e4 = held
    blocks = [own, d1, *(both.at[:64] for both in (d2, d3, u4, u3, u2)), u1]
    blocks += [other, d2.at[64:], d3.at[64:], e3, e4, *(both.at[64:] for both in (u4, u3, u2))]
    first = 2 * (lax.axis_index("c") ^ theirs)
    yh = lax.axis_index("yh")
    for pick in (0, 2):

        @pl.when(first == pick)
        def _():
            at = 0
            for part in groups[2:] if pick else groups[:2]:
                for g in range(2):
                    for p in range(2):
                        half = pl.ds(pl.multiple_of(512 * g + 256 * (yh ^ p), 256), 256)
                        to = 512 * g + 256 * p
                        rows[at : at + part.shape[0], to : to + 256] = part[:, half]
                at += part.shape[0]

    for n in range(7):
        columns = slice(256 * n, 256 * n + 256)
        weights = jnp.concatenate(
            [
                block[32 * g : 32 * g + 32, columns]
                for g in range(2)
                for block in blocks
            ],
            0,
        )
        total[:, columns] = jnp.dot(rows[...], weights, preferred_element_type=F32)
    for out, d in zip((outs[0], *(outs[1].at[i] for i in range(3))), (2, 0, 1, 3)):
        span = slice(448 * d, 448 * d + 448)
        for j in range(2):
            top = total[256 * j : 256 * j + 128, span]
            low = total[256 * j + 128 : 256 * j + 256, span]
            out[128 * j : 128 * j + 128, :] = jnp.concatenate([top, low], 1).astype(out.dtype)


def whole(n):
    return [pl.BlockSpec(memory_space=VMEM)] * n


def placed(n):
    return [pl.BlockSpec(memory_space=pl.ANY)] * n


def kept(n=1):
    return [pl.BlockSpec(memory_space=pltpu.MemorySpace.HBM)] * n


def scalars(n=1):
    return [pl.BlockSpec(memory_space=pltpu.MemorySpace.SMEM)] * n


def quarters(rows):
    return pl.pallas_call(
        quarter_kernel,
        out_shape=[jax.ShapeDtypeStruct((64, 1792), BF)] * 2,
        in_specs=whole(1),
        out_specs=whole(2),
        name="quarters",
        cost_estimate=pl.CostEstimate(flops=0, bytes_accessed=2 << 20, transcendentals=0),
    )(rows)


def call(kernel, shapes, specs, args, name, flops, moved_bytes, room, scratch=()):
    many = isinstance(shapes, list)
    return pl.pallas_call(
        kernel,
        out_shape=shapes,
        in_specs=specs,
        out_specs=whole(len(shapes)) if many else whole(1)[0],
        scratch_shapes=list(scratch),
        compiler_params=pltpu.CompilerParams(vmem_limit_bytes=room << 20),
        name=name,
        cost_estimate=pl.CostEstimate(
            flops=flops, bytes_accessed=moved_bytes, transcendentals=0
        ),
    )(*args)


def array(shape, kind=BF):
    return jax.ShapeDtypeStruct(shape, kind)


def after(value, *others):
    return lax.optimization_barrier((value, *others))[0]


def project(theirs, groups, blocks, kind):
    return call(
        functools.partial(project_kernel, theirs),
        [array((256, 896), kind), array((3, 256, 896), kind)],
        whole(16),
        (*groups, *blocks),
        "project",
        2 * 512 * 1024 * 1792,
        8 << 20,
        12,
        [pltpu.VMEM((512, 1024), BF), pltpu.VMEM((512, 1792), F32)],
    )


def local(query_latent, key_rows, key_cache, prompt_start, w_query, w_key_up, w_value_up, w_output):
    yh, z, x, c, yl = (lax.axis_index(a) for a in AXES)
    slab = 8 * yh + z
    own, given = quarters(w_output.reshape(64, 7168))
    other = xor_y(given, 3)
    u1, d1 = up_z(own), down_z(own)

    own_keys = key_rows.T
    half = lax.dynamic_slice_in_dim(own_keys, 128 * c, 128, 1)
    near, far = (
        lax.ppermute(half, CTX, [(i, i + by) for i in range(16 - by)]) for by in (1, 2)
    )
    cosines, sines, all_cosines, all_sines = turns(slab * 256)
    queries = call(
        queries_kernel,
        [array((1024, 640))] * 2,
        kept(2) + whole(3),
        (query_latent, w_query, w_key_up, cosines, sines),
        "queries",
        2 * 256 * 1536 * 1536 + 2 * 2048 * 128 * 512,
        8 << 20,
        60,
        [
            pltpu.VMEM((2, 1536, 768), BF),
            pltpu.VMEM((256, 1536), BF),
            pltpu.SemaphoreType.DMA((3,)),
        ],
    )
    swapped = other_core(jnp.concatenate([near, far], 1))
    u2 = up_z(after(jnp.concatenate([u1, other], 0), queries[0]))
    d2 = down_z(after(jnp.concatenate([d1, other], 0), queries[0]))

    keys, hidden = call(
        keys_kernel,
        [array((640, 768)), array((256, 768), F32)],
        scalars() + kept() + placed(3) + kept() + whole(2),
        (prompt_start, own_keys, near, far, swapped, key_cache.T, all_cosines, all_sines),
        "keys",
        768 * 640 * 8,
        4 << 20,
        8,
        [pltpu.VMEM((576, 768), BF), pltpu.SemaphoreType.DMA((5,))],
    )
    column = jnp.arange(512, dtype=jnp.int32)
    source = (
        (column // 8 % 4) * 128 + (column // 256) * 64 + ((z + column // 32) % 8) * 8 + column % 8
    )
    reorder = (column[:, None] == source[None, :]).astype(BF)
    rows = call(
        attend_kernel,
        array((256, 1024)),
        whole(6),
        (*queries, keys, hidden, w_value_up, reorder),
        "attend",
        4 * 1024 * 768 * 1152 + 4 * 1024 * 512 * 128,
        10 << 20,
        16,
    )
    one, three = xor_y(rows, 1), xor_y(rows, 3)
    groups = [rows, one, xor_y(one[:128], 3), xor_y(three[128:], 1), three]
    u3, d3 = up_z(after(u2, rows)), down_z(after(d2, rows))
    u4 = up_z(u3)
    e3 = down_z(d3[64:])
    e4 = down_z(e3)
    blocks = [own, d1, d2, d3, u4, u3, u2, u1, other, e3, e4]

    first, rest = project(1, groups, blocks, BF)
    first, rest = other_core(first), other_core(rest)
    mine, mine_rest = project(0, groups, blocks, F32)
    sums = [mine_rest[i] + rest[i].astype(F32) for i in range(3)]
    early_up, early_down, first, mine = lax.optimization_barrier(
        (sums[1][128:].astype(BF), sums[2][:128].astype(BF), first, mine)
    )
    far_sum = (mine + first.astype(F32)).astype(BF)
    passing_up = along_x(far_sum[:128], 1)
    passing_down = along_x(far_sum[128:], 3)
    early_up, early_down = along_x(early_up, 1), along_x(early_down, 3)
    late_up = home((sums[1][:128] + passing_up.astype(F32)).astype(BF), 0, 1)
    late_down = home((sums[2][128:] + passing_down.astype(F32)).astype(BF), 1, 3)
    parts = [
        [home((sums[0][:128] + early_down.astype(F32)).astype(BF), 0), late_up],
        [home((sums[0][128:] + early_up.astype(F32)).astype(BF), 1), late_down],
    ]
    pieces = [sum(part.astype(F32) for part in piece).astype(BF) for piece in parts]
    even = yl == 0
    pair = jnp.where(even, pieces[0], pieces[1]), jnp.where(even, pieces[1], pieces[0])
    return jnp.concatenate(
        [jnp.concatenate([p[:, 448 * i : 448 * i + 448] for p in pair], 1) for i in range(2)], 0
    )


def solution(mesh):
    cut = Mesh(mesh.devices.reshape(SIZES), AXES) if hasattr(mesh, "devices") else mesh
    tokens = ("yl", "yh", "z")
    return jax.shard_map(
        local,
        mesh=cut,
        in_specs=(
            P(tokens, None),
            P(tokens, None),
            P("yl", None),
            P("yl"),
            P(None, HEAD),
            P(HEAD, None, None),
            P(HEAD, None, None),
            P(HEAD, CTX, None),
        ),
        out_specs=P(tokens, HEAD),
        check_vma=False,
    )
```

```python
import functools

import jax
import jax.numpy as jnp
from jax import lax
from jax.experimental import pallas as pl
from jax.experimental.pallas import tpu as pltpu
from jax.sharding import Mesh
from jax.sharding import PartitionSpec as P

AXES = ("yh", "z", "x", "c", "yl")
SIZES = (2, 8, 4, 2, 2)
CTX = ("yh", "z")
HEAD = ("x", "c")
BF = jnp.bfloat16
F32 = jnp.float32
VMEM = pltpu.MemorySpace.VMEM


def number_of(yh, z, x, c, yl):
    return (((yh * 8 + z) * 4 + x) * 2 + c) * 2 + yl


def moved(a, target):
    pairs = []
    for yh in range(2):
        for z in range(8):
            for x in range(4):
                for c in range(2):
                    for yl in range(2):
                        t = target(yh, z, x, c, yl)
                        pairs.append((number_of(yh, z, x, c, yl), number_of(*t)))
    return lax.ppermute(a, AXES, pairs)


def up_z(a):
    return moved(a, lambda yh, z, x, c, yl: (yh, (z + 1) % 8, x, c, yl))


def down_z(a):
    return moved(a, lambda yh, z, x, c, yl: (yh, (z - 1) % 8, x, c, yl))


def xor_y(a, q):
    return moved(a, lambda yh, z, x, c, yl: (yh ^ (q >> 1), z, x, c, yl ^ (q & 1)))


def other_core(a):
    return moved(a, lambda yh, z, x, c, yl: (yh, z, x, 1 - c, yl))


def along_x(a, d):
    return moved(a, lambda yh, z, x, c, yl: (yh, z, (x + d) % 4, c, yl))


def home(a, r, d=0):
    return moved(a, lambda yh, z, x, c, yl: (yh ^ c, z, (x + d) % 4, yh, yl ^ r))


def turn_of(table):
    return jnp.concatenate([table[:, 32 * i : 32 * i + 32] for i in range(4)], 0)


def turned(rot, cosine, sine):
    other = jnp.concatenate([rot[:, 32:], rot[:, :32]], 1)
    cosine = jnp.concatenate([cosine, cosine], 1)
    sine = jnp.concatenate([-sine, sine], 1)
    rot = rot * cosine + other * sine
    return jnp.concatenate([rot, jnp.zeros_like(rot)], 1).astype(BF)


def queries_kernel(rows, w_query, w_key_up, cosines, sines, out, out_next, held, rows_held, sem):
    copies = [
        pltpu.make_async_copy(w_query.at[:, pl.ds(768 * part, 768)], held.at[part], sem.at[part])
        for part in range(2)
    ]
    copies.append(pltpu.make_async_copy(rows, rows_held, sem.at[2]))
    for i in (2, 0, 1):
        copies[i].start()
    cosine, sine = turn_of(cosines), turn_of(sines)
    copies[2].wait()
    for part in range(2):
        copies[part].wait()
        queries = jnp.dot(rows_held[...], held[part], preferred_element_type=F32).astype(BF)
        for i in range(4):
            h = 4 * part + i
            plain = queries[:, 192 * i : 192 * i + 128]
            lat = jnp.dot(plain, w_key_up[h], preferred_element_type=F32)
            rot = queries[:, 192 * i + 128 : 192 * i + 192].astype(F32)
            tokens = slice(256 * i, 256 * i + 256)
            to = out_next if part else out
            to[tokens, :512] = lat.astype(BF)
            to[tokens, 512:] = turned(rot, cosine, sine)


def keys_kernel(start, own, near, far, swapped, cache, cosines, sines, keys, hidden, raw, sem):
    c = lax.axis_index("c")
    slab = 8 * lax.axis_index("yh") + lax.axis_index("z")

    def at(column, columns):
        return raw.at[:, pl.ds(pl.multiple_of(column, 128), columns)]

    copies = [
        pltpu.make_async_copy(own, at(512, 256), sem.at[0]),
        pltpu.make_async_copy(near, at(256 + 128 * c, 128), sem.at[1]),
        pltpu.make_async_copy(swapped.at[:, pl.ds(0, 128)], at(384 - 128 * c, 128), sem.at[2]),
        pltpu.make_async_copy(far, at(128 * c, 128), sem.at[3]),
        pltpu.make_async_copy(swapped.at[:, pl.ds(128, 128)], at(128 - 128 * c, 128), sem.at[4]),
    ]
    for copy in copies:
        copy.start()
    row = lax.broadcasted_iota(jnp.int32, (256, 768), 0)
    col = lax.broadcasted_iota(jnp.int32, (256, 768), 1)
    relative = col - 512 - row
    visible = (relative <= 0) & (relative > -512) & (slab * 256 + col - 512 >= -start[0])
    hidden[...] = jnp.where(visible, 0.0, -1e30)
    for copy in copies:
        copy.wait()
    low, high = raw[512:544, :].astype(F32), raw[544:, :].astype(F32)
    cosine, sine = cosines[...], sines[...]
    keys[:512, :] = raw[:512, :]
    keys[512:544, :] = (low * cosine - high * sine).astype(BF)
    keys[544:576, :] = (low * sine + high * cosine).astype(BF)
    keys[576:, :] = jnp.zeros((64, 768), BF)

    @pl.when(slab < 2)
    def _():
        copy = pltpu.make_async_copy(cache, at(0, 512), sem.at[0])
        copy.start()
        copy.wait()

    @pl.when(slab == 0)
    def _():
        keys[:576, :512] = raw[:, :512]

    @pl.when(slab == 1)
    def _():
        keys[:576, :256] = raw[:, 256:512]


def attend_kernel(group, queries, keys, hidden, w_value_up, reorder, out):
    scale = 192.0**-0.5 * 1.4426950408889634
    heads = []
    for pair in range(2):
        scores = jnp.dot(
            queries[512 * pair : 512 * pair + 512, :], keys[...], preferred_element_type=F32
        )
        for i in range(2):
            part = scores[256 * i : 256 * i + 256] * scale + hidden[...]
            top = jnp.max(part, axis=1, keepdims=True)
            powers = jnp.exp2(part - top)
            share = 1.0 / jnp.sum(powers, axis=1, keepdims=True)
            mixed = lax.dot_general(
                powers.astype(BF),
                keys[:512, :],
                (((1,), (1,)), ((), ())),
                preferred_element_type=F32,
            )
            attention = jnp.dot(
                (mixed * share).astype(BF),
                w_value_up[4 * group + 2 * pair + i],
                preferred_element_type=F32,
            )
            heads.append(attention.astype(BF))
    rows = jnp.concatenate(heads, 1)
    out[...] = jnp.dot(rows, reorder[...], preferred_element_type=F32).astype(BF)


def turns(first):
    inverse = jnp.power(jnp.float32(10000.0), -jnp.arange(32, dtype=F32) * (2.0 / 64))
    row = lax.broadcasted_iota(jnp.int32, (64, 128), 0)
    lane = lax.broadcasted_iota(jnp.int32, (64, 128), 1)
    own = (first + (lane // 32) * 64 + row).astype(F32) * jnp.tile(inverse, 4)[None, :]
    place = first - 512 + lax.broadcasted_iota(jnp.int32, (32, 768), 1)
    every = place.astype(F32) * inverse[:, None]
    return jnp.cos(own), jnp.sin(own), jnp.cos(every), jnp.sin(every)


def quarter_kernel(rows, own, other):
    x = lax.axis_index("x")
    for out, flip in ((own, 0), (other, 1)):
        odd = lax.axis_index("yl") ^ flip
        base = 896 * (lax.axis_index("yh") ^ flip) + 384 * odd
        pieces = []
        for d in range(4):
            start = pl.multiple_of(1792 * ((x + d) % 4) + base, 128)
            wide = rows[:, pl.ds(start, 512)]
            pieces.append(jnp.where(odd == 1, wide[:, 64:], wide[:, :448]))
        out[...] = jnp.concatenate(pieces, 1)


def project_kernel(theirs, *refs):
    groups, held, outs, (rows, total) = refs[:8], refs[8:19], refs[19:-2], refs[-2:]
    own, d1, d2, d3, u4, u3, u2, u1, other, e3, e4 = held
    blocks = [own, d1, *(both.at[:64] for both in (d2, d3, u4, u3, u2)), u1]
    blocks += [other, d2.at[64:], d3.at[64:], e3, e4, *(both.at[64:] for both in (u4, u3, u2))]
    first = 2 * (lax.axis_index("c") ^ theirs)
    yh = lax.axis_index("yh")
    for pick in (0, 2):

        @pl.when(first == pick)
        def _():
            for g in range(2):
                for j in range(2):
                    for p in range(2):
                        half = pl.ds(pl.multiple_of(256 * (yh ^ p), 256), 256)
                        rows[256 * j : 256 * j + 256, 512 * g + 256 * p : 512 * g + 256 * p + 256] = (
                            groups[2 * (pick + j) + g][:, half]
                        )

    for n in range(7):
        columns = slice(256 * n, 256 * n + 256)
        weights = jnp.concatenate(
            [
                block[32 * g : 32 * g + 32, columns]
                for g in range(2)
                for block in blocks
            ],
            0,
        )
        total[:, columns] = jnp.dot(rows[...], weights, preferred_element_type=F32)
    for out, d in zip((outs[0], *(outs[1].at[i] for i in range(3))), (2, 0, 1, 3)):
        span = slice(448 * d, 448 * d + 448)
        for j in range(2):
            top = total[256 * j : 256 * j + 128, span]
            low = total[256 * j + 128 : 256 * j + 256, span]
            out[128 * j : 128 * j + 128, :] = jnp.concatenate([top, low], 1).astype(out.dtype)


def whole(n):
    return [pl.BlockSpec(memory_space=VMEM)] * n


def placed(n):
    return [pl.BlockSpec(memory_space=pl.ANY)] * n


def kept(n=1):
    return [pl.BlockSpec(memory_space=pltpu.MemorySpace.HBM)] * n


def scalars(n=1):
    return [pl.BlockSpec(memory_space=pltpu.MemorySpace.SMEM)] * n


def quarters(rows):
    return pl.pallas_call(
        quarter_kernel,
        out_shape=[jax.ShapeDtypeStruct((64, 1792), BF)] * 2,
        in_specs=whole(1),
        out_specs=whole(2),
        name="quarters",
        cost_estimate=pl.CostEstimate(flops=0, bytes_accessed=2 << 20, transcendentals=0),
    )(rows)


def call(kernel, shapes, specs, args, name, flops, moved_bytes, room, scratch=()):
    many = isinstance(shapes, list)
    return pl.pallas_call(
        kernel,
        out_shape=shapes,
        in_specs=specs,
        out_specs=whole(len(shapes)) if many else whole(1)[0],
        scratch_shapes=list(scratch),
        compiler_params=pltpu.CompilerParams(vmem_limit_bytes=room << 20),
        name=name,
        cost_estimate=pl.CostEstimate(
            flops=flops, bytes_accessed=moved_bytes, transcendentals=0
        ),
    )(*args)


def array(shape, kind=BF):
    return jax.ShapeDtypeStruct(shape, kind)


def after(value, *others):
    return lax.optimization_barrier((value, *others))[0]


def project(theirs, groups, blocks, kind):
    return call(
        functools.partial(project_kernel, theirs),
        [array((256, 896), kind), array((3, 256, 896), kind)],
        whole(19),
        (*groups, *blocks),
        "project",
        2 * 512 * 1024 * 1792,
        8 << 20,
        12,
        [pltpu.VMEM((512, 1024), BF), pltpu.VMEM((512, 1792), F32)],
    )


def local(query_latent, key_rows, key_cache, prompt_start, w_query, w_key_up, w_value_up, w_output):
    yh, z, x, c, yl = (lax.axis_index(a) for a in AXES)
    slab = 8 * yh + z
    own, given = quarters(w_output.reshape(64, 7168))
    other = xor_y(given, 3)
    u1, d1 = up_z(own), down_z(own)

    own_keys = key_rows.T
    half = lax.dynamic_slice_in_dim(own_keys, 128 * c, 128, 1)
    near, far = (
        lax.ppermute(half, CTX, [(i, (i + by) % 16) for i in range(16)]) for by in (1, 2)
    )
    cosines, sines, all_cosines, all_sines = turns(slab * 256)
    queries = call(
        queries_kernel,
        [array((1024, 640))] * 2,
        kept(2) + whole(3),
        (query_latent, w_query, w_key_up, cosines, sines),
        "queries",
        2 * 256 * 1536 * 1536 + 2 * 2048 * 128 * 512,
        8 << 20,
        60,
        [
            pltpu.VMEM((2, 1536, 768), BF),
            pltpu.VMEM((256, 1536), BF),
            pltpu.SemaphoreType.DMA((3,)),
        ],
    )
    swapped = other_core(jnp.concatenate([near, far], 1))
    u2 = up_z(after(jnp.concatenate([u1, other], 0), queries[0]))
    d2 = down_z(after(jnp.concatenate([d1, other], 0), queries[0]))

    keys, hidden = call(
        keys_kernel,
        [array((640, 768)), array((256, 768), F32)],
        scalars() + kept() + placed(3) + kept() + whole(2),
        (prompt_start, own_keys, near, far, swapped, key_cache.T, all_cosines, all_sines),
        "keys",
        768 * 640 * 8,
        4 << 20,
        8,
        [pltpu.VMEM((576, 768), BF), pltpu.SemaphoreType.DMA((5,))],
    )
    column = jnp.arange(512, dtype=jnp.int32)
    source = (
        (column // 8 % 4) * 128 + (column // 256) * 64 + ((z + column // 32) % 8) * 8 + column % 8
    )
    reorder = (column[:, None] == source[None, :]).astype(BF)
    rows = [
        call(
            functools.partial(attend_kernel, g),
            array((256, 512)),
            whole(5),
            (queries[g], keys, hidden, w_value_up, reorder),
            "attend",
            2 * 1024 * 768 * 1152 + 2 * 1024 * 512 * 128,
            5 << 20,
            14,
        )
        for g in range(2)
    ]
    one = [xor_y(part, 1) for part in rows]
    three = [xor_y(part, 3) for part in rows]
    two = [xor_y(one[0], 3), xor_y(three[1], 1)]
    groups = [*rows, *one, *two, *three]
    u3, d3 = up_z(after(u2, *rows)), down_z(after(d2, *rows))
    u4 = up_z(u3)
    e3 = down_z(d3[64:])
    e4 = down_z(e3)
    blocks = [own, d1, d2, d3, u4, u3, u2, u1, other, e3, e4]

    first, rest = project(1, groups, blocks, BF)
    first, rest = other_core(first), other_core(rest)
    mine, mine_rest = project(0, groups, blocks, F32)
    sums = [mine_rest[i] + rest[i].astype(F32) for i in range(3)]
    early_up, early_down, first, mine = lax.optimization_barrier(
        (sums[1][128:].astype(BF), sums[2][:128].astype(BF), first, mine)
    )
    far_sum = (mine + first.astype(F32)).astype(BF)
    passing_up = along_x(far_sum[:128], 1)
    passing_down = along_x(far_sum[128:], 3)
    early_up, early_down = along_x(early_up, 1), along_x(early_down, 3)
    late_up = home((sums[1][:128] + passing_up.astype(F32)).astype(BF), 0, 1)
    late_down = home((sums[2][128:] + passing_down.astype(F32)).astype(BF), 1, 3)
    parts = [
        [home((sums[0][:128] + early_down.astype(F32)).astype(BF), 0), late_up],
        [home((sums[0][128:] + early_up.astype(F32)).astype(BF), 1), late_down],
    ]
    pieces = [sum(part.astype(F32) for part in piece).astype(BF) for piece in parts]
    even = yl == 0
    pair = jnp.where(even, pieces[0], pieces[1]), jnp.where(even, pieces[1], pieces[0])
    return jnp.concatenate(
        [jnp.concatenate([p[:, 448 * i : 448 * i + 448] for p in pair], 1) for i in range(2)], 0
    )


def solution(mesh):
    cut = Mesh(mesh.devices.reshape(SIZES), AXES) if hasattr(mesh, "devices") else mesh
    tokens = ("yl", "yh", "z")
    return jax.shard_map(
        local,
        mesh=cut,
        in_specs=(
            P(tokens, None),
            P(tokens, None),
            P("yl", None),
            P("yl"),
            P(None, HEAD),
            P(HEAD, None, None),
            P(HEAD, None, None),
            P(HEAD, CTX, None),
        ),
        out_specs=P(tokens, HEAD),
        check_vma=False,
    )
```

```python
import functools

import jax
import jax.numpy as jnp
from jax import lax
from jax.experimental import pallas as pl
from jax.experimental.pallas import tpu as pltpu
from jax.sharding import Mesh
from jax.sharding import PartitionSpec as P

AXES = ("yh", "z", "x", "c", "yl")
SIZES = (2, 8, 4, 2, 2)
CTX = ("yh", "z")
HEAD = ("x", "c")
BF = jnp.bfloat16
F32 = jnp.float32
VMEM = pltpu.MemorySpace.VMEM


def number_of(yh, z, x, c, yl):
    return (((yh * 8 + z) * 4 + x) * 2 + c) * 2 + yl


def moved(a, target):
    pairs = []
    for yh in range(2):
        for z in range(8):
            for x in range(4):
                for c in range(2):
                    for yl in range(2):
                        t = target(yh, z, x, c, yl)
                        pairs.append((number_of(yh, z, x, c, yl), number_of(*t)))
    return lax.ppermute(a, AXES, pairs)


def up_z(a):
    return moved(a, lambda yh, z, x, c, yl: (yh, (z + 1) % 8, x, c, yl))


def down_z(a):
    return moved(a, lambda yh, z, x, c, yl: (yh, (z - 1) % 8, x, c, yl))


def xor_y(a, q):
    return moved(a, lambda yh, z, x, c, yl: (yh ^ (q >> 1), z, x, c, yl ^ (q & 1)))


def other_core(a):
    return moved(a, lambda yh, z, x, c, yl: (yh, z, x, 1 - c, yl))


def along_x(a, d):
    return moved(a, lambda yh, z, x, c, yl: (yh, z, (x + d) % 4, c, yl))


def home(a, r, d=0):
    return moved(a, lambda yh, z, x, c, yl: (yh ^ c, z, (x + d) % 4, yh, yl ^ r))


def turn_of(table):
    return jnp.concatenate([table[:, 32 * i : 32 * i + 32] for i in range(4)], 0)


def turned(rot, cosine, sine):
    other = jnp.concatenate([rot[:, 32:], rot[:, :32]], 1)
    cosine = jnp.concatenate([cosine, cosine], 1)
    sine = jnp.concatenate([-sine, sine], 1)
    rot = rot * cosine + other * sine
    return jnp.concatenate([rot, jnp.zeros_like(rot)], 1).astype(BF)


def queries_kernel(rows, w_query, w_key_up, cosines, sines, out, out_next, held, rows_held, sem):
    copies = [
        pltpu.make_async_copy(w_query.at[:, pl.ds(768 * part, 768)], held.at[part], sem.at[part])
        for part in range(2)
    ]
    copies.append(pltpu.make_async_copy(rows, rows_held, sem.at[2]))
    for i in (2, 0, 1):
        copies[i].start()
    cosine, sine = turn_of(cosines), turn_of(sines)
    copies[2].wait()
    for part in range(2):
        copies[part].wait()
        queries = jnp.dot(rows_held[...], held[part], preferred_element_type=F32).astype(BF)
        for i in range(4):
            h = 4 * part + i
            plain = queries[:, 192 * i : 192 * i + 128]
            lat = jnp.dot(plain, w_key_up[h], preferred_element_type=F32)
            rot = queries[:, 192 * i + 128 : 192 * i + 192].astype(F32)
            tokens = slice(256 * i, 256 * i + 256)
            to = out_next if part else out
            to[tokens, :512] = lat.astype(BF)
            to[tokens, 512:] = turned(rot, cosine, sine)


def keys_kernel(start, own, near, far, swapped, cache, cosines, sines, keys, hidden, raw, sem):
    c = lax.axis_index("c")
    slab = 8 * lax.axis_index("yh") + lax.axis_index("z")

    def at(column, columns):
        return raw.at[:, pl.ds(pl.multiple_of(column, 128), columns)]

    copies = [
        pltpu.make_async_copy(own, at(512, 256), sem.at[0]),
        pltpu.make_async_copy(near, at(256 + 128 * c, 128), sem.at[1]),
        pltpu.make_async_copy(swapped.at[:, pl.ds(0, 128)], at(384 - 128 * c, 128), sem.at[2]),
        pltpu.make_async_copy(far, at(128 * c, 128), sem.at[3]),
        pltpu.make_async_copy(swapped.at[:, pl.ds(128, 128)], at(128 - 128 * c, 128), sem.at[4]),
    ]
    for copy in copies:
        copy.start()
    row = lax.broadcasted_iota(jnp.int32, (256, 768), 0)
    col = lax.broadcasted_iota(jnp.int32, (256, 768), 1)
    relative = col - 512 - row
    visible = (relative <= 0) & (relative > -512) & (slab * 256 + col - 512 >= -start[0])
    hidden[...] = jnp.where(visible, 0.0, -1e30)
    for copy in copies:
        copy.wait()
    low, high = raw[512:544, :].astype(F32), raw[544:, :].astype(F32)
    cosine, sine = cosines[...], sines[...]
    keys[:512, :] = raw[:512, :]
    keys[512:544, :] = (low * cosine - high * sine).astype(BF)
    keys[544:576, :] = (low * sine + high * cosine).astype(BF)
    keys[576:, :] = jnp.zeros((64, 768), BF)

    @pl.when(slab < 2)
    def _():
        copy = pltpu.make_async_copy(cache, at(0, 512), sem.at[0])
        copy.start()
        copy.wait()

    @pl.when(slab == 0)
    def _():
        keys[:576, :512] = raw[:, :512]

    @pl.when(slab == 1)
    def _():
        keys[:576, :256] = raw[:, 256:512]


def attend_kernel(queries, queries_next, keys, hidden, w_value_up, reorder, out):
    scale = 192.0**-0.5 * 1.4426950408889634
    for group, held in enumerate((queries, queries_next)):
        heads = []
        for pair in range(2):
            scores = jnp.dot(
                held[512 * pair : 512 * pair + 512, :], keys[...], preferred_element_type=F32
            )
            for i in range(2):
                part = scores[256 * i : 256 * i + 256] * scale + hidden[...]
                top = jnp.max(part, axis=1, keepdims=True)
                powers = jnp.exp2(part - top)
                share = 1.0 / jnp.sum(powers, axis=1, keepdims=True)
                mixed = lax.dot_general(
                    powers.astype(BF),
                    keys[:512, :],
                    (((1,), (1,)), ((), ())),
                    preferred_element_type=F32,
                )
                attention = jnp.dot(
                    (mixed * share).astype(BF),
                    w_value_up[4 * group + 2 * pair + i],
                    preferred_element_type=F32,
                )
                heads.append(attention.astype(BF))
        rows = jnp.concatenate(heads, 1)
        out[:, 512 * group : 512 * group + 512] = jnp.dot(
            rows, reorder[...], preferred_element_type=F32
        ).astype(BF)


def turns(first):
    inverse = jnp.power(jnp.float32(10000.0), -jnp.arange(32, dtype=F32) * (2.0 / 64))
    row = lax.broadcasted_iota(jnp.int32, (64, 128), 0)
    lane = lax.broadcasted_iota(jnp.int32, (64, 128), 1)
    own = (first + (lane // 32) * 64 + row).astype(F32) * jnp.tile(inverse, 4)[None, :]
    place = first - 512 + lax.broadcasted_iota(jnp.int32, (32, 768), 1)
    every = place.astype(F32) * inverse[:, None]
    return jnp.cos(own), jnp.sin(own), jnp.cos(every), jnp.sin(every)


def quarter_kernel(rows, own, other):
    x = lax.axis_index("x")
    for out, flip in ((own, 0), (other, 1)):
        odd = lax.axis_index("yl") ^ flip
        base = 896 * (lax.axis_index("yh") ^ flip) + 384 * odd
        pieces = []
        for d in range(4):
            start = pl.multiple_of(1792 * ((x + d) % 4) + base, 128)
            wide = rows[:, pl.ds(start, 512)]
            pieces.append(jnp.where(odd == 1, wide[:, 64:], wide[:, :448]))
        out[...] = jnp.concatenate(pieces, 1)


def project_kernel(theirs, *refs):
    groups, held, outs, (rows, total) = refs[:5], refs[5:16], refs[16:-2], refs[-2:]
    own, d1, d2, d3, u4, u3, u2, u1, other, e3, e4 = held
    blocks = [own, d1, *(both.at[:64] for both in (d2, d3, u4, u3, u2)), u1]
    blocks += [other, d2.at[64:], d3.at[64:], e3, e4, *(both.at[64:] for both in (u4, u3, u2))]
    first = 2 * (lax.axis_index("c") ^ theirs)
    yh = lax.axis_index("yh")
    for pick in (0, 2):

        @pl.when(first == pick)
        def _():
            at = 0
            for part in groups[2:] if pick else groups[:2]:
                for g in range(2):
                    for p in range(2):
                        half = pl.ds(pl.multiple_of(512 * g + 256 * (yh ^ p), 256), 256)
                        to = 512 * g + 256 * p
                        rows[at : at + part.shape[0], to : to + 256] = part[:, half]
                at += part.shape[0]

    for n in range(7):
        columns = slice(256 * n, 256 * n + 256)
        weights = jnp.concatenate(
            [
                block[32 * g : 32 * g + 32, columns]
                for g in range(2)
                for block in blocks
            ],
            0,
        )
        total[:, columns] = jnp.dot(rows[...], weights, preferred_element_type=F32)
    for out, d in zip((outs[0], *(outs[1].at[i] for i in range(3))), (2, 0, 1, 3)):
        span = slice(448 * d, 448 * d + 448)
        for j in range(2):
            top = total[256 * j : 256 * j + 128, span]
            low = total[256 * j + 128 : 256 * j + 256, span]
            out[128 * j : 128 * j + 128, :] = jnp.concatenate([top, low], 1).astype(out.dtype)


def whole(n):
    return [pl.BlockSpec(memory_space=VMEM)] * n


def placed(n):
    return [pl.BlockSpec(memory_space=pl.ANY)] * n


def kept(n=1):
    return [pl.BlockSpec(memory_space=pltpu.MemorySpace.HBM)] * n


def scalars(n=1):
    return [pl.BlockSpec(memory_space=pltpu.MemorySpace.SMEM)] * n


def quarters(rows):
    return pl.pallas_call(
        quarter_kernel,
        out_shape=[jax.ShapeDtypeStruct((64, 1792), BF)] * 2,
        in_specs=whole(1),
        out_specs=whole(2),
        name="quarters",
        cost_estimate=pl.CostEstimate(flops=0, bytes_accessed=2 << 20, transcendentals=0),
    )(rows)


def call(kernel, shapes, specs, args, name, flops, moved_bytes, room, scratch=()):
    many = isinstance(shapes, list)
    return pl.pallas_call(
        kernel,
        out_shape=shapes,
        in_specs=specs,
        out_specs=whole(len(shapes)) if many else whole(1)[0],
        scratch_shapes=list(scratch),
        compiler_params=pltpu.CompilerParams(vmem_limit_bytes=room << 20),
        name=name,
        cost_estimate=pl.CostEstimate(
            flops=flops, bytes_accessed=moved_bytes, transcendentals=0
        ),
    )(*args)


def array(shape, kind=BF):
    return jax.ShapeDtypeStruct(shape, kind)


def after(value, *others):
    return lax.optimization_barrier((value, *others))[0]


def project(theirs, groups, blocks, kind):
    return call(
        functools.partial(project_kernel, theirs),
        [array((256, 896), kind), array((3, 256, 896), kind)],
        whole(16),
        (*groups, *blocks),
        "project",
        2 * 512 * 1024 * 1792,
        8 << 20,
        12,
        [pltpu.VMEM((512, 1024), BF), pltpu.VMEM((512, 1792), F32)],
    )


def local(query_latent, key_rows, key_cache, prompt_start, w_query, w_key_up, w_value_up, w_output):
    yh, z, x, c, yl = (lax.axis_index(a) for a in AXES)
    slab = 8 * yh + z
    own, given = quarters(w_output.reshape(64, 7168))
    other = xor_y(given, 3)
    u1, d1 = up_z(own), down_z(own)

    own_keys = key_rows.T
    half = lax.dynamic_slice_in_dim(own_keys, 128 * c, 128, 1)
    near, far = (
        lax.ppermute(half, CTX, [(i, (i + by) % 16) for i in range(16)]) for by in (1, 2)
    )
    cosines, sines, all_cosines, all_sines = turns(slab * 256)
    queries = call(
        queries_kernel,
        [array((1024, 640))] * 2,
        kept(2) + whole(3),
        (query_latent, w_query, w_key_up, cosines, sines),
        "queries",
        2 * 256 * 1536 * 1536 + 2 * 2048 * 128 * 512,
        8 << 20,
        60,
        [
            pltpu.VMEM((2, 1536, 768), BF),
            pltpu.VMEM((256, 1536), BF),
            pltpu.SemaphoreType.DMA((3,)),
        ],
    )
    swapped = other_core(jnp.concatenate([near, far], 1))
    u2 = up_z(after(jnp.concatenate([u1, other], 0), queries[0]))
    d2 = down_z(after(jnp.concatenate([d1, other], 0), queries[0]))

    keys, hidden = call(
        keys_kernel,
        [array((640, 768)), array((256, 768), F32)],
        scalars() + kept() + placed(3) + kept() + whole(2),
        (prompt_start, own_keys, near, far, swapped, key_cache.T, all_cosines, all_sines),
        "keys",
        768 * 640 * 8,
        4 << 20,
        8,
        [pltpu.VMEM((576, 768), BF), pltpu.SemaphoreType.DMA((5,))],
    )
    column = jnp.arange(512, dtype=jnp.int32)
    source = (
        (column // 8 % 4) * 128 + (column // 256) * 64 + ((z + column // 32) % 8) * 8 + column % 8
    )
    reorder = (column[:, None] == source[None, :]).astype(BF)
    rows = call(
        attend_kernel,
        array((256, 1024)),
        whole(6),
        (*queries, keys, hidden, w_value_up, reorder),
        "attend",
        4 * 1024 * 768 * 1152 + 4 * 1024 * 512 * 128,
        10 << 20,
        16,
    )
    one, three = xor_y(rows, 1), xor_y(rows, 3)
    groups = [rows, one, xor_y(one[:128], 3), xor_y(three[128:], 1), three]
    u3, d3 = up_z(after(u2, rows)), down_z(after(d2, rows))
    u4 = up_z(u3)
    e3 = down_z(d3[64:])
    e4 = down_z(e3)
    blocks = [own, d1, d2, d3, u4, u3, u2, u1, other, e3, e4]

    first, rest = project(1, groups, blocks, BF)
    first, rest = other_core(first), other_core(rest)
    mine, mine_rest = project(0, groups, blocks, F32)
    sums = [mine_rest[i] + rest[i].astype(F32) for i in range(3)]
    early_up, early_down, first, mine = lax.optimization_barrier(
        (sums[1][128:].astype(BF), sums[2][:128].astype(BF), first, mine)
    )
    far_sum = (mine + first.astype(F32)).astype(BF)
    passing_up = along_x(far_sum[:128], 1)
    passing_down = along_x(far_sum[128:], 3)
    early_up, early_down = along_x(early_up, 1), along_x(early_down, 3)
    late_up = home((sums[1][:128] + passing_up.astype(F32)).astype(BF), 0, 1)
    late_down = home((sums[2][128:] + passing_down.astype(F32)).astype(BF), 1, 3)
    parts = [
        [home((sums[0][:128] + early_down.astype(F32)).astype(BF), 0), late_up],
        [home((sums[0][128:] + early_up.astype(F32)).astype(BF), 1), late_down],
    ]
    pieces = [sum(part.astype(F32) for part in piece).astype(BF) for piece in parts]
    even = yl == 0
    pair = jnp.where(even, pieces[0], pieces[1]), jnp.where(even, pieces[1], pieces[0])
    return jnp.concatenate(
        [jnp.concatenate([p[:, 448 * i : 448 * i + 448] for p in pair], 1) for i in range(2)], 0
    )


def solution(mesh):
    cut = Mesh(mesh.devices.reshape(SIZES), AXES) if hasattr(mesh, "devices") else mesh
    tokens = ("yl", "yh", "z")
    return jax.shard_map(
        local,
        mesh=cut,
        in_specs=(
            P(tokens, None),
            P(tokens, None),
            P("yl", None),
            P("yl"),
            P(None, HEAD),
            P(HEAD, None, None),
            P(HEAD, None, None),
            P(HEAD, CTX, None),
        ),
        out_specs=P(tokens, HEAD),
        check_vma=False,
    )
```

```python
import functools

import jax
import jax.numpy as jnp
from jax import lax
from jax.experimental import pallas as pl
from jax.experimental.pallas import tpu as pltpu
from jax.sharding import Mesh
from jax.sharding import PartitionSpec as P

AXES = ("yh", "z", "x", "c", "yl")
SIZES = (2, 8, 4, 2, 2)
CTX = ("yh", "z")
HEAD = ("x", "c")
BF = jnp.bfloat16
F32 = jnp.float32
VMEM = pltpu.MemorySpace.VMEM


def number_of(yh, z, x, c, yl):
    return (((yh * 8 + z) * 4 + x) * 2 + c) * 2 + yl


def moved(a, target):
    pairs = []
    for yh in range(2):
        for z in range(8):
            for x in range(4):
                for c in range(2):
                    for yl in range(2):
                        t = target(yh, z, x, c, yl)
                        pairs.append((number_of(yh, z, x, c, yl), number_of(*t)))
    return lax.ppermute(a, AXES, pairs)


def up_z(a):
    return moved(a, lambda yh, z, x, c, yl: (yh, (z + 1) % 8, x, c, yl))


def down_z(a):
    return moved(a, lambda yh, z, x, c, yl: (yh, (z - 1) % 8, x, c, yl))


def xor_y(a, q):
    return moved(a, lambda yh, z, x, c, yl: (yh ^ (q >> 1), z, x, c, yl ^ (q & 1)))


def other_core(a):
    return moved(a, lambda yh, z, x, c, yl: (yh, z, x, 1 - c, yl))


def along_x(a, d):
    return moved(a, lambda yh, z, x, c, yl: (yh, z, (x + d) % 4, c, yl))


def home(a, r, d=0):
    return moved(a, lambda yh, z, x, c, yl: (yh ^ c, z, (x + d) % 4, yh, yl ^ r))


def turn_of(table):
    return jnp.concatenate([table[:, 32 * i : 32 * i + 32] for i in range(4)], 0)


def turned(rot, cosine, sine):
    other = jnp.concatenate([rot[:, 32:], rot[:, :32]], 1)
    cosine = jnp.concatenate([cosine, cosine], 1)
    sine = jnp.concatenate([-sine, sine], 1)
    rot = rot * cosine + other * sine
    return jnp.concatenate([rot, jnp.zeros_like(rot)], 1).astype(BF)


def queries_kernel(rows, w_query, w_key_up, cosines, sines, out, out_next, held, rows_held, sem):
    copies = [
        pltpu.make_async_copy(w_query.at[:, pl.ds(768 * part, 768)], held.at[part], sem.at[part])
        for part in range(2)
    ]
    copies.append(pltpu.make_async_copy(rows, rows_held, sem.at[2]))
    for i in (2, 0, 1):
        copies[i].start()
    cosine, sine = turn_of(cosines), turn_of(sines)
    copies[2].wait()
    for part in range(2):
        copies[part].wait()
        queries = jnp.dot(rows_held[...], held[part], preferred_element_type=F32).astype(BF)
        for i in range(4):
            h = 4 * part + i
            plain = queries[:, 192 * i : 192 * i + 128]
            lat = jnp.dot(plain, w_key_up[h], preferred_element_type=F32)
            rot = queries[:, 192 * i + 128 : 192 * i + 192].astype(F32)
            tokens = slice(256 * i, 256 * i + 256)
            to = out_next if part else out
            to[tokens, :512] = lat.astype(BF)
            to[tokens, 512:] = turned(rot, cosine, sine)


def keys_kernel(start, own, near, far, swapped, cache, cosines, sines, keys, hidden, raw, sem):
    c = lax.axis_index("c")
    slab = 8 * lax.axis_index("yh") + lax.axis_index("z")

    def at(column, columns):
        return raw.at[:, pl.ds(pl.multiple_of(column, 128), columns)]

    copies = [
        pltpu.make_async_copy(own, at(512, 256), sem.at[0]),
        pltpu.make_async_copy(near, at(256 + 128 * c, 128), sem.at[1]),
        pltpu.make_async_copy(swapped.at[:, pl.ds(0, 128)], at(384 - 128 * c, 128), sem.at[2]),
        pltpu.make_async_copy(far, at(128 * c, 128), sem.at[3]),
        pltpu.make_async_copy(swapped.at[:, pl.ds(128, 128)], at(128 - 128 * c, 128), sem.at[4]),
    ]
    for copy in copies:
        copy.start()
    row = lax.broadcasted_iota(jnp.int32, (256, 768), 0)
    col = lax.broadcasted_iota(jnp.int32, (256, 768), 1)
    relative = col - 512 - row
    visible = (relative <= 0) & (relative > -512) & (slab * 256 + col - 512 >= -start[0])
    hidden[...] = jnp.where(visible, 0.0, -1e30)
    for copy in copies:
        copy.wait()
    low, high = raw[512:544, :].astype(F32), raw[544:, :].astype(F32)
    cosine, sine = cosines[...], sines[...]
    keys[:512, :] = raw[:512, :]
    keys[512:544, :] = (low * cosine - high * sine).astype(BF)
    keys[544:576, :] = (low * sine + high * cosine).astype(BF)
    keys[576:, :] = jnp.zeros((64, 768), BF)

    @pl.when(slab < 2)
    def _():
        copy = pltpu.make_async_copy(cache, at(0, 512), sem.at[0])
        copy.start()
        copy.wait()

    @pl.when(slab == 0)
    def _():
        keys[:576, :512] = raw[:, :512]

    @pl.when(slab == 1)
    def _():
        keys[:576, :256] = raw[:, 256:512]


def attend_kernel(group, queries, keys, hidden, w_value_up, reorder, out):
    scale = 192.0**-0.5 * 1.4426950408889634
    heads = []
    for pair in range(2):
        scores = jnp.dot(
            queries[512 * pair : 512 * pair + 512, :], keys[...], preferred_element_type=F32
        )
        for i in range(2):
            part = scores[256 * i : 256 * i + 256] * scale + hidden[...]
            top = jnp.max(part, axis=1, keepdims=True)
            powers = jnp.exp2(part - top)
            share = 1.0 / jnp.sum(powers, axis=1, keepdims=True)
            mixed = lax.dot_general(
                powers.astype(BF),
                keys[:512, :],
                (((1,), (1,)), ((), ())),
                preferred_element_type=F32,
            )
            attention = jnp.dot(
                (mixed * share).astype(BF),
                w_value_up[4 * group + 2 * pair + i],
                preferred_element_type=F32,
            )
            heads.append(attention.astype(BF))
    rows = jnp.concatenate(heads, 1)
    out[...] = jnp.dot(rows, reorder[...], preferred_element_type=F32).astype(BF)


def turns(first):
    inverse = jnp.power(jnp.float32(10000.0), -jnp.arange(32, dtype=F32) * (2.0 / 64))
    row = lax.broadcasted_iota(jnp.int32, (64, 128), 0)
    lane = lax.broadcasted_iota(jnp.int32, (64, 128), 1)
    own = (first + (lane // 32) * 64 + row).astype(F32) * jnp.tile(inverse, 4)[None, :]
    place = first - 512 + lax.broadcasted_iota(jnp.int32, (32, 768), 1)
    every = place.astype(F32) * inverse[:, None]
    return jnp.cos(own), jnp.sin(own), jnp.cos(every), jnp.sin(every)


def quarter_kernel(rows, own, other):
    x = lax.axis_index("x")
    for out, flip in ((own, 0), (other, 1)):
        odd = lax.axis_index("yl") ^ flip
        base = 896 * (lax.axis_index("yh") ^ flip) + 384 * odd
        pieces = []
        for d in range(4):
            start = pl.multiple_of(1792 * ((x + d) % 4) + base, 128)
            wide = rows[:, pl.ds(start, 512)]
            pieces.append(jnp.where(odd == 1, wide[:, 64:], wide[:, :448]))
        out[...] = jnp.concatenate(pieces, 1)


def project_kernel(theirs, *refs):
    groups, held, outs, (rows, total) = refs[:8], refs[8:19], refs[19:-2], refs[-2:]
    own, d1, d2, d3, u4, u3, u2, u1, other, e3, e4 = held
    blocks = [own, d1, *(both.at[:64] for both in (d2, d3, u4, u3, u2)), u1]
    blocks += [other, d2.at[64:], d3.at[64:], e3, e4, *(both.at[64:] for both in (u4, u3, u2))]
    first = 2 * (lax.axis_index("c") ^ theirs)
    yh = lax.axis_index("yh")
    for pick in (0, 2):

        @pl.when(first == pick)
        def _():
            for g in range(2):
                for j in range(2):
                    for p in range(2):
                        half = pl.ds(pl.multiple_of(256 * (yh ^ p), 256), 256)
                        rows[256 * j : 256 * j + 256, 512 * g + 256 * p : 512 * g + 256 * p + 256] = (
                            groups[2 * (pick + j) + g][:, half]
                        )

    for n in range(7):
        columns = slice(256 * n, 256 * n + 256)
        weights = jnp.concatenate(
            [
                block[32 * g : 32 * g + 32, columns]
                for g in range(2)
                for block in blocks
            ],
            0,
        )
        total[:, columns] = jnp.dot(rows[...], weights, preferred_element_type=F32)
    for out, d in zip((outs[0], *(outs[1].at[i] for i in range(3))), (2, 0, 1, 3)):
        span = slice(448 * d, 448 * d + 448)
        for j in range(2):
            top = total[256 * j : 256 * j + 128, span]
            low = total[256 * j + 128 : 256 * j + 256, span]
            out[128 * j : 128 * j + 128, :] = jnp.concatenate([top, low], 1).astype(out.dtype)


def whole(n):
    return [pl.BlockSpec(memory_space=VMEM)] * n


def placed(n):
    return [pl.BlockSpec(memory_space=pl.ANY)] * n


def kept(n=1):
    return [pl.BlockSpec(memory_space=pltpu.MemorySpace.HBM)] * n


def scalars(n=1):
    return [pl.BlockSpec(memory_space=pltpu.MemorySpace.SMEM)] * n


def quarters(rows):
    return pl.pallas_call(
        quarter_kernel,
        out_shape=[jax.ShapeDtypeStruct((64, 1792), BF)] * 2,
        in_specs=whole(1),
        out_specs=whole(2),
        name="quarters",
        cost_estimate=pl.CostEstimate(flops=0, bytes_accessed=2 << 20, transcendentals=0),
    )(rows)


def call(kernel, shapes, specs, args, name, flops, moved_bytes, room, scratch=()):
    many = isinstance(shapes, list)
    return pl.pallas_call(
        kernel,
        out_shape=shapes,
        in_specs=specs,
        out_specs=whole(len(shapes)) if many else whole(1)[0],
        scratch_shapes=list(scratch),
        compiler_params=pltpu.CompilerParams(vmem_limit_bytes=room << 20),
        name=name,
        cost_estimate=pl.CostEstimate(
            flops=flops, bytes_accessed=moved_bytes, transcendentals=0
        ),
    )(*args)


def array(shape, kind=BF):
    return jax.ShapeDtypeStruct(shape, kind)


def after(value, *others):
    return lax.optimization_barrier((value, *others))[0]


def project(theirs, groups, blocks, kind):
    return call(
        functools.partial(project_kernel, theirs),
        [array((256, 896), kind), array((3, 256, 896), kind)],
        whole(19),
        (*groups, *blocks),
        "project",
        2 * 512 * 1024 * 1792,
        8 << 20,
        12,
        [pltpu.VMEM((512, 1024), BF), pltpu.VMEM((512, 1792), F32)],
    )


def local(query_latent, key_rows, key_cache, prompt_start, w_query, w_key_up, w_value_up, w_output):
    yh, z, x, c, yl = (lax.axis_index(a) for a in AXES)
    slab = 8 * yh + z
    own, given = quarters(w_output.reshape(64, 7168))
    other = xor_y(given, 3)
    u1, d1 = up_z(own), down_z(own)

    own_keys = key_rows.T
    half = lax.dynamic_slice_in_dim(own_keys, 128 * c, 128, 1)
    near, far = (
        lax.ppermute(half, CTX, [(i, (i + by) % 16) for i in range(16)]) for by in (1, 2)
    )
    cosines, sines, all_cosines, all_sines = turns(slab * 256)
    queries = call(
        queries_kernel,
        [array((1024, 640))] * 2,
        kept(2) + whole(3),
        (query_latent, w_query, w_key_up, cosines, sines),
        "queries",
        2 * 256 * 1536 * 1536 + 2 * 2048 * 128 * 512,
        8 << 20,
        60,
        [
            pltpu.VMEM((2, 1536, 768), BF),
            pltpu.VMEM((256, 1536), BF),
            pltpu.SemaphoreType.DMA((3,)),
        ],
    )
    swapped = other_core(jnp.concatenate([near, far], 1))
    u2 = up_z(after(jnp.concatenate([u1, other], 0), queries[0]))
    d2 = down_z(after(jnp.concatenate([d1, other], 0), queries[0]))

    keys, hidden = call(
        keys_kernel,
        [array((640, 768)), array((256, 768), F32)],
        scalars() + kept() + placed(3) + kept() + whole(2),
        (prompt_start, own_keys, near, far, swapped, key_cache.T, all_cosines, all_sines),
        "keys",
        768 * 640 * 8,
        4 << 20,
        8,
        [pltpu.VMEM((576, 768), BF), pltpu.SemaphoreType.DMA((5,))],
    )
    column = jnp.arange(512, dtype=jnp.int32)
    source = (
        (column // 8 % 4) * 128 + (column // 256) * 64 + ((z + column // 32) % 8) * 8 + column % 8
    )
    reorder = (column[:, None] == source[None, :]).astype(BF)
    rows = [
        call(
            functools.partial(attend_kernel, g),
            array((256, 512)),
            whole(5),
            (queries[g], keys, hidden, w_value_up, reorder),
            "attend",
            2 * 1024 * 768 * 1152 + 2 * 1024 * 512 * 128,
            5 << 20,
            14,
        )
        for g in range(2)
    ]
    one = [xor_y(part, 1) for part in rows]
    three = [xor_y(part, 3) for part in rows]
    two = [xor_y(one[0], 3), xor_y(three[1], 1)]
    groups = [*rows, *one, *two, *three]
    u3, d3 = up_z(after(u2, *rows)), down_z(after(d2, *rows))
    u4 = up_z(u3)
    e3 = down_z(d3[64:])
    e4 = down_z(e3)
    blocks = [own, d1, d2, d3, u4, u3, u2, u1, other, e3, e4]

    first, rest = project(1, groups, blocks, BF)
    first, rest = other_core(first), other_core(rest)
    mine, mine_rest = project(0, groups, blocks, F32)
    sums = [mine_rest[i] + rest[i].astype(F32) for i in range(3)]
    early_up, early_down, first, mine = lax.optimization_barrier(
        (sums[1][:128].astype(BF), sums[2][128:].astype(BF), first, mine)
    )
    far_sum = (mine + first.astype(F32)).astype(BF)
    passing_up = along_x(far_sum[128:], 1)
    passing_down = along_x(far_sum[:128], 3)
    early_up, early_down = along_x(early_up, 1), along_x(early_down, 3)
    late_up = home((sums[1][128:] + passing_up.astype(F32)).astype(BF), 1, 1)
    late_down = home((sums[2][:128] + passing_down.astype(F32)).astype(BF), 0, 3)
    parts = [
        [home((sums[0][:128] + early_up.astype(F32)).astype(BF), 0), late_down],
        [home((sums[0][128:] + early_down.astype(F32)).astype(BF), 1), late_up],
    ]
    pieces = [sum(part.astype(F32) for part in piece).astype(BF) for piece in parts]
    even = yl == 0
    pair = jnp.where(even, pieces[0], pieces[1]), jnp.where(even, pieces[1], pieces[0])
    return jnp.concatenate(
        [jnp.concatenate([p[:, 448 * i : 448 * i + 448] for p in pair], 1) for i in range(2)], 0
    )


def solution(mesh):
    cut = Mesh(mesh.devices.reshape(SIZES), AXES) if hasattr(mesh, "devices") else mesh
    tokens = ("yl", "yh", "z")
    return jax.shard_map(
        local,
        mesh=cut,
        in_specs=(
            P(tokens, None),
            P(tokens, None),
            P("yl", None),
            P("yl"),
            P(None, HEAD),
            P(HEAD, None, None),
            P(HEAD, None, None),
            P(HEAD, CTX, None),
        ),
        out_specs=P(tokens, HEAD),
        check_vma=False,
    )
```

```python
import functools

import jax
import jax.numpy as jnp
from jax import lax
from jax.experimental import pallas as pl
from jax.experimental.pallas import tpu as pltpu
from jax.sharding import Mesh
from jax.sharding import PartitionSpec as P

AXES = ("yh", "z", "x", "c", "yl")
SIZES = (2, 8, 4, 2, 2)
CTX = ("yh", "z")
HEAD = ("x", "c")
BF = jnp.bfloat16
F32 = jnp.float32
VMEM = pltpu.MemorySpace.VMEM


def number_of(yh, z, x, c, yl):
    return (((yh * 8 + z) * 4 + x) * 2 + c) * 2 + yl


def moved(a, target):
    pairs = []
    for yh in range(2):
        for z in range(8):
            for x in range(4):
                for c in range(2):
                    for yl in range(2):
                        t = target(yh, z, x, c, yl)
                        pairs.append((number_of(yh, z, x, c, yl), number_of(*t)))
    return lax.ppermute(a, AXES, pairs)


def up_z(a):
    return moved(a, lambda yh, z, x, c, yl: (yh, (z + 1) % 8, x, c, yl))


def down_z(a):
    return moved(a, lambda yh, z, x, c, yl: (yh, (z - 1) % 8, x, c, yl))


def xor_y(a, q):
    return moved(a, lambda yh, z, x, c, yl: (yh ^ (q >> 1), z, x, c, yl ^ (q & 1)))


def other_core(a):
    return moved(a, lambda yh, z, x, c, yl: (yh, z, x, 1 - c, yl))


def along_x(a, d):
    return moved(a, lambda yh, z, x, c, yl: (yh, z, (x + d) % 4, c, yl))


def home(a, r, d=0):
    return moved(a, lambda yh, z, x, c, yl: (yh ^ c, z, (x + d) % 4, yh, yl ^ r))


def turn_of(table):
    return jnp.concatenate([table[:, 32 * i : 32 * i + 32] for i in range(4)], 0)


def turned(rot, cosine, sine):
    other = jnp.concatenate([rot[:, 32:], rot[:, :32]], 1)
    cosine = jnp.concatenate([cosine, cosine], 1)
    sine = jnp.concatenate([-sine, sine], 1)
    rot = rot * cosine + other * sine
    return jnp.concatenate([rot, jnp.zeros_like(rot)], 1).astype(BF)


def queries_kernel(rows, w_query, w_key_up, cosines, sines, out, out_next, held, rows_held, sem):
    copies = [
        pltpu.make_async_copy(w_query.at[:, pl.ds(768 * part, 768)], held.at[part], sem.at[part])
        for part in range(2)
    ]
    copies.append(pltpu.make_async_copy(rows, rows_held, sem.at[2]))
    for i in (2, 0, 1):
        copies[i].start()
    cosine, sine = turn_of(cosines), turn_of(sines)
    copies[2].wait()
    for part in range(2):
        copies[part].wait()
        queries = jnp.dot(rows_held[...], held[part], preferred_element_type=F32).astype(BF)
        for i in range(4):
            h = 4 * part + i
            plain = queries[:, 192 * i : 192 * i + 128]
            lat = jnp.dot(plain, w_key_up[h], preferred_element_type=F32)
            rot = queries[:, 192 * i + 128 : 192 * i + 192].astype(F32)
            tokens = slice(256 * i, 256 * i + 256)
            to = out_next if part else out
            to[tokens, :512] = lat.astype(BF)
            to[tokens, 512:] = turned(rot, cosine, sine)


def keys_kernel(start, own, near, far, swapped, cache, cosines, sines, keys, hidden, raw, sem):
    c = lax.axis_index("c")
    slab = 8 * lax.axis_index("yh") + lax.axis_index("z")

    def at(column, columns):
        return raw.at[:, pl.ds(pl.multiple_of(column, 128), columns)]

    copies = [
        pltpu.make_async_copy(own, at(512, 256), sem.at[0]),
        pltpu.make_async_copy(near, at(256 + 128 * c, 128), sem.at[1]),
        pltpu.make_async_copy(swapped.at[:, pl.ds(0, 128)], at(384 - 128 * c, 128), sem.at[2]),
        pltpu.make_async_copy(far, at(128 * c, 128), sem.at[3]),
        pltpu.make_async_copy(swapped.at[:, pl.ds(128, 128)], at(128 - 128 * c, 128), sem.at[4]),
    ]
    for copy in copies:
        copy.start()
    row = lax.broadcasted_iota(jnp.int32, (256, 768), 0)
    col = lax.broadcasted_iota(jnp.int32, (256, 768), 1)
    relative = col - 512 - row
    visible = (relative <= 0) & (relative > -512) & (slab * 256 + col - 512 >= -start[0])
    hidden[...] = jnp.where(visible, 0.0, -1e30)
    for copy in copies:
        copy.wait()
    low, high = raw[512:544, :].astype(F32), raw[544:, :].astype(F32)
    cosine, sine = cosines[...], sines[...]
    keys[:512, :] = raw[:512, :]
    keys[512:544, :] = (low * cosine - high * sine).astype(BF)
    keys[544:576, :] = (low * sine + high * cosine).astype(BF)
    keys[576:, :] = jnp.zeros((64, 768), BF)

    @pl.when(slab < 2)
    def _():
        copy = pltpu.make_async_copy(cache, at(0, 512), sem.at[0])
        copy.start()
        copy.wait()

    @pl.when(slab == 0)
    def _():
        keys[:576, :512] = raw[:, :512]

    @pl.when(slab == 1)
    def _():
        keys[:576, :256] = raw[:, 256:512]


def attend_kernel(queries, queries_next, keys, hidden, w_value_up, reorder, out):
    scale = 192.0**-0.5 * 1.4426950408889634
    for group, held in enumerate((queries, queries_next)):
        heads = []
        for pair in range(2):
            scores = jnp.dot(
                held[512 * pair : 512 * pair + 512, :], keys[...], preferred_element_type=F32
            )
            for i in range(2):
                part = scores[256 * i : 256 * i + 256] * scale + hidden[...]
                top = jnp.max(part, axis=1, keepdims=True)
                powers = jnp.exp2(part - top)
                share = 1.0 / jnp.sum(powers, axis=1, keepdims=True)
                mixed = lax.dot_general(
                    powers.astype(BF),
                    keys[:512, :],
                    (((1,), (1,)), ((), ())),
                    preferred_element_type=F32,
                )
                attention = jnp.dot(
                    (mixed * share).astype(BF),
                    w_value_up[4 * group + 2 * pair + i],
                    preferred_element_type=F32,
                )
                heads.append(attention.astype(BF))
        rows = jnp.concatenate(heads, 1)
        out[:, 512 * group : 512 * group + 512] = jnp.dot(
            rows, reorder[...], preferred_element_type=F32
        ).astype(BF)


def turns(first):
    inverse = jnp.power(jnp.float32(10000.0), -jnp.arange(32, dtype=F32) * (2.0 / 64))
    row = lax.broadcasted_iota(jnp.int32, (64, 128), 0)
    lane = lax.broadcasted_iota(jnp.int32, (64, 128), 1)
    own = (first + (lane // 32) * 64 + row).astype(F32) * jnp.tile(inverse, 4)[None, :]
    place = first - 512 + lax.broadcasted_iota(jnp.int32, (32, 768), 1)
    every = place.astype(F32) * inverse[:, None]
    return jnp.cos(own), jnp.sin(own), jnp.cos(every), jnp.sin(every)


def quarter_kernel(rows, own, other):
    x = lax.axis_index("x")
    for out, flip in ((own, 0), (other, 1)):
        odd = lax.axis_index("yl") ^ flip
        base = 896 * (lax.axis_index("yh") ^ flip) + 384 * odd
        pieces = []
        for d in range(4):
            start = pl.multiple_of(1792 * ((x + d) % 4) + base, 128)
            wide = rows[:, pl.ds(start, 512)]
            pieces.append(jnp.where(odd == 1, wide[:, 64:], wide[:, :448]))
        out[...] = jnp.concatenate(pieces, 1)


def project_kernel(theirs, *refs):
    groups, held, outs, (rows, total) = refs[:5], refs[5:16], refs[16:-2], refs[-2:]
    own, d1, d2, d3, u4, u3, u2, u1, other, e3, e4 = held
    blocks = [own, d1, *(both.at[:64] for both in (d2, d3, u4, u3, u2)), u1]
    blocks += [other, d2.at[64:], d3.at[64:], e3, e4, *(both.at[64:] for both in (u4, u3, u2))]
    first = 2 * (lax.axis_index("c") ^ theirs)
    yh = lax.axis_index("yh")
    for pick in (0, 2):

        @pl.when(first == pick)
        def _():
            at = 0
            for part in groups[2:] if pick else groups[:2]:
                for g in range(2):
                    for p in range(2):
                        half = pl.ds(pl.multiple_of(512 * g + 256 * (yh ^ p), 256), 256)
                        to = 512 * g + 256 * p
                        rows[at : at + part.shape[0], to : to + 256] = part[:, half]
                at += part.shape[0]

    for n in range(7):
        columns = slice(256 * n, 256 * n + 256)
        weights = jnp.concatenate(
            [
                block[32 * g : 32 * g + 32, columns]
                for g in range(2)
                for block in blocks
            ],
            0,
        )
        total[:, columns] = jnp.dot(rows[...], weights, preferred_element_type=F32)
    for out, d in zip((outs[0], *(outs[1].at[i] for i in range(3))), (2, 0, 1, 3)):
        span = slice(448 * d, 448 * d + 448)
        for j in range(2):
            top = total[256 * j : 256 * j + 128, span]
            low = total[256 * j + 128 : 256 * j + 256, span]
            out[128 * j : 128 * j + 128, :] = jnp.concatenate([top, low], 1).astype(out.dtype)


def whole(n):
    return [pl.BlockSpec(memory_space=VMEM)] * n


def placed(n):
    return [pl.BlockSpec(memory_space=pl.ANY)] * n


def kept(n=1):
    return [pl.BlockSpec(memory_space=pltpu.MemorySpace.HBM)] * n


def scalars(n=1):
    return [pl.BlockSpec(memory_space=pltpu.MemorySpace.SMEM)] * n


def quarters(rows):
    return pl.pallas_call(
        quarter_kernel,
        out_shape=[jax.ShapeDtypeStruct((64, 1792), BF)] * 2,
        in_specs=whole(1),
        out_specs=whole(2),
        name="quarters",
        cost_estimate=pl.CostEstimate(flops=0, bytes_accessed=2 << 20, transcendentals=0),
    )(rows)


def call(kernel, shapes, specs, args, name, flops, moved_bytes, room, scratch=()):
    many = isinstance(shapes, list)
    return pl.pallas_call(
        kernel,
        out_shape=shapes,
        in_specs=specs,
        out_specs=whole(len(shapes)) if many else whole(1)[0],
        scratch_shapes=list(scratch),
        compiler_params=pltpu.CompilerParams(vmem_limit_bytes=room << 20),
        name=name,
        cost_estimate=pl.CostEstimate(
            flops=flops, bytes_accessed=moved_bytes, transcendentals=0
        ),
    )(*args)


def array(shape, kind=BF):
    return jax.ShapeDtypeStruct(shape, kind)


def after(value, *others):
    return lax.optimization_barrier((value, *others))[0]


def project(theirs, groups, blocks, kind):
    return call(
        functools.partial(project_kernel, theirs),
        [array((256, 896), kind), array((3, 256, 896), kind)],
        whole(16),
        (*groups, *blocks),
        "project",
        2 * 512 * 1024 * 1792,
        8 << 20,
        12,
        [pltpu.VMEM((512, 1024), BF), pltpu.VMEM((512, 1792), F32)],
    )


def local(query_latent, key_rows, key_cache, prompt_start, w_query, w_key_up, w_value_up, w_output):
    yh, z, x, c, yl = (lax.axis_index(a) for a in AXES)
    slab = 8 * yh + z
    own, given = quarters(w_output.reshape(64, 7168))
    other = xor_y(given, 3)
    u1, d1 = up_z(own), down_z(own)

    own_keys = key_rows.T
    half = lax.dynamic_slice_in_dim(own_keys, 128 * c, 128, 1)
    near, far = (
        lax.ppermute(half, CTX, [(i, (i + by) % 16) for i in range(16)]) for by in (1, 2)
    )
    cosines, sines, all_cosines, all_sines = turns(slab * 256)
    queries = call(
        queries_kernel,
        [array((1024, 640))] * 2,
        kept(2) + whole(3),
        (query_latent, w_query, w_key_up, cosines, sines),
        "queries",
        2 * 256 * 1536 * 1536 + 2 * 2048 * 128 * 512,
        8 << 20,
        60,
        [
            pltpu.VMEM((2, 1536, 768), BF),
            pltpu.VMEM((256, 1536), BF),
            pltpu.SemaphoreType.DMA((3,)),
        ],
    )
    swapped = other_core(jnp.concatenate([near, far], 1))
    u2 = up_z(after(jnp.concatenate([u1, other], 0), queries[0]))
    d2 = down_z(after(jnp.concatenate([d1, other], 0), queries[0]))

    keys, hidden = call(
        keys_kernel,
        [array((640, 768)), array((256, 768), F32)],
        scalars() + kept() + placed(3) + kept() + whole(2),
        (prompt_start, own_keys, near, far, swapped, key_cache.T, all_cosines, all_sines),
        "keys",
        768 * 640 * 8,
        4 << 20,
        8,
        [pltpu.VMEM((576, 768), BF), pltpu.SemaphoreType.DMA((5,))],
    )
    column = jnp.arange(512, dtype=jnp.int32)
    source = (
        (column // 8 % 4) * 128 + (column // 256) * 64 + ((z + column // 32) % 8) * 8 + column % 8
    )
    reorder = (column[:, None] == source[None, :]).astype(BF)
    rows = call(
        attend_kernel,
        array((256, 1024)),
        whole(6),
        (*queries, keys, hidden, w_value_up, reorder),
        "attend",
        4 * 1024 * 768 * 1152 + 4 * 1024 * 512 * 128,
        10 << 20,
        16,
    )
    one, three = xor_y(rows, 1), xor_y(rows, 3)
    groups = [rows, one, xor_y(one[:128], 3), xor_y(three[128:], 1), three]
    u3, d3 = up_z(after(u2, rows)), down_z(after(d2, rows))
    u4 = up_z(u3)
    e3 = down_z(d3[64:])
    e4 = down_z(e3)
    blocks = [own, d1, d2, d3, u4, u3, u2, u1, other, e3, e4]

    first, rest = project(1, groups, blocks, BF)
    first, rest = other_core(first), other_core(rest)
    mine, mine_rest = project(0, groups, blocks, F32)
    sums = [mine_rest[i] + rest[i].astype(F32) for i in range(3)]
    early_up, early_down, first, mine = lax.optimization_barrier(
        (sums[1][:128].astype(BF), sums[2][128:].astype(BF), first, mine)
    )
    far_sum = (mine + first.astype(F32)).astype(BF)
    passing_up = along_x(far_sum[128:], 1)
    passing_down = along_x(far_sum[:128], 3)
    early_up, early_down = along_x(early_up, 1), along_x(early_down, 3)
    late_up = home((sums[1][128:] + passing_up.astype(F32)).astype(BF), 1, 1)
    late_down = home((sums[2][:128] + passing_down.astype(F32)).astype(BF), 0, 3)
    parts = [
        [home((sums[0][:128] + early_up.astype(F32)).astype(BF), 0), late_down],
        [home((sums[0][128:] + early_down.astype(F32)).astype(BF), 1), late_up],
    ]
    pieces = [sum(part.astype(F32) for part in piece).astype(BF) for piece in parts]
    even = yl == 0
    pair = jnp.where(even, pieces[0], pieces[1]), jnp.where(even, pieces[1], pieces[0])
    return jnp.concatenate(
        [jnp.concatenate([p[:, 448 * i : 448 * i + 448] for p in pair], 1) for i in range(2)], 0
    )


def solution(mesh):
    cut = Mesh(mesh.devices.reshape(SIZES), AXES) if hasattr(mesh, "devices") else mesh
    tokens = ("yl", "yh", "z")
    return jax.shard_map(
        local,
        mesh=cut,
        in_specs=(
            P(tokens, None),
            P(tokens, None),
            P("yl", None),
            P("yl"),
            P(None, HEAD),
            P(HEAD, None, None),
            P(HEAD, None, None),
            P(HEAD, CTX, None),
        ),
        out_specs=P(tokens, HEAD),
        check_vma=False,
    )
```
